32 devices in a mesh: dp: 8 (over y, x, core), seq: 4 (over z).
Axes of the slice: x: 2, y: 2, z: 4, core: 2. Of those that a mesh axis runs over, the one named last changes fastest.
Arguments:
- tokens: bfloat16 [16, 1024, 1024], P('dp', 'seq'), may hold values from -6 to 6
- w_qkv: bfloat16 [1024, 3072], P('dp'), may hold values from -0.1875 to 0.1875
- w_out: bfloat16 [1024, 1024], P('dp'), may hold values from -2 to 2
- w_up: bfloat16 [1024, 4096], P('dp'), may hold values from -0.1875 to 0.1875
- w_down: bfloat16 [4096, 1024], P(None, 'dp'), may hold values from -0.09375 to 0.09375
- b_query: bfloat16 [1024], P('dp'), may hold values from -4 to 4
- b_value: bfloat16 [1024], P('dp'), may hold values from -0.75 to 0.75
- b_out: bfloat16 [1024], P('dp'), may hold values from -4 to 4
- b_up: bfloat16 [4096], P('dp'), may hold values from -4 to 4
- b_down: bfloat16 [1024], P('dp'), may hold values from -4 to 4
- ln1_gain: bfloat16 [1024], P('dp'), may hold values from 0.5 to 1.5
- ln1_bias: bfloat16 [1024], P('dp'), may hold values from -4 to 4
- ln2_gain: bfloat16 [1024], P('dp'), may hold values from 0.5 to 1.5
- ln2_bias: bfloat16 [1024], P('dp'), may hold values from -4 to 4
- cotangent: bfloat16 [16, 1024, 1024], P('dp', 'seq'), may hold values from -6 to 6
Outputs:
- result: bfloat16 [16, 1024, 1024], P('dp', 'seq')
- grad_input: bfloat16 [16, 1024, 1024], P('dp', 'seq')
- grad_w_qkv: float32 [1024, 3072], P('dp')
- grad_w_out: float32 [1024, 1024], P('dp')
- grad_w_up: float32 [1024, 4096], P('dp')
- grad_w_down: float32 [4096, 1024], P(None, 'dp')
- grad_b_query: float32 [1024], P('dp')
- grad_b_value: float32 [1024], P('dp')
- grad_b_out: float32 [1024], P('dp')
- grad_b_up: float32 [4096], P('dp')
- grad_b_down: float32 [1024], P('dp')
- grad_ln1_gain: float32 [1024], P('dp')
- grad_ln1_bias: float32 [1024], P('dp')
- grad_ln2_gain: float32 [1024], P('dp')
- grad_ln2_bias: float32 [1024], P('dp')
The draws below stay inside these ranges and needn't reach their ends.
All inputs are finite; a program needn't handle non-finite values.
Results may differ from the reference program's by a relative error of at most 0.02.
Values may be sent and summed in bfloat16 or wider, within the bound.
A program may use at most 192 MiB of HBM per device.

```python
import jax
import jax.numpy as jnp
from jax import lax

D = 1024
H = 16
DH = 64
FF = 4096
PATCH = 1024
IMAGES = 16


def shard_levels(rng, shape, cuts, smallest, top_value):
    factor_of, own = 1.0, jax.random.fold_in(rng, 6)
    for axis_at, parts in cuts:
        steps = jnp.exp(jax.random.uniform(jax.random.fold_in(own, axis_at), (parts,), jnp.float32, smallest / len(cuts), top_value / len(cuts)))
        factor_of = factor_of * jnp.repeat(steps, shape[axis_at] // parts).reshape([-1 if axis == axis_at else 1 for axis in range(len(shape))])
    return factor_of


def scatter_about(own_key, extent, width, bound, split=(), dtype=jnp.bfloat16):
    entries = width * jax.random.normal(own_key, extent, jnp.float32)
    if split:
        entries = entries * shard_levels(own_key, extent, split, -0.22, 0.18)
    return jnp.clip(entries, -bound, bound).astype(dtype)


def setup_inputs(seed: int = 0) -> dict:
    streams_of = jax.random.split(jax.random.key(seed), 16)
    return {
        "tokens": scatter_about(streams_of[0], (IMAGES, PATCH, D), 1.0, 6.0, ((0, 8), (1, 4))),
        "w_qkv": scatter_about(streams_of[1], (D, 3 * D), D ** -0.5, 0.1875, ((0, 8),)),
        "w_out": scatter_about(streams_of[2], (D, D), (max(D // 128, 1)) ** -0.5, 2.0, ((0, 8),)),
        "w_up": scatter_about(streams_of[3], (D, FF), D ** -0.5, 0.1875, ((0, 8),)),
        "w_down": scatter_about(streams_of[4], (FF, D), FF ** -0.5, 0.09375, ((1, 8),)),
        "b_query": scatter_about(streams_of[5], (D,), 0.3, 4.0, ((0, 8),)),
        "b_value": scatter_about(streams_of[6], (D,), 0.05, 0.75, ((0, 8),)),
        "b_out": scatter_about(streams_of[7], (D,), 0.3, 4.0, ((0, 8),)),
        "b_up": scatter_about(streams_of[8], (FF,), 0.3, 4.0, ((0, 8),)),
        "b_down": scatter_about(streams_of[9], (D,), 0.3, 4.0, ((0, 8),)),
        "ln1_gain": jnp.clip(1.0 + 0.1 * jax.random.normal(streams_of[10], (D,), jnp.float32), 0.5, 1.5).astype(jnp.bfloat16),
        "ln1_bias": scatter_about(streams_of[11], (D,), 0.3, 4.0, ((0, 8),)),
        "ln2_gain": jnp.clip(1.0 + 0.1 * jax.random.normal(streams_of[12], (D,), jnp.float32), 0.5, 1.5).astype(jnp.bfloat16),
        "ln2_bias": scatter_about(streams_of[13], (D,), 0.3, 4.0, ((0, 8),)),
        "cotangent": scatter_about(streams_of[14], (IMAGES, PATCH, D), 1.0, 6.0, ((0, 8), (1, 4))),
    }


@jax.custom_vjp
def low(v):
    return lax.optimization_barrier(v.astype(jnp.bfloat16)).astype(jnp.float32)

@jax.custom_vjp
def low_back(v):
    return v

def low_keep(v):
    return (low(v), None)

def low_pass(kept, grad):
    return (grad,)

def back_keep(v):
    return (v, None)

def back_low(kept, grad):
    return (low(grad),)
low.defvjp(low_keep, low_pass)
low_back.defvjp(back_keep, back_low)
norm_eps = 1e-06

def matmul(left_side, right_side):
    return jnp.einsum('...i,ij->...j', left_side, right_side, precision=lax.Precision.HIGHEST)

def normalize(inputs, ln_gain, ln_offset):
    centre = lax.optimization_barrier(jnp.mean(inputs, axis=-1, keepdims=True))
    spread = lax.optimization_barrier(jnp.mean(jnp.square(inputs - centre), axis=-1, keepdims=True))
    return (inputs - centre) * lax.rsqrt(spread + norm_eps) * ln_gain + ln_offset

def image_attention(element):
    queries, keyed, valued = element
    scores = low_back(jnp.einsum('qhd,khd->hqk', queries, keyed, precision=lax.Precision.HIGHEST) * DH ** (-0.5))
    attn_probs = low(jax.nn.softmax(scores, axis=-1))
    return jnp.einsum('hqk,khd->qhd', attn_probs, valued, precision=lax.Precision.HIGHEST)

def block_layer(inputs, w_qkv, w_out, w_up, w_down, b_query, b_value, b_out, b_up, b_down, gain_one, offset_one, gain_two, offset_two):
    images = inputs.shape[0]
    normed_one = low(normalize(inputs, gain_one, offset_one))
    qkv_bias = jnp.concatenate([b_query, jnp.zeros_like(b_query), b_value])
    projected = low(low_back(matmul(normed_one, w_qkv) + qkv_bias))
    projected = projected.reshape(images, PATCH, 3, H, DH)
    attended = lax.map(jax.checkpoint(image_attention), (projected[:, :, 0], projected[:, :, 1], projected[:, :, 2]))
    attended = low(low_back(attended.reshape(images, PATCH, D)))
    residual = inputs + low_back(matmul(attended, w_out) + b_out)
    normed_two = low(normalize(residual, gain_two, offset_two))
    upward = low_back(matmul(normed_two, w_up) + b_up)
    activated = low(jax.nn.gelu(upward, approximate=True))
    return residual + low_back(matmul(activated, w_down) + b_down)

def reference(tokens, w_qkv, w_out, w_up, w_down, b_query, b_value, b_out, b_up, b_down, ln1_gain, ln1_bias, ln2_gain, ln2_bias, cotangent):
    params = tuple((argument.astype(jnp.float32) for argument in (w_qkv, w_out, w_up, w_down, b_query, b_value, b_out, b_up, b_down, ln1_gain, ln1_bias, ln2_gain, ln2_bias)))
    group_size = 4 if IMAGES % 4 == 0 else 1
    group_count = IMAGES // group_size
    inputs = tokens.astype(jnp.float32).reshape(group_count, group_size, PATCH, D)
    cot_groups = cotangent.astype(jnp.float32).reshape(group_count, group_size, PATCH, D)

    def one_group(totals, element):
        group_in, group_cot = element
        layer_out, pullback = jax.vjp(block_layer, group_in, *params)
        gradients = pullback(group_cot)
        totals = tuple((running + update for running, update in zip(totals, gradients[1:])))
        return (totals, (layer_out.astype(jnp.bfloat16), gradients[0].astype(jnp.bfloat16)))
    empty_sums = tuple((jnp.zeros_like(argument) for argument in params))
    totals, (layer_outs, grad_inputs) = lax.scan(one_group, empty_sums, (inputs, cot_groups))
    return (layer_outs.reshape(IMAGES, PATCH, D), grad_inputs.reshape(IMAGES, PATCH, D), totals[0], totals[1], totals[2], totals[3], totals[4], totals[5], totals[6], totals[7], totals[8], totals[9], totals[10], totals[11], totals[12])
```

```python
import functools

import jax
import jax.numpy as jnp
from jax import lax
from jax.experimental import pallas as pl
from jax.experimental.pallas import tpu as pltpu
from jax.sharding import PartitionSpec as P

H = 16
DH = 64
MICRO = 2
IMG_MB = 1


norm_eps = 1e-06


def normalize(inputs, ln_gain, ln_offset):
    centre = jnp.mean(inputs, axis=-1, keepdims=True)
    spread = jnp.mean(jnp.square(inputs - centre), axis=-1, keepdims=True)
    return (inputs - centre) * lax.rsqrt(spread + norm_eps) * ln_gain + ln_offset


def activate(upward):
    return jax.nn.gelu(upward, approximate=True)


def add_pairs(first_set, second_set):
    return tuple(
        (first_item + second_item for first_item, second_item in zip(first_set, second_set))
    )


def forward_heads(queries, keyed, valued, factor):
    images, length, head_count, head_size = queries.shape
    block_rows = min(512, length)
    blocks = length // block_rows
    query_blocks = queries.reshape(images, blocks, block_rows, head_count, head_size)

    def forward_per_image(element):
        q_image, k_image, v_image = element

        def forward_per_block(q_block):
            scores = (
                jnp.einsum("qhd,khd->hqk", q_block, k_image, preferred_element_type=jnp.float32)
                * factor
            )
            row_max = jnp.max(scores, axis=-1, keepdims=True)
            exponent = jnp.exp(scores - row_max)
            row_total = jnp.sum(exponent, axis=-1, keepdims=True)
            attn_probs = (exponent / row_total).astype(jnp.bfloat16)
            mixture = jnp.einsum(
                "hqk,khd->qhd", attn_probs, v_image, preferred_element_type=jnp.float32
            )
            return (mixture, row_max[..., 0] + jnp.log(row_total[..., 0]))

        return lax.map(forward_per_block, q_image)

    mixture, log_total = lax.map(forward_per_image, (query_blocks, keyed, valued))
    return (mixture.reshape(images, length, head_count * head_size), log_total)


def backward_heads(queries, keyed, valued, grad_mixed, log_total, factor):
    images, length, head_count, head_size = queries.shape
    block_rows = min(512, length)
    blocks = length // block_rows
    query_blocks = queries.reshape(images, blocks, block_rows, head_count, head_size)
    grad_blocks = grad_mixed.reshape(images, blocks, block_rows, head_count, head_size)

    def backward_per_image(element):
        q_image, k_image, v_image, g_image, l_image = element

        def backward_per_block(running, pieces):
            grad_key, grad_value = running
            q_block, g_block, l_block = pieces
            scores = (
                jnp.einsum("qhd,khd->hqk", q_block, k_image, preferred_element_type=jnp.float32)
                * factor
            )
            full_probs = jnp.exp(scores - l_block[..., None])
            grad_probs = jnp.einsum(
                "qhd,khd->hqk", g_block, v_image, preferred_element_type=jnp.float32
            )
            row_inner = jnp.sum(full_probs * grad_probs, axis=-1, keepdims=True)
            grad_scores = (full_probs * (grad_probs - row_inner)).astype(jnp.bfloat16)
            grad_query = (
                jnp.einsum("hqk,khd->qhd", grad_scores, k_image, preferred_element_type=jnp.float32)
                * factor
            )
            grad_key = (
                grad_key
                + jnp.einsum(
                    "hqk,qhd->khd", grad_scores, q_block, preferred_element_type=jnp.float32
                )
                * factor
            )
            grad_value = grad_value + jnp.einsum(
                "hqk,qhd->khd",
                full_probs.astype(jnp.bfloat16),
                g_block,
                preferred_element_type=jnp.float32,
            )
            return ((grad_key, grad_value), grad_query)

        empty_sum = jnp.zeros((length, head_count, head_size), jnp.float32)
        (grad_key, grad_value), grad_query = lax.scan(
            backward_per_block, (empty_sum, empty_sum), (q_image, g_image, l_image)
        )
        return (grad_query.reshape(length, head_count, head_size), grad_key, grad_value)

    return lax.map(backward_per_image, (query_blocks, keyed, valued, grad_blocks, log_total))


def weight_grads(
    normed_one_low,
    grad_projected,
    mixed_tokens,
    grad_attn_low,
    normed_two_low,
    grad_upward_low,
    activated_low,
    grad_branch,
    model_width,
):
    grad_qkv = jnp.einsum(
        "ptd,pte->de", normed_one_low, grad_projected, preferred_element_type=jnp.float32
    )
    grad_bquery = jnp.sum(grad_projected[:, :, :model_width], axis=(0, 1), dtype=jnp.float32)
    grad_bvalue = jnp.sum(grad_projected[:, :, 2 * model_width :], axis=(0, 1), dtype=jnp.float32)
    grad_wout = jnp.einsum(
        "pte,ptd->ed", mixed_tokens, grad_attn_low, preferred_element_type=jnp.float32
    )
    grad_bout = jnp.sum(grad_attn_low, axis=(0, 1), dtype=jnp.float32)
    grad_up = jnp.einsum(
        "ptd,ptf->df", normed_two_low, grad_upward_low, preferred_element_type=jnp.float32
    )
    grad_bup = jnp.sum(grad_upward_low, axis=(0, 1), dtype=jnp.float32)
    grad_down = jnp.einsum(
        "ptf,ptd->fd", activated_low, grad_branch, preferred_element_type=jnp.float32
    )
    grad_bdown = jnp.sum(grad_branch, axis=(0, 1), dtype=jnp.float32)
    return (
        grad_qkv,
        grad_wout,
        grad_up,
        grad_down,
        grad_bquery,
        grad_bvalue,
        grad_bout,
        grad_bup,
        grad_bdown,
    )


def local(
    tokens,
    w_qkv,
    w_out,
    w_up,
    w_down,
    b_query,
    b_value,
    b_out,
    b_up,
    b_down,
    ln1_gain,
    ln1_bias,
    ln2_gain,
    ln2_bias,
    cotangent,
):
    seq_count = lax.axis_size("seq")
    local_patches = tokens.shape[1]
    model_width = tokens.shape[2]
    patches = local_patches * seq_count
    head_local = H // seq_count
    factor = DH ** (-0.5)
    gathered = (
        lax.all_gather(w_qkv, "dp", axis=0, tiled=True),
        lax.all_gather(w_out, "dp", axis=0, tiled=True),
        lax.all_gather(w_up, "dp", axis=0, tiled=True),
        lax.all_gather(w_down, "dp", axis=1, tiled=True),
        lax.all_gather(b_query, "dp", axis=0, tiled=True),
        lax.all_gather(b_value, "dp", axis=0, tiled=True),
        lax.all_gather(b_out, "dp", axis=0, tiled=True),
        lax.all_gather(b_up, "dp", axis=0, tiled=True),
        lax.all_gather(b_down, "dp", axis=0, tiled=True),
        lax.all_gather(ln1_gain, "dp", axis=0, tiled=True),
        lax.all_gather(ln1_bias, "dp", axis=0, tiled=True),
        lax.all_gather(ln2_gain, "dp", axis=0, tiled=True),
        lax.all_gather(ln2_bias, "dp", axis=0, tiled=True),
    )
    outputs = []
    grad_inputs = []
    kept = []
    for micro_idx in range(MICRO):
        w_qkv_full, w_out_full, w_up_full, w_down_full = (
            gathered[0],
            gathered[1],
            gathered[2],
            gathered[3],
        )
        vectors = [piece.astype(jnp.float32) for piece in gathered[4:]]
        (
            bias_query,
            bias_value,
            bias_out,
            bias_up,
            bias_down,
            gain_one,
            offset_one,
            gain_two,
            offset_two,
        ) = vectors
        start = micro_idx * IMG_MB
        inputs = tokens[start : start + IMG_MB].astype(jnp.float32)
        normed_one, norm_one_back = jax.vjp(normalize, inputs, gain_one, offset_one)
        normed_one_low = normed_one.astype(jnp.bfloat16)
        qkv_bias = jnp.concatenate([bias_query, jnp.zeros_like(bias_query), bias_value])
        projected = (
            jnp.einsum(
                "ptd,de->pte", normed_one_low, w_qkv_full, preferred_element_type=jnp.float32
            )
            + qkv_bias
        )
        projected_low = projected.astype(jnp.bfloat16).reshape(
            IMG_MB, local_patches, 3, model_width
        )
        by_heads = lax.all_to_all(projected_low, "seq", split_axis=3, concat_axis=1, tiled=True)
        queries = by_heads[:, :, 0].reshape(IMG_MB, patches, head_local, DH)
        keyed = by_heads[:, :, 1].reshape(IMG_MB, patches, head_local, DH)
        valued = by_heads[:, :, 2].reshape(IMG_MB, patches, head_local, DH)
        attended, log_total = forward_heads(queries, keyed, valued, factor)
        attended_low = attended.astype(jnp.bfloat16)
        mixed_tokens = lax.all_to_all(attended_low, "seq", split_axis=1, concat_axis=2, tiled=True)
        residual = (
            inputs
            + jnp.einsum(
                "pte,ed->ptd", mixed_tokens, w_out_full, preferred_element_type=jnp.float32
            )
            + bias_out
        )
        normed_two, norm_two_back = jax.vjp(normalize, residual, gain_two, offset_two)
        normed_two_low = normed_two.astype(jnp.bfloat16)
        upward = (
            jnp.einsum("ptd,df->ptf", normed_two_low, w_up_full, preferred_element_type=jnp.float32)
            + bias_up
        )
        activated, activate_back = jax.vjp(activate, upward)
        activated_low = activated.astype(jnp.bfloat16)
        layer_out = (
            residual
            + jnp.einsum(
                "ptf,fd->ptd", activated_low, w_down_full, preferred_element_type=jnp.float32
            )
            + bias_down
        )
        outputs.append(layer_out.astype(jnp.bfloat16))
        grad_result = cotangent[start : start + IMG_MB].astype(jnp.float32)
        grad_branch = grad_result.astype(jnp.bfloat16)
        grad_active = jnp.einsum(
            "ptd,fd->ptf", grad_branch, w_down_full, preferred_element_type=jnp.float32
        )
        (grad_upward,) = activate_back(grad_active)
        grad_upward_low = grad_upward.astype(jnp.bfloat16)
        grad_normed_two = jnp.einsum(
            "ptf,df->ptd", grad_upward_low, w_up_full, preferred_element_type=jnp.float32
        )
        grad_from_two, grad_gain2, grad_bias2 = norm_two_back(grad_normed_two)
        grad_residual = grad_result + grad_from_two
        grad_attn_low = grad_residual.astype(jnp.bfloat16)
        grad_mixed = jnp.einsum(
            "ptd,ed->pte", grad_attn_low, w_out_full, preferred_element_type=jnp.float32
        ).astype(jnp.bfloat16)
        grad_heads = lax.all_to_all(grad_mixed, "seq", split_axis=2, concat_axis=1, tiled=True)
        grad_query, grad_key, grad_value = backward_heads(
            queries,
            keyed,
            valued,
            grad_heads.reshape(IMG_MB, patches, head_local, DH),
            log_total,
            factor,
        )
        stacked = (
            jnp.stack([grad_query, grad_key, grad_value], axis=2)
            .reshape(IMG_MB, patches, 3, head_local * DH)
            .astype(jnp.bfloat16)
        )
        grad_parts = lax.all_to_all(stacked, "seq", split_axis=1, concat_axis=3, tiled=True)
        grad_projected = grad_parts.reshape(IMG_MB, local_patches, 3 * model_width)
        grad_normed_one = jnp.einsum(
            "pte,de->ptd", grad_projected, w_qkv_full, preferred_element_type=jnp.float32
        )
        grad_from_one, grad_gain1, grad_bias1 = norm_one_back(grad_normed_one)
        grad_inputs.append((grad_residual + grad_from_one).astype(jnp.bfloat16))
        norm_grads = (grad_gain1, grad_bias1, grad_gain2, grad_bias2)
        norm_total = norm_grads if micro_idx == 0 else add_pairs(norm_total, norm_grads)
        kept.append(
            (
                normed_one_low,
                grad_projected,
                mixed_tokens,
                grad_attn_low,
                normed_two_low,
                grad_upward_low,
                activated_low,
                grad_branch,
            )
        )
    joined = [jnp.concatenate([item[index] for item in kept], axis=0) for index in range(8)]
    big = weight_grads(
        joined[0],
        joined[1],
        joined[2],
        joined[3],
        joined[4],
        joined[5],
        joined[6],
        joined[7],
        model_width,
    )
    owned = (
        lax.psum_scatter(big[0].astype(jnp.bfloat16), "dp", scatter_dimension=0, tiled=True).astype(
            jnp.float32
        ),
        lax.psum_scatter(big[1].astype(jnp.bfloat16), "dp", scatter_dimension=0, tiled=True).astype(
            jnp.float32
        ),
        lax.psum_scatter(big[2].astype(jnp.bfloat16), "dp", scatter_dimension=0, tiled=True).astype(
            jnp.float32
        ),
        lax.psum_scatter(big[3].astype(jnp.bfloat16), "dp", scatter_dimension=1, tiled=True).astype(
            jnp.float32
        ),
        lax.psum_scatter(big[4].astype(jnp.bfloat16), "dp", scatter_dimension=0, tiled=True).astype(
            jnp.float32
        ),
        lax.psum_scatter(big[5].astype(jnp.bfloat16), "dp", scatter_dimension=0, tiled=True).astype(
            jnp.float32
        ),
        lax.psum_scatter(big[6].astype(jnp.bfloat16), "dp", scatter_dimension=0, tiled=True).astype(
            jnp.float32
        ),
        lax.psum_scatter(big[7].astype(jnp.bfloat16), "dp", scatter_dimension=0, tiled=True).astype(
            jnp.float32
        ),
        lax.psum_scatter(big[8].astype(jnp.bfloat16), "dp", scatter_dimension=0, tiled=True).astype(
            jnp.float32
        ),
        lax.psum_scatter(
            norm_total[0].astype(jnp.bfloat16), "dp", scatter_dimension=0, tiled=True
        ).astype(jnp.float32),
        lax.psum_scatter(
            norm_total[1].astype(jnp.bfloat16), "dp", scatter_dimension=0, tiled=True
        ).astype(jnp.float32),
        lax.psum_scatter(
            norm_total[2].astype(jnp.bfloat16), "dp", scatter_dimension=0, tiled=True
        ).astype(jnp.float32),
        lax.psum_scatter(
            norm_total[3].astype(jnp.bfloat16), "dp", scatter_dimension=0, tiled=True
        ).astype(jnp.float32),
    )
    owned = (
        lax.psum(owned[0].astype(jnp.bfloat16), "seq").astype(jnp.float32),
        lax.psum(owned[1].astype(jnp.bfloat16), "seq").astype(jnp.float32),
        lax.psum(owned[2].astype(jnp.bfloat16), "seq").astype(jnp.float32),
        lax.psum(owned[3].astype(jnp.bfloat16), "seq").astype(jnp.float32),
        lax.psum(owned[4].astype(jnp.bfloat16), "seq").astype(jnp.float32),
        lax.psum(owned[5].astype(jnp.bfloat16), "seq").astype(jnp.float32),
        lax.psum(owned[6].astype(jnp.bfloat16), "seq").astype(jnp.float32),
        lax.psum(owned[7].astype(jnp.bfloat16), "seq").astype(jnp.float32),
        lax.psum(owned[8].astype(jnp.bfloat16), "seq").astype(jnp.float32),
        lax.psum(owned[9].astype(jnp.bfloat16), "seq").astype(jnp.float32),
        lax.psum(owned[10].astype(jnp.bfloat16), "seq").astype(jnp.float32),
        lax.psum(owned[11].astype(jnp.bfloat16), "seq").astype(jnp.float32),
        lax.psum(owned[12].astype(jnp.bfloat16), "seq").astype(jnp.float32),
    )
    return (
        jnp.concatenate(outputs, axis=0),
        jnp.concatenate(grad_inputs, axis=0),
        owned[0],
        owned[1],
        owned[2],
        owned[3],
        owned[4],
        owned[5],
        owned[6],
        owned[7],
        owned[8],
        owned[9],
        owned[10],
        owned[11],
        owned[12],
    )


F32=jnp.float32; BF16=jnp.bfloat16
NT=(((1,),(1,)),((),())); TN=(((0,),(0,)),((),())); NN=(((1,),(0,)),((),()))
def dg(a,b,dims): return lax.dot_general(a,b,dims,preferred_element_type=F32)

def attn_fwd_kernel(q_ref, ka_ref, kb_ref, va_ref, vb_ref, o_ref, l_ref):
    rows=q_ref.shape[0]
    lane=lax.broadcasted_iota(jnp.int32,(rows,128),1)
    q=q_ref[...]*jnp.asarray(0.125,BF16)
    outs=[]; ls=[]
    for h in range(2):
        qh=jnp.where((lane<64) if h==0 else (lane>=64), q, jnp.zeros_like(q))
        sa=dg(ka_ref[...],qh,NT); sb=dg(kb_ref[...],qh,NT)
        m=jnp.maximum(jnp.max(sa,axis=0,keepdims=True),jnp.max(sb,axis=0,keepdims=True))
        pa=jnp.exp(sa-m); pb=jnp.exp(sb-m)
        tot=jnp.sum(pa,axis=0,keepdims=True)+jnp.sum(pb,axis=0,keepdims=True)
        oT=dg(va_ref[...],pa.astype(BF16),TN)+dg(vb_ref[...],pb.astype(BF16),TN)
        outs.append(oT[64*h:64*h+64]*(1.0/tot))
        ls.append(m+jnp.log(tot))
    oT=jnp.concatenate(outs,axis=0)
    o_ref[...]=oT.T.astype(BF16)
    l_ref[0]=jnp.concatenate(ls+[jnp.zeros((6,rows),F32)],axis=0)

def attn_fwd(q,ka,kb,va,vb):
    rows,width=q.shape
    spec=pl.BlockSpec((rows,128),lambda i:(0,i))
    keys=ka.shape[0]
    ks=pl.BlockSpec((keys,128),lambda i:(0,i))
    return pl.pallas_call(attn_fwd_kernel,grid=(width//128,),
        in_specs=[spec,ks,ks,ks,ks],
        out_specs=[spec,pl.BlockSpec((1,8,rows),lambda i:(i,0,0))],
        out_shape=[jax.ShapeDtypeStruct((rows,width),BF16),jax.ShapeDtypeStruct((width//128,8,rows),F32)],
        compiler_params=pltpu.CompilerParams(vmem_limit_bytes=48<<20),name="attn_fwd",
        cost_estimate=pl.CostEstimate(flops=4*rows*2*keys*width,bytes_accessed=12*rows*width,transcendentals=rows*2*keys*width//64))(q,ka,kb,va,vb)

def attn_bwd_kernel(q_ref, ka_ref, kb_ref, va_ref, vb_ref, o_ref, do_ref, l_ref, dq_ref, dka_ref, dkb_ref, dva_ref, dvb_ref):
    rows=q_ref.shape[0]
    lane=lax.broadcasted_iota(jnp.int32,(rows,128),1)
    q=q_ref[...]*jnp.asarray(0.125,BF16)
    do=do_ref[...]
    t=(do.astype(F32)*o_ref[...].astype(F32)).T
    klane=lax.broadcasted_iota(jnp.int32,(ka_ref.shape[0],128),1)
    dq=None; dk=[None,None]; dv=[None,None]
    add=lambda a,b: b if a is None else a+b
    for h in range(2):
        sel=(lane<64) if h==0 else (lane>=64)
        ksel=(klane<64) if h==0 else (klane>=64)
        qh=jnp.where(sel,q,jnp.zeros_like(q)); doh=jnp.where(sel,do,jnp.zeros_like(do))
        delta=jnp.sum(t[64*h:64*h+64],axis=0,keepdims=True)
        lse=l_ref[0,h:h+1,:]
        for n,(k_ref,v_ref) in enumerate(((ka_ref,va_ref),(kb_ref,vb_ref))):
            s=dg(k_ref[...],qh,NT)
            p=jnp.exp(s-lse)
            dp=dg(v_ref[...],doh,NT)
            ds=(p*(dp-delta)).astype(BF16)
            dv[n]=add(dv[n],dg(p.astype(BF16),doh,NN))
            dk[n]=add(dk[n],dg(ds,qh,NN))
            kh=jnp.where(ksel,k_ref[...],jnp.zeros_like(k_ref[...]))
            dq=add(dq,dg(kh,ds,TN))
    dq_ref[...]=(dq*0.125).T.astype(BF16)
    dka_ref[...]=dk[0].astype(BF16); dkb_ref[...]=dk[1].astype(BF16)
    dva_ref[...]=dv[0].astype(BF16); dvb_ref[...]=dv[1].astype(BF16)

def attn_bwd(q,ka,kb,va,vb,o,do,l):
    rows,width=q.shape; keys=ka.shape[0]
    spec=pl.BlockSpec((rows,128),lambda i:(0,i))
    ks=pl.BlockSpec((keys,128),lambda i:(0,i))
    sh=jax.ShapeDtypeStruct((rows,width),BF16); kh=jax.ShapeDtypeStruct((keys,width),BF16)
    return pl.pallas_call(attn_bwd_kernel,grid=(width//128,),
        in_specs=[spec,ks,ks,ks,ks,spec,spec,pl.BlockSpec((1,8,rows),lambda i:(i,0,0))],
        out_specs=[spec,ks,ks,ks,ks],
        out_shape=[sh,kh,kh,kh,kh],
        compiler_params=pltpu.CompilerParams(vmem_limit_bytes=48<<20),name="attn_bwd",
        cost_estimate=pl.CostEstimate(flops=10*rows*2*keys*width,bytes_accessed=26*rows*width,transcendentals=rows*2*keys*width//64))(q,ka,kb,va,vb,o,do,l)


def image_moves(shift):
    pairs = []
    for p in range(4):
        for c in range(2):
            for z in range(4):
                to_core, to_z = z // 2, 2 * c + (shift ^ (z & 1))
                pairs.append(((2 * p + c) * 4 + z, (2 * p + to_core) * 4 + to_z))
    return pairs


def gather_image(blocks):
    odd = lax.axis_index("seq") % 2
    parts = []
    for shift in range(2):
        mine = lax.dynamic_index_in_dim(blocks, odd ^ shift, 0, keepdims=False)
        parts.append(lax.ppermute(mine, ("dp", "seq"), image_moves(shift)))
    rows = parts[0].shape[0]
    swapped = jnp.where(odd == 0, jnp.stack(parts), jnp.stack(parts[::-1]))
    return swapped.reshape(2 * rows, parts[0].shape[1])


def return_image(rows_all):
    odd = lax.axis_index("seq") % 2
    halves = rows_all.reshape(2, rows_all.shape[0] // 2, rows_all.shape[1])
    parts = []
    for shift in range(2):
        mine = lax.dynamic_index_in_dim(halves, odd ^ shift, 0, keepdims=False)
        back = [(to, start) for start, to in image_moves(shift)]
        parts.append(lax.ppermute(mine, ("dp", "seq"), back))
    return jnp.where(odd == 0, jnp.stack(parts), jnp.stack(parts[::-1]))


def other_core(value):
    return lax.ppermute(value, "dp", [(i, i ^ 1) for i in range(lax.axis_size("dp"))])


def dot_nn(left, right):
    return dg(left, right, NN)


def norm_parts(value):
    centre = jnp.mean(value, axis=-1, keepdims=True)
    spread = jnp.mean(jnp.square(value - centre), axis=-1, keepdims=True)
    rstd = lax.rsqrt(spread + norm_eps)
    return ((value - centre) * rstd, rstd)


def norm_back(xhat, rstd, grad, gain):
    e = grad * gain
    return rstd * (
        e - jnp.mean(e, axis=-1, keepdims=True) - xhat * jnp.mean(e * xhat, axis=-1, keepdims=True)
    )


def local_fast(
    tokens, w_qkv, w_out, w_up, w_down, b_query, b_value, b_out, b_up, b_down,
    ln1_gain, ln1_bias, ln2_gain, ln2_bias, cotangent,
):
    d = tokens.shape[2]
    small = (b_query, b_value, b_out, b_up, b_down, ln1_gain, ln1_bias, ln2_gain, ln2_bias)
    sizes = [item.shape[0] for item in small]
    packed = lax.all_gather(jnp.concatenate(small), "dp", axis=0, tiled=False)
    vectors, at = [], 0
    for size in sizes:
        vectors.append(packed[:, at : at + size].reshape(1, -1).astype(F32))
        at += size
    bias_query, bias_value, bias_out, bias_up, bias_down, gain1, shift1, gain2, shift2 = vectors
    wq = lax.all_gather(w_qkv, "dp", axis=0, tiled=True)
    wo = lax.all_gather(w_out, "dp", axis=0, tiled=True)
    wu = lax.all_gather(w_up, "dp", axis=0, tiled=True)
    wd = lax.all_gather(w_down, "dp", axis=1, tiled=True)

    x_low = gather_image(tokens)
    cot_low = gather_image(cotangent)
    x = x_low.astype(F32)
    xhat1, rstd1 = norm_parts(x)
    n1 = (xhat1 * gain1 + shift1).astype(BF16)
    bias = jnp.concatenate([bias_query, jnp.zeros_like(bias_query), bias_value], axis=1)
    projected = (dot_nn(n1, wq) + bias).astype(BF16)
    q, k, v = (projected[:, i * d : (i + 1) * d] for i in range(3))
    kv_other = other_core(projected[:, d:])
    kb, vb = kv_other[:, :d], kv_other[:, d:]
    attended, lse = attn_fwd(q, k, kb, v, vb)
    residual = x + dot_nn(attended, wo) + bias_out
    xhat2, rstd2 = norm_parts(residual)
    n2 = (xhat2 * gain2 + shift2).astype(BF16)
    upward = dot_nn(n2, wu) + bias_up
    activated, activate_back = jax.vjp(activate, upward)
    act = activated.astype(BF16)
    result = return_image((residual + dot_nn(act, wd) + bias_down).astype(BF16))

    (grad_up,) = activate_back(dg(cot_low, wd, NT))
    grad_up = grad_up.astype(BF16)
    gn2 = dg(grad_up, wu, NT)
    grad_residual = cot_low.astype(F32) + norm_back(xhat2, rstd2, gn2, gain2)
    grad_attn = grad_residual.astype(BF16)
    grad_mixed = dg(grad_attn, wo, NT).astype(BF16)
    dq, dka, dkb, dva, dvb = attn_bwd(q, k, kb, v, vb, attended, grad_mixed, lse)
    dkv_other = other_core(jnp.concatenate([dkb, dvb], axis=1))
    dkv = (jnp.concatenate([dka, dva], axis=1).astype(F32) + dkv_other.astype(F32)).astype(BF16)
    gproj = jnp.concatenate([dq, dkv], axis=1)
    gn1 = dg(gproj, wq, NT)
    grad_input = return_image((grad_residual + norm_back(xhat1, rstd1, gn1, gain1)).astype(BF16))

    total = lambda value: jnp.sum(value, axis=0, dtype=F32)
    small_grads = (
        total(gproj[:, :d]), total(gproj[:, 2 * d :]), total(grad_attn), total(grad_up), total(cot_low),
        total(gn1 * xhat1), total(gn1), total(gn2 * xhat2), total(gn2),
    )
    packed_grads = jnp.concatenate([g.reshape(8, -1) for g in small_grads], axis=1)
    packed_grads = lax.psum(lax.psum_scatter(packed_grads, "dp", scatter_dimension=0, tiled=True), "seq")[0]

    def owned(grad, axis):
        part = lax.psum_scatter(grad.astype(BF16), "dp", scatter_dimension=axis, tiled=True)
        return lax.psum(part, "seq").astype(F32)

    g_down = owned(dg(act, cot_low, TN), 1)
    g_up = owned(dg(n2, grad_up, TN), 0)
    g_out = owned(dg(attended, grad_attn, TN), 0)
    g_qkv = owned(dg(n1, gproj, TN), 0)
    outs, at = [], 0
    for size in sizes:
        outs.append(packed_grads[at : at + size])
        at += size
    return (result, grad_input, g_qkv, g_out, g_up, g_down, *outs)


def solution(mesh):
    in_specs = (
        P("dp", "seq", None),
        P("dp", None),
        P("dp", None),
        P("dp", None),
        P(None, "dp"),
        P("dp"),
        P("dp"),
        P("dp"),
        P("dp"),
        P("dp"),
        P("dp"),
        P("dp"),
        P("dp"),
        P("dp"),
        P("dp", "seq", None),
    )
    out_specs = (
        P("dp", "seq", None),
        P("dp", "seq", None),
        P("dp", None),
        P("dp", None),
        P("dp", None),
        P(None, "dp"),
        P("dp"),
        P("dp"),
        P("dp"),
        P("dp"),
        P("dp"),
        P("dp"),
        P("dp"),
        P("dp"),
        P("dp"),
    )
    fn = local_fast if dict(mesh.shape) == {"dp": 8, "seq": 4} else local
    return jax.shard_map(fn, mesh=mesh, in_specs=in_specs, out_specs=out_specs, check_vma=False)
```

```python
import functools

import jax
import jax.numpy as jnp
from jax import lax
from jax.experimental import pallas as pl
from jax.experimental.pallas import tpu as pltpu
from jax.sharding import PartitionSpec as P

H = 16
DH = 64
MICRO = 2
IMG_MB = 1


norm_eps = 1e-06


def normalize(inputs, ln_gain, ln_offset):
    centre = jnp.mean(inputs, axis=-1, keepdims=True)
    spread = jnp.mean(jnp.square(inputs - centre), axis=-1, keepdims=True)
    return (inputs - centre) * lax.rsqrt(spread + norm_eps) * ln_gain + ln_offset


def activate(upward):
    return jax.nn.gelu(upward, approximate=True)


def add_pairs(first_set, second_set):
    return tuple(
        (first_item + second_item for first_item, second_item in zip(first_set, second_set))
    )


def forward_heads(queries, keyed, valued, factor):
    images, length, head_count, head_size = queries.shape
    block_rows = min(512, length)
    blocks = length // block_rows
    query_blocks = queries.reshape(images, blocks, block_rows, head_count, head_size)

    def forward_per_image(element):
        q_image, k_image, v_image = element

        def forward_per_block(q_block):
            scores = (
                jnp.einsum("qhd,khd->hqk", q_block, k_image, preferred_element_type=jnp.float32)
                * factor
            )
            row_max = jnp.max(scores, axis=-1, keepdims=True)
            exponent = jnp.exp(scores - row_max)
            row_total = jnp.sum(exponent, axis=-1, keepdims=True)
            attn_probs = (exponent / row_total).astype(jnp.bfloat16)
            mixture = jnp.einsum(
                "hqk,khd->qhd", attn_probs, v_image, preferred_element_type=jnp.float32
            )
            return (mixture, row_max[..., 0] + jnp.log(row_total[..., 0]))

        return lax.map(forward_per_block, q_image)

    mixture, log_total = lax.map(forward_per_image, (query_blocks, keyed, valued))
    return (mixture.reshape(images, length, head_count * head_size), log_total)


def backward_heads(queries, keyed, valued, grad_mixed, log_total, factor):
    images, length, head_count, head_size = queries.shape
    block_rows = min(512, length)
    blocks = length // block_rows
    query_blocks = queries.reshape(images, blocks, block_rows, head_count, head_size)
    grad_blocks = grad_mixed.reshape(images, blocks, block_rows, head_count, head_size)

    def backward_per_image(element):
        q_image, k_image, v_image, g_image, l_image = element

        def backward_per_block(running, pieces):
            grad_key, grad_value = running
            q_block, g_block, l_block = pieces
            scores = (
                jnp.einsum("qhd,khd->hqk", q_block, k_image, preferred_element_type=jnp.float32)
                * factor
            )
            full_probs = jnp.exp(scores - l_block[..., None])
            grad_probs = jnp.einsum(
                "qhd,khd->hqk", g_block, v_image, preferred_element_type=jnp.float32
            )
            row_inner = jnp.sum(full_probs * grad_probs, axis=-1, keepdims=True)
            grad_scores = (full_probs * (grad_probs - row_inner)).astype(jnp.bfloat16)
            grad_query = (
                jnp.einsum("hqk,khd->qhd", grad_scores, k_image, preferred_element_type=jnp.float32)
                * factor
            )
            grad_key = (
                grad_key
                + jnp.einsum(
                    "hqk,qhd->khd", grad_scores, q_block, preferred_element_type=jnp.float32
                )
                * factor
            )
            grad_value = grad_value + jnp.einsum(
                "hqk,qhd->khd",
                full_probs.astype(jnp.bfloat16),
                g_block,
                preferred_element_type=jnp.float32,
            )
            return ((grad_key, grad_value), grad_query)

        empty_sum = jnp.zeros((length, head_count, head_size), jnp.float32)
        (grad_key, grad_value), grad_query = lax.scan(
            backward_per_block, (empty_sum, empty_sum), (q_image, g_image, l_image)
        )
        return (grad_query.reshape(length, head_count, head_size), grad_key, grad_value)

    return lax.map(backward_per_image, (query_blocks, keyed, valued, grad_blocks, log_total))


def weight_grads(
    normed_one_low,
    grad_projected,
    mixed_tokens,
    grad_attn_low,
    normed_two_low,
    grad_upward_low,
    activated_low,
    grad_branch,
    model_width,
):
    grad_qkv = jnp.einsum(
        "ptd,pte->de", normed_one_low, grad_projected, preferred_element_type=jnp.float32
    )
    grad_bquery = jnp.sum(grad_projected[:, :, :model_width], axis=(0, 1), dtype=jnp.float32)
    grad_bvalue = jnp.sum(grad_projected[:, :, 2 * model_width :], axis=(0, 1), dtype=jnp.float32)
    grad_wout = jnp.einsum(
        "pte,ptd->ed", mixed_tokens, grad_attn_low, preferred_element_type=jnp.float32
    )
    grad_bout = jnp.sum(grad_attn_low, axis=(0, 1), dtype=jnp.float32)
    grad_up = jnp.einsum(
        "ptd,ptf->df", normed_two_low, grad_upward_low, preferred_element_type=jnp.float32
    )
    grad_bup = jnp.sum(grad_upward_low, axis=(0, 1), dtype=jnp.float32)
    grad_down = jnp.einsum(
        "ptf,ptd->fd", activated_low, grad_branch, preferred_element_type=jnp.float32
    )
    grad_bdown = jnp.sum(grad_branch, axis=(0, 1), dtype=jnp.float32)
    return (
        grad_qkv,
        grad_wout,
        grad_up,
        grad_down,
        grad_bquery,
        grad_bvalue,
        grad_bout,
        grad_bup,
        grad_bdown,
    )


def local(
    tokens,
    w_qkv,
    w_out,
    w_up,
    w_down,
    b_query,
    b_value,
    b_out,
    b_up,
    b_down,
    ln1_gain,
    ln1_bias,
    ln2_gain,
    ln2_bias,
    cotangent,
):
    seq_count = lax.axis_size("seq")
    local_patches = tokens.shape[1]
    model_width = tokens.shape[2]
    patches = local_patches * seq_count
    head_local = H // seq_count
    factor = DH ** (-0.5)
    gathered = (
        lax.all_gather(w_qkv, "dp", axis=0, tiled=True),
        lax.all_gather(w_out, "dp", axis=0, tiled=True),
        lax.all_gather(w_up, "dp", axis=0, tiled=True),
        lax.all_gather(w_down, "dp", axis=1, tiled=True),
        lax.all_gather(b_query, "dp", axis=0, tiled=True),
        lax.all_gather(b_value, "dp", axis=0, tiled=True),
        lax.all_gather(b_out, "dp", axis=0, tiled=True),
        lax.all_gather(b_up, "dp", axis=0, tiled=True),
        lax.all_gather(b_down, "dp", axis=0, tiled=True),
        lax.all_gather(ln1_gain, "dp", axis=0, tiled=True),
        lax.all_gather(ln1_bias, "dp", axis=0, tiled=True),
        lax.all_gather(ln2_gain, "dp", axis=0, tiled=True),
        lax.all_gather(ln2_bias, "dp", axis=0, tiled=True),
    )
    outputs = []
    grad_inputs = []
    kept = []
    for micro_idx in range(MICRO):
        w_qkv_full, w_out_full, w_up_full, w_down_full = (
            gathered[0],
            gathered[1],
            gathered[2],
            gathered[3],
        )
        vectors = [piece.astype(jnp.float32) for piece in gathered[4:]]
        (
            bias_query,
            bias_value,
            bias_out,
            bias_up,
            bias_down,
            gain_one,
            offset_one,
            gain_two,
            offset_two,
        ) = vectors
        start = micro_idx * IMG_MB
        inputs = tokens[start : start + IMG_MB].astype(jnp.float32)
        normed_one, norm_one_back = jax.vjp(normalize, inputs, gain_one, offset_one)
        normed_one_low = normed_one.astype(jnp.bfloat16)
        qkv_bias = jnp.concatenate([bias_query, jnp.zeros_like(bias_query), bias_value])
        projected = (
            jnp.einsum(
                "ptd,de->pte", normed_one_low, w_qkv_full, preferred_element_type=jnp.float32
            )
            + qkv_bias
        )
        projected_low = projected.astype(jnp.bfloat16).reshape(
            IMG_MB, local_patches, 3, model_width
        )
        by_heads = lax.all_to_all(projected_low, "seq", split_axis=3, concat_axis=1, tiled=True)
        queries = by_heads[:, :, 0].reshape(IMG_MB, patches, head_local, DH)
        keyed = by_heads[:, :, 1].reshape(IMG_MB, patches, head_local, DH)
        valued = by_heads[:, :, 2].reshape(IMG_MB, patches, head_local, DH)
        attended, log_total = forward_heads(queries, keyed, valued, factor)
        attended_low = attended.astype(jnp.bfloat16)
        mixed_tokens = lax.all_to_all(attended_low, "seq", split_axis=1, concat_axis=2, tiled=True)
        residual = (
            inputs
            + jnp.einsum(
                "pte,ed->ptd", mixed_tokens, w_out_full, preferred_element_type=jnp.float32
            )
            + bias_out
        )
        normed_two, norm_two_back = jax.vjp(normalize, residual, gain_two, offset_two)
        normed_two_low = normed_two.astype(jnp.bfloat16)
        upward = (
            jnp.einsum("ptd,df->ptf", normed_two_low, w_up_full, preferred_element_type=jnp.float32)
            + bias_up
        )
        activated, activate_back = jax.vjp(activate, upward)
        activated_low = activated.astype(jnp.bfloat16)
        layer_out = (
            residual
            + jnp.einsum(
                "ptf,fd->ptd", activated_low, w_down_full, preferred_element_type=jnp.float32
            )
            + bias_down
        )
        outputs.append(layer_out.astype(jnp.bfloat16))
        grad_result = cotangent[start : start + IMG_MB].astype(jnp.float32)
        grad_branch = grad_result.astype(jnp.bfloat16)
        grad_active = jnp.einsum(
            "ptd,fd->ptf", grad_branch, w_down_full, preferred_element_type=jnp.float32
        )
        (grad_upward,) = activate_back(grad_active)
        grad_upward_low = grad_upward.astype(jnp.bfloat16)
        grad_normed_two = jnp.einsum(
            "ptf,df->ptd", grad_upward_low, w_up_full, preferred_element_type=jnp.float32
        )
        grad_from_two, grad_gain2, grad_bias2 = norm_two_back(grad_normed_two)
        grad_residual = grad_result + grad_from_two
        grad_attn_low = grad_residual.astype(jnp.bfloat16)
        grad_mixed = jnp.einsum(
            "ptd,ed->pte", grad_attn_low, w_out_full, preferred_element_type=jnp.float32
        ).astype(jnp.bfloat16)
        grad_heads = lax.all_to_all(grad_mixed, "seq", split_axis=2, concat_axis=1, tiled=True)
        grad_query, grad_key, grad_value = backward_heads(
            queries,
            keyed,
            valued,
            grad_heads.reshape(IMG_MB, patches, head_local, DH),
            log_total,
            factor,
        )
        stacked = (
            jnp.stack([grad_query, grad_key, grad_value], axis=2)
            .reshape(IMG_MB, patches, 3, head_local * DH)
            .astype(jnp.bfloat16)
        )
        grad_parts = lax.all_to_all(stacked, "seq", split_axis=1, concat_axis=3, tiled=True)
        grad_projected = grad_parts.reshape(IMG_MB, local_patches, 3 * model_width)
        grad_normed_one = jnp.einsum(
            "pte,de->ptd", grad_projected, w_qkv_full, preferred_element_type=jnp.float32
        )
        grad_from_one, grad_gain1, grad_bias1 = norm_one_back(grad_normed_one)
        grad_inputs.append((grad_residual + grad_from_one).astype(jnp.bfloat16))
        norm_grads = (grad_gain1, grad_bias1, grad_gain2, grad_bias2)
        norm_total = norm_grads if micro_idx == 0 else add_pairs(norm_total, norm_grads)
        kept.append(
            (
                normed_one_low,
                grad_projected,
                mixed_tokens,
                grad_attn_low,
                normed_two_low,
                grad_upward_low,
                activated_low,
                grad_branch,
            )
        )
    joined = [jnp.concatenate([item[index] for item in kept], axis=0) for index in range(8)]
    big = weight_grads(
        joined[0],
        joined[1],
        joined[2],
        joined[3],
        joined[4],
        joined[5],
        joined[6],
        joined[7],
        model_width,
    )
    owned = (
        lax.psum_scatter(big[0].astype(jnp.bfloat16), "dp", scatter_dimension=0, tiled=True).astype(
            jnp.float32
        ),
        lax.psum_scatter(big[1].astype(jnp.bfloat16), "dp", scatter_dimension=0, tiled=True).astype(
            jnp.float32
        ),
        lax.psum_scatter(big[2].astype(jnp.bfloat16), "dp", scatter_dimension=0, tiled=True).astype(
            jnp.float32
        ),
        lax.psum_scatter(big[3].astype(jnp.bfloat16), "dp", scatter_dimension=1, tiled=True).astype(
            jnp.float32
        ),
        lax.psum_scatter(big[4].astype(jnp.bfloat16), "dp", scatter_dimension=0, tiled=True).astype(
            jnp.float32
        ),
        lax.psum_scatter(big[5].astype(jnp.bfloat16), "dp", scatter_dimension=0, tiled=True).astype(
            jnp.float32
        ),
        lax.psum_scatter(big[6].astype(jnp.bfloat16), "dp", scatter_dimension=0, tiled=True).astype(
            jnp.float32
        ),
        lax.psum_scatter(big[7].astype(jnp.bfloat16), "dp", scatter_dimension=0, tiled=True).astype(
            jnp.float32
        ),
        lax.psum_scatter(big[8].astype(jnp.bfloat16), "dp", scatter_dimension=0, tiled=True).astype(
            jnp.float32
        ),
        lax.psum_scatter(
            norm_total[0].astype(jnp.bfloat16), "dp", scatter_dimension=0, tiled=True
        ).astype(jnp.float32),
        lax.psum_scatter(
            norm_total[1].astype(jnp.bfloat16), "dp", scatter_dimension=0, tiled=True
        ).astype(jnp.float32),
        lax.psum_scatter(
            norm_total[2].astype(jnp.bfloat16), "dp", scatter_dimension=0, tiled=True
        ).astype(jnp.float32),
        lax.psum_scatter(
            norm_total[3].astype(jnp.bfloat16), "dp", scatter_dimension=0, tiled=True
        ).astype(jnp.float32),
    )
    owned = (
        lax.psum(owned[0].astype(jnp.bfloat16), "seq").astype(jnp.float32),
        lax.psum(owned[1].astype(jnp.bfloat16), "seq").astype(jnp.float32),
        lax.psum(owned[2].astype(jnp.bfloat16), "seq").astype(jnp.float32),
        lax.psum(owned[3].astype(jnp.bfloat16), "seq").astype(jnp.float32),
        lax.psum(owned[4].astype(jnp.bfloat16), "seq").astype(jnp.float32),
        lax.psum(owned[5].astype(jnp.bfloat16), "seq").astype(jnp.float32),
        lax.psum(owned[6].astype(jnp.bfloat16), "seq").astype(jnp.float32),
        lax.psum(owned[7].astype(jnp.bfloat16), "seq").astype(jnp.float32),
        lax.psum(owned[8].astype(jnp.bfloat16), "seq").astype(jnp.float32),
        lax.psum(owned[9].astype(jnp.bfloat16), "seq").astype(jnp.float32),
        lax.psum(owned[10].astype(jnp.bfloat16), "seq").astype(jnp.float32),
        lax.psum(owned[11].astype(jnp.bfloat16), "seq").astype(jnp.float32),
        lax.psum(owned[12].astype(jnp.bfloat16), "seq").astype(jnp.float32),
    )
    return (
        jnp.concatenate(outputs, axis=0),
        jnp.concatenate(grad_inputs, axis=0),
        owned[0],
        owned[1],
        owned[2],
        owned[3],
        owned[4],
        owned[5],
        owned[6],
        owned[7],
        owned[8],
        owned[9],
        owned[10],
        owned[11],
        owned[12],
    )


F32=jnp.float32; BF16=jnp.bfloat16
NT=(((1,),(1,)),((),())); TN=(((0,),(0,)),((),())); NN=(((1,),(0,)),((),()))
def dg(a,b,dims): return lax.dot_general(a,b,dims,preferred_element_type=F32)

def attn_fwd_kernel(q_ref, ka_ref, kb_ref, va_ref, vb_ref, o_ref, l_ref):
    rows=q_ref.shape[0]
    lane=lax.broadcasted_iota(jnp.int32,(rows,128),1)
    q=q_ref[...]*jnp.asarray(0.125,BF16)
    outs=[]; ls=[]
    for h in range(2):
        qh=jnp.where((lane<64) if h==0 else (lane>=64), q, jnp.zeros_like(q))
        sa=dg(ka_ref[...],qh,NT); sb=dg(kb_ref[...],qh,NT)
        m=jnp.maximum(jnp.max(sa,axis=0,keepdims=True),jnp.max(sb,axis=0,keepdims=True))
        pa=jnp.exp(sa-m); pb=jnp.exp(sb-m)
        tot=jnp.sum(pa,axis=0,keepdims=True)+jnp.sum(pb,axis=0,keepdims=True)
        oT=dg(va_ref[...],pa.astype(BF16),TN)+dg(vb_ref[...],pb.astype(BF16),TN)
        outs.append(oT[64*h:64*h+64]*(1.0/tot))
        ls.append(m+jnp.log(tot))
    oT=jnp.concatenate(outs,axis=0)
    o_ref[...]=oT.T.astype(BF16)
    l_ref[0]=jnp.concatenate(ls+[jnp.zeros((6,rows),F32)],axis=0)

def attn_fwd(q,ka,kb,va,vb):
    rows,width=q.shape
    spec=pl.BlockSpec((rows,128),lambda i:(0,i))
    keys=ka.shape[0]
    ks=pl.BlockSpec((keys,128),lambda i:(0,i))
    return pl.pallas_call(attn_fwd_kernel,grid=(width//128,),
        in_specs=[spec,ks,ks,ks,ks],
        out_specs=[spec,pl.BlockSpec((1,8,rows),lambda i:(i,0,0))],
        out_shape=[jax.ShapeDtypeStruct((rows,width),BF16),jax.ShapeDtypeStruct((width//128,8,rows),F32)],
        compiler_params=pltpu.CompilerParams(vmem_limit_bytes=48<<20),name="attn_fwd",
        cost_estimate=pl.CostEstimate(flops=4*rows*2*keys*width,bytes_accessed=12*rows*width,transcendentals=rows*2*keys*width//64))(q,ka,kb,va,vb)

def attn_bwd_kernel(q_ref, ka_ref, kb_ref, va_ref, vb_ref, o_ref, do_ref, l_ref, dq_ref, dka_ref, dkb_ref, dva_ref, dvb_ref):
    rows=q_ref.shape[0]
    lane=lax.broadcasted_iota(jnp.int32,(rows,128),1)
    q=q_ref[...]*jnp.asarray(0.125,BF16)
    do=do_ref[...]
    t=(do.astype(F32)*o_ref[...].astype(F32)).T
    klane=lax.broadcasted_iota(jnp.int32,(ka_ref.shape[0],128),1)
    dq=None; dk=[None,None]; dv=[None,None]
    add=lambda a,b: b if a is None else a+b
    for h in range(2):
        sel=(lane<64) if h==0 else (lane>=64)
        ksel=(klane<64) if h==0 else (klane>=64)
        qh=jnp.where(sel,q,jnp.zeros_like(q)); doh=jnp.where(sel,do,jnp.zeros_like(do))
        delta=jnp.sum(t[64*h:64*h+64],axis=0,keepdims=True)
        lse=l_ref[0,h:h+1,:]
        for n,(k_ref,v_ref) in enumerate(((ka_ref,va_ref),(kb_ref,vb_ref))):
            s=dg(k_ref[...],qh,NT)
            p=jnp.exp(s-lse)
            dp=dg(v_ref[...],doh,NT)
            ds=(p*(dp-delta)).astype(BF16)
            dv[n]=add(dv[n],dg(p.astype(BF16),doh,NN))
            dk[n]=add(dk[n],dg(ds,qh,NN))
            kh=jnp.where(ksel,k_ref[...],jnp.zeros_like(k_ref[...]))
            dq=add(dq,dg(kh,ds,TN))
    dq_ref[...]=(dq*0.125).T.astype(BF16)
    dka_ref[...]=dk[0].astype(BF16); dkb_ref[...]=dk[1].astype(BF16)
    dva_ref[...]=dv[0].astype(BF16); dvb_ref[...]=dv[1].astype(BF16)

def attn_bwd(q,ka,kb,va,vb,o,do,l):
    rows,width=q.shape; keys=ka.shape[0]
    spec=pl.BlockSpec((rows,128),lambda i:(0,i))
    ks=pl.BlockSpec((keys,128),lambda i:(0,i))
    sh=jax.ShapeDtypeStruct((rows,width),BF16); kh=jax.ShapeDtypeStruct((keys,width),BF16)
    return pl.pallas_call(attn_bwd_kernel,grid=(width//128,),
        in_specs=[spec,ks,ks,ks,ks,spec,spec,pl.BlockSpec((1,8,rows),lambda i:(i,0,0))],
        out_specs=[spec,ks,ks,ks,ks],
        out_shape=[sh,kh,kh,kh,kh],
        compiler_params=pltpu.CompilerParams(vmem_limit_bytes=48<<20),name="attn_bwd",
        cost_estimate=pl.CostEstimate(flops=10*rows*2*keys*width,bytes_accessed=26*rows*width,transcendentals=rows*2*keys*width//64))(q,ka,kb,va,vb,o,do,l)


def image_moves(shift):
    pairs = []
    for p in range(4):
        for c in range(2):
            for z in range(4):
                to_core, to_z = z // 2, 2 * c + (shift ^ (z & 1))
                pairs.append(((2 * p + c) * 4 + z, (2 * p + to_core) * 4 + to_z))
    return pairs


def gather_image(blocks):
    odd = lax.axis_index("seq") % 2
    parts = []
    for shift in range(2):
        mine = lax.dynamic_index_in_dim(blocks, odd ^ shift, 0, keepdims=False)
        parts.append(lax.ppermute(mine, ("dp", "seq"), image_moves(shift)))
    rows = parts[0].shape[0]
    swapped = jnp.where(odd == 0, jnp.stack(parts), jnp.stack(parts[::-1]))
    return swapped.reshape(2 * rows, parts[0].shape[1])


def return_image(rows_all):
    odd = lax.axis_index("seq") % 2
    halves = rows_all.reshape(2, rows_all.shape[0] // 2, rows_all.shape[1])
    parts = []
    for shift in range(2):
        mine = lax.dynamic_index_in_dim(halves, odd ^ shift, 0, keepdims=False)
        back = [(to, start) for start, to in image_moves(shift)]
        parts.append(lax.ppermute(mine, ("dp", "seq"), back))
    return jnp.where(odd == 0, jnp.stack(parts), jnp.stack(parts[::-1]))


def other_core(value):
    return lax.ppermute(value, "dp", [(i, i ^ 1) for i in range(lax.axis_size("dp"))])


def dot_nn(left, right):
    return dg(left, right, NN)


def norm_parts(value):
    centre = jnp.mean(value, axis=-1, keepdims=True)
    spread = jnp.mean(jnp.square(value - centre), axis=-1, keepdims=True)
    rstd = lax.rsqrt(spread + norm_eps)
    return ((value - centre) * rstd, rstd)


def norm_back(xhat, rstd, grad, gain):
    e = grad * gain
    return rstd * (
        e - jnp.mean(e, axis=-1, keepdims=True) - xhat * jnp.mean(e * xhat, axis=-1, keepdims=True)
    )


MESH = pl.DeviceIdType.MESH
HBM = pltpu.MemorySpace.HBM


def flip(value, bits):
    return lax.ppermute(value, "dp", [(i, i ^ bits) for i in range(8)])


def flip_z(value, bits):
    return lax.ppermute(value, "seq", [(i, i ^ bits) for i in range(4)])


def after(value, *earlier):
    return lax.optimization_barrier((value,) + earlier)[0]


def finish_kernel(a01, a2, b01, b2, out, kept, in_sem, out_sem, send_sem, recv_sem):
    d, z = lax.axis_index("dp"), lax.axis_index("seq")
    core, x, y = lax.rem(d, 2), lax.rem(d // 2, 2), d // 4
    sibling = (d + 1 - 2 * core, z)
    half = a01.shape[2]
    barrier = pltpu.get_barrier_semaphore()
    pl.semaphore_signal(barrier, inc=1, device_id=sibling, device_id_type=MESH)
    pl.semaphore_wait(barrier, 1)
    pieces = (
        (a01.at[0], y, x, 0), (b01.at[0], y, x, 1),
        (a01.at[1], y, 1 - x, 0), (b01.at[1], 1 - y, x, 1),
        (a2.at[0], 1 - y, x, 0), (b2.at[0], y, 1 - x, 1),
        (a2.at[1], 1 - y, 1 - x, 0), (b2.at[1], 1 - y, 1 - x, 1),
    )
    sends, loads, stores = [], [], []
    for k, (piece, py, px, side) in enumerate(pieces):
        row = pl.multiple_of(((py * 2 + px) * 2 + core) * 128, 128)
        target = out.at[pl.ds(row, 128), pl.ds(side * half, half)]
        sends.append(
            pltpu.make_async_remote_copy(
                src_ref=piece, dst_ref=target, send_sem=send_sem.at[k], recv_sem=recv_sem.at[k],
                device_id=sibling, device_id_type=MESH,
            )
        )
        loads.append(pltpu.make_async_copy(piece, kept.at[k], in_sem.at[k]))
        stores.append(pltpu.make_async_copy(kept.at[k], target, out_sem.at[k]))
    for k in range(8):
        sends[k].start()
        loads[k].start()
    for k in range(8):
        loads[k].wait()
        stores[k].start()
    for k in range(8):
        stores[k].wait()
        sends[k].wait()


def finish(parts, ident):
    half = parts[0].shape[2]
    return pl.pallas_call(
        finish_kernel,
        in_specs=[pl.BlockSpec(memory_space=pl.ANY)] * 4,
        out_specs=pl.BlockSpec(memory_space=HBM),
        out_shape=jax.ShapeDtypeStruct((1024, 2 * half), BF16),
        scratch_shapes=[pltpu.VMEM((8, 128, half), BF16)] + [pltpu.SemaphoreType.DMA((8,))] * 4,
        compiler_params=pltpu.CompilerParams(collective_id=ident, has_side_effects=True),
        cost_estimate=pl.CostEstimate(flops=0, bytes_accessed=8192 * half, transcendentals=0),
        name="finish%d" % ident,
    )(*parts)


def first_hop(shard):
    half = shard.shape[1] // 2
    a, b = shard[:, :half], shard[:, half:]
    return jnp.stack([a, flip(a, 2)]), jnp.stack([b, flip(b, 4)])


def second_hop(first):
    return first[0], flip(first[0], 4), first[1], flip(first[1], 2)


def relative(value, order, me):
    return jnp.concatenate(
        [lax.dynamic_slice_in_dim(value, 128 * (me ^ r), 128, axis=1) for r in order], axis=1
    )


def to_sibling(odd, right):
    half = right.shape[1] // 2
    return [flip(dg(odd, right[:, i * half : (i + 1) * half], TN).astype(BF16), 1) for i in range(2)]


def f32_add(left, right):
    return left.astype(F32) + right.astype(F32)


def low_add(left, right):
    return f32_add(left, right).astype(BF16)


def scatter(even, right, from_sibling):
    half = right.shape[1] // 2
    ga, gb = (
        (dg(even, right[:, i * half : (i + 1) * half], TN) + from_sibling[i].astype(F32)).astype(BF16)
        for i in range(2)
    )
    ga2 = low_add(ga[:256], flip(ga[256:], 4))
    gb_keep = jnp.concatenate([gb[:128], gb[256:384]])
    gb2 = low_add(gb_keep, flip(jnp.concatenate([gb[128:256], gb[384:]]), 2))
    return low_add(ga2[:128], flip(ga2[128:], 2)), low_add(gb2[:128], flip(gb2[128:], 4))


def sum_z(halves):
    odd = lax.axis_index("seq") % 2 == 1
    keep = jnp.where(odd, halves[1], halves[0])
    give = jnp.where(odd, halves[0], halves[1])
    kept = lax.optimization_barrier(low_add(keep, flip_z(give, 1)))
    mine = lax.optimization_barrier(low_add(kept, flip_z(kept, 2)))
    other = flip_z(mine, 1)
    return jnp.concatenate([jnp.where(odd, other, mine), jnp.where(odd, mine, other)], axis=1).astype(F32)


def local_fast(
    tokens, w_qkv, w_out, w_up, w_down, b_query, b_value, b_out, b_up, b_down,
    ln1_gain, ln1_bias, ln2_gain, ln2_bias, cotangent,
):
    d = tokens.shape[2]
    me = lax.axis_index("dp")
    small = (b_query, b_value, b_out, b_up, b_down, ln1_gain, ln1_bias, ln2_gain, ln2_bias)
    sizes = [item.shape[0] for item in small]

    x_low = gather_image(tokens)
    pack = jnp.concatenate(small).reshape(1, -1)
    for bits in (1, 2, 4):
        pack = jnp.concatenate([pack, flip(pack, bits)])
    packed = jnp.concatenate([lax.dynamic_slice_in_dim(pack, me ^ r, 1, axis=0) for r in range(8)])
    vectors, at = [], 0
    for size in sizes:
        vectors.append(packed[:, at : at + size].reshape(1, -1).astype(F32))
        at += size
    bias_query, bias_value, bias_out, bias_up, bias_down, gain1, shift1, gain2, shift2 = vectors

    qkv1 = first_hop(w_qkv)
    qkv2 = second_hop(qkv1)
    out1 = first_hop(after(w_out, *qkv1))
    out2 = second_hop(out1)
    up1 = first_hop(after(w_up, *qkv2))
    up2 = second_hop(up1)
    down1 = first_hop(after(w_down.T, *out2))
    down2 = second_hop(down1)
    wq = finish(qkv2, 0)
    cot_low = gather_image(after(cotangent, x_low))

    x = x_low.astype(F32)
    xhat1, rstd1 = norm_parts(x)
    n1 = (xhat1 * gain1 + shift1).astype(BF16)
    bias = jnp.concatenate([bias_query, jnp.zeros_like(bias_query), bias_value], axis=1)
    projected = (dot_nn(n1, wq) + bias).astype(BF16)
    q, k, v = (projected[:, i * d : (i + 1) * d] for i in range(3))
    kv_other = other_core(projected[:, d:])
    kb, vb = kv_other[:, :d], kv_other[:, d:]
    attended, lse = attn_fwd(q, k, kb, v, vb)
    wo = finish(out2, 1)
    residual = x + dot_nn(attended, wo) + bias_out
    xhat2, rstd2 = norm_parts(residual)
    n2 = (xhat2 * gain2 + shift2).astype(BF16)
    wu = finish(up2, 2)
    upward = dot_nn(n2, wu) + bias_up
    activated, activate_back = jax.vjp(activate, upward)
    act = activated.astype(BF16)
    down_sib = to_sibling(relative(cot_low, (1, 3, 5, 7), me), act)
    g_down = scatter(relative(cot_low, (0, 2, 4, 6), me), act, down_sib)
    wdt = finish(down2, 3)
    result = return_image((residual + dg(act, wdt, NT) + bias_down).astype(BF16))

    (grad_up,) = activate_back(dg(cot_low, wdt, NN))
    grad_up = grad_up.astype(BF16)
    up_sib = to_sibling(relative(n2, (1, 3, 5, 7), me), grad_up)
    g_up = scatter(relative(n2, (0, 2, 4, 6), me), grad_up, up_sib)
    gn2 = dg(grad_up, wu, NT)
    grad_residual = cot_low.astype(F32) + norm_back(xhat2, rstd2, gn2, gain2)
    grad_attn = grad_residual.astype(BF16)
    out_sib = to_sibling(relative(attended, (1, 3, 5, 7), me), grad_attn)
    g_out = scatter(relative(attended, (0, 2, 4, 6), me), grad_attn, out_sib)
    grad_mixed = dg(grad_attn, wo, NT).astype(BF16)
    dq, dka, dkb, dva, dvb = attn_bwd(q, k, kb, v, vb, attended, grad_mixed, lse)
    dkv_other = other_core(jnp.concatenate([dkb, dvb], axis=1))
    dkv = (jnp.concatenate([dka, dva], axis=1).astype(F32) + dkv_other.astype(F32)).astype(BF16)
    gproj = jnp.concatenate([dq, dkv], axis=1)
    qkv_sib = to_sibling(relative(n1, (1, 3, 5, 7), me), gproj)
    g_qkv = scatter(relative(n1, (0, 2, 4, 6), me), gproj, qkv_sib)
    gn1 = dg(gproj, wq, NT)
    grad_input = return_image((grad_residual + norm_back(xhat1, rstd1, gn1, gain1)).astype(BF16))

    total = lambda value: jnp.sum(value, axis=0, dtype=F32)
    small_grads = (
        total(gproj[:, :d]), total(gproj[:, 2 * d :]), total(grad_attn), total(grad_up), total(cot_low),
        total(gn1 * xhat1), total(gn1), total(gn2 * xhat2), total(gn2),
    )
    sums = jnp.concatenate([g.reshape(8, -1) for g in small_grads], axis=1)
    for bits in (1, 2, 4):
        sums = lax.optimization_barrier(sums + flip(sums, bits))
    for bits in (1, 2):
        sums = lax.optimization_barrier(sums + flip_z(sums, bits))
    mine = lax.dynamic_slice_in_dim(sums, me, 1, axis=0)[0]
    outs, at = [], 0
    for size in sizes:
        outs.append(mine[at : at + size])
        at += size
    return (result, grad_input, sum_z(g_qkv), sum_z(g_out), sum_z(g_up), sum_z(g_down).T, *outs)


def solution(mesh):
    in_specs = (
        P("dp", "seq", None),
        P("dp", None),
        P("dp", None),
        P("dp", None),
        P(None, "dp"),
        P("dp"),
        P("dp"),
        P("dp"),
        P("dp"),
        P("dp"),
        P("dp"),
        P("dp"),
        P("dp"),
        P("dp"),
        P("dp", "seq", None),
    )
    out_specs = (
        P("dp", "seq", None),
        P("dp", "seq", None),
        P("dp", None),
        P("dp", None),
        P("dp", None),
        P(None, "dp"),
        P("dp"),
        P("dp"),
        P("dp"),
        P("dp"),
        P("dp"),
        P("dp"),
        P("dp"),
        P("dp"),
        P("dp"),
    )
    fn = local_fast if dict(mesh.shape) == {"dp": 8, "seq": 4} else local
    return jax.shard_map(fn, mesh=mesh, in_specs=in_specs, out_specs=out_specs, check_vma=False)
```

```python
import functools

import jax
import jax.numpy as jnp
from jax import lax
from jax.experimental import pallas as pl
from jax.experimental.pallas import tpu as pltpu
from jax.sharding import PartitionSpec as P

H = 16
DH = 64
MICRO = 2
IMG_MB = 1


norm_eps = 1e-06


def normalize(inputs, ln_gain, ln_offset):
    centre = jnp.mean(inputs, axis=-1, keepdims=True)
    spread = jnp.mean(jnp.square(inputs - centre), axis=-1, keepdims=True)
    return (inputs - centre) * lax.rsqrt(spread + norm_eps) * ln_gain + ln_offset


def activate(upward):
    return jax.nn.gelu(upward, approximate=True)


def add_pairs(first_set, second_set):
    return tuple(
        (first_item + second_item for first_item, second_item in zip(first_set, second_set))
    )


def forward_heads(queries, keyed, valued, factor):
    images, length, head_count, head_size = queries.shape
    block_rows = min(512, length)
    blocks = length // block_rows
    query_blocks = queries.reshape(images, blocks, block_rows, head_count, head_size)

    def forward_per_image(element):
        q_image, k_image, v_image = element

        def forward_per_block(q_block):
            scores = (
                jnp.einsum("qhd,khd->hqk", q_block, k_image, preferred_element_type=jnp.float32)
                * factor
            )
            row_max = jnp.max(scores, axis=-1, keepdims=True)
            exponent = jnp.exp(scores - row_max)
            row_total = jnp.sum(exponent, axis=-1, keepdims=True)
            attn_probs = (exponent / row_total).astype(jnp.bfloat16)
            mixture = jnp.einsum(
                "hqk,khd->qhd", attn_probs, v_image, preferred_element_type=jnp.float32
            )
            return (mixture, row_max[..., 0] + jnp.log(row_total[..., 0]))

        return lax.map(forward_per_block, q_image)

    mixture, log_total = lax.map(forward_per_image, (query_blocks, keyed, valued))
    return (mixture.reshape(images, length, head_count * head_size), log_total)


def backward_heads(queries, keyed, valued, grad_mixed, log_total, factor):
    images, length, head_count, head_size = queries.shape
    block_rows = min(512, length)
    blocks = length // block_rows
    query_blocks = queries.reshape(images, blocks, block_rows, head_count, head_size)
    grad_blocks = grad_mixed.reshape(images, blocks, block_rows, head_count, head_size)

    def backward_per_image(element):
        q_image, k_image, v_image, g_image, l_image = element

        def backward_per_block(running, pieces):
            grad_key, grad_value = running
            q_block, g_block, l_block = pieces
            scores = (
                jnp.einsum("qhd,khd->hqk", q_block, k_image, preferred_element_type=jnp.float32)
                * factor
            )
            full_probs = jnp.exp(scores - l_block[..., None])
            grad_probs = jnp.einsum(
                "qhd,khd->hqk", g_block, v_image, preferred_element_type=jnp.float32
            )
            row_inner = jnp.sum(full_probs * grad_probs, axis=-1, keepdims=True)
            grad_scores = (full_probs * (grad_probs - row_inner)).astype(jnp.bfloat16)
            grad_query = (
                jnp.einsum("hqk,khd->qhd", grad_scores, k_image, preferred_element_type=jnp.float32)
                * factor
            )
            grad_key = (
                grad_key
                + jnp.einsum(
                    "hqk,qhd->khd", grad_scores, q_block, preferred_element_type=jnp.float32
                )
                * factor
            )
            grad_value = grad_value + jnp.einsum(
                "hqk,qhd->khd",
                full_probs.astype(jnp.bfloat16),
                g_block,
                preferred_element_type=jnp.float32,
            )
            return ((grad_key, grad_value), grad_query)

        empty_sum = jnp.zeros((length, head_count, head_size), jnp.float32)
        (grad_key, grad_value), grad_query = lax.scan(
            backward_per_block, (empty_sum, empty_sum), (q_image, g_image, l_image)
        )
        return (grad_query.reshape(length, head_count, head_size), grad_key, grad_value)

    return lax.map(backward_per_image, (query_blocks, keyed, valued, grad_blocks, log_total))


def weight_grads(
    normed_one_low,
    grad_projected,
    mixed_tokens,
    grad_attn_low,
    normed_two_low,
    grad_upward_low,
    activated_low,
    grad_branch,
    model_width,
):
    grad_qkv = jnp.einsum(
        "ptd,pte->de", normed_one_low, grad_projected, preferred_element_type=jnp.float32
    )
    grad_bquery = jnp.sum(grad_projected[:, :, :model_width], axis=(0, 1), dtype=jnp.float32)
    grad_bvalue = jnp.sum(grad_projected[:, :, 2 * model_width :], axis=(0, 1), dtype=jnp.float32)
    grad_wout = jnp.einsum(
        "pte,ptd->ed", mixed_tokens, grad_attn_low, preferred_element_type=jnp.float32
    )
    grad_bout = jnp.sum(grad_attn_low, axis=(0, 1), dtype=jnp.float32)
    grad_up = jnp.einsum(
        "ptd,ptf->df", normed_two_low, grad_upward_low, preferred_element_type=jnp.float32
    )
    grad_bup = jnp.sum(grad_upward_low, axis=(0, 1), dtype=jnp.float32)
    grad_down = jnp.einsum(
        "ptf,ptd->fd", activated_low, grad_branch, preferred_element_type=jnp.float32
    )
    grad_bdown = jnp.sum(grad_branch, axis=(0, 1), dtype=jnp.float32)
    return (
        grad_qkv,
        grad_wout,
        grad_up,
        grad_down,
        grad_bquery,
        grad_bvalue,
        grad_bout,
        grad_bup,
        grad_bdown,
    )


def local(
    tokens,
    w_qkv,
    w_out,
    w_up,
    w_down,
    b_query,
    b_value,
    b_out,
    b_up,
    b_down,
    ln1_gain,
    ln1_bias,
    ln2_gain,
    ln2_bias,
    cotangent,
):
    seq_count = lax.axis_size("seq")
    local_patches = tokens.shape[1]
    model_width = tokens.shape[2]
    patches = local_patches * seq_count
    head_local = H // seq_count
    factor = DH ** (-0.5)
    gathered = (
        lax.all_gather(w_qkv, "dp", axis=0, tiled=True),
        lax.all_gather(w_out, "dp", axis=0, tiled=True),
        lax.all_gather(w_up, "dp", axis=0, tiled=True),
        lax.all_gather(w_down, "dp", axis=1, tiled=True),
        lax.all_gather(b_query, "dp", axis=0, tiled=True),
        lax.all_gather(b_value, "dp", axis=0, tiled=True),
        lax.all_gather(b_out, "dp", axis=0, tiled=True),
        lax.all_gather(b_up, "dp", axis=0, tiled=True),
        lax.all_gather(b_down, "dp", axis=0, tiled=True),
        lax.all_gather(ln1_gain, "dp", axis=0, tiled=True),
        lax.all_gather(ln1_bias, "dp", axis=0, tiled=True),
        lax.all_gather(ln2_gain, "dp", axis=0, tiled=True),
        lax.all_gather(ln2_bias, "dp", axis=0, tiled=True),
    )
    outputs = []
    grad_inputs = []
    kept = []
    for micro_idx in range(MICRO):
        w_qkv_full, w_out_full, w_up_full, w_down_full = (
            gathered[0],
            gathered[1],
            gathered[2],
            gathered[3],
        )
        vectors = [piece.astype(jnp.float32) for piece in gathered[4:]]
        (
            bias_query,
            bias_value,
            bias_out,
            bias_up,
            bias_down,
            gain_one,
            offset_one,
            gain_two,
            offset_two,
        ) = vectors
        start = micro_idx * IMG_MB
        inputs = tokens[start : start + IMG_MB].astype(jnp.float32)
        normed_one, norm_one_back = jax.vjp(normalize, inputs, gain_one, offset_one)
        normed_one_low = normed_one.astype(jnp.bfloat16)
        qkv_bias = jnp.concatenate([bias_query, jnp.zeros_like(bias_query), bias_value])
        projected = (
            jnp.einsum(
                "ptd,de->pte", normed_one_low, w_qkv_full, preferred_element_type=jnp.float32
            )
            + qkv_bias
        )
        projected_low = projected.astype(jnp.bfloat16).reshape(
            IMG_MB, local_patches, 3, model_width
        )
        by_heads = lax.all_to_all(projected_low, "seq", split_axis=3, concat_axis=1, tiled=True)
        queries = by_heads[:, :, 0].reshape(IMG_MB, patches, head_local, DH)
        keyed = by_heads[:, :, 1].reshape(IMG_MB, patches, head_local, DH)
        valued = by_heads[:, :, 2].reshape(IMG_MB, patches, head_local, DH)
        attended, log_total = forward_heads(queries, keyed, valued, factor)
        attended_low = attended.astype(jnp.bfloat16)
        mixed_tokens = lax.all_to_all(attended_low, "seq", split_axis=1, concat_axis=2, tiled=True)
        residual = (
            inputs
            + jnp.einsum(
                "pte,ed->ptd", mixed_tokens, w_out_full, preferred_element_type=jnp.float32
            )
            + bias_out
        )
        normed_two, norm_two_back = jax.vjp(normalize, residual, gain_two, offset_two)
        normed_two_low = normed_two.astype(jnp.bfloat16)
        upward = (
            jnp.einsum("ptd,df->ptf", normed_two_low, w_up_full, preferred_element_type=jnp.float32)
            + bias_up
        )
        activated, activate_back = jax.vjp(activate, upward)
        activated_low = activated.astype(jnp.bfloat16)
        layer_out = (
            residual
            + jnp.einsum(
                "ptf,fd->ptd", activated_low, w_down_full, preferred_element_type=jnp.float32
            )
            + bias_down
        )
        outputs.append(layer_out.astype(jnp.bfloat16))
        grad_result = cotangent[start : start + IMG_MB].astype(jnp.float32)
        grad_branch = grad_result.astype(jnp.bfloat16)
        grad_active = jnp.einsum(
            "ptd,fd->ptf", grad_branch, w_down_full, preferred_element_type=jnp.float32
        )
        (grad_upward,) = activate_back(grad_active)
        grad_upward_low = grad_upward.astype(jnp.bfloat16)
        grad_normed_two = jnp.einsum(
            "ptf,df->ptd", grad_upward_low, w_up_full, preferred_element_type=jnp.float32
        )
        grad_from_two, grad_gain2, grad_bias2 = norm_two_back(grad_normed_two)
        grad_residual = grad_result + grad_from_two
        grad_attn_low = grad_residual.astype(jnp.bfloat16)
        grad_mixed = jnp.einsum(
            "ptd,ed->pte", grad_attn_low, w_out_full, preferred_element_type=jnp.float32
        ).astype(jnp.bfloat16)
        grad_heads = lax.all_to_all(grad_mixed, "seq", split_axis=2, concat_axis=1, tiled=True)
        grad_query, grad_key, grad_value = backward_heads(
            queries,
            keyed,
            valued,
            grad_heads.reshape(IMG_MB, patches, head_local, DH),
            log_total,
            factor,
        )
        stacked = (
            jnp.stack([grad_query, grad_key, grad_value], axis=2)
            .reshape(IMG_MB, patches, 3, head_local * DH)
            .astype(jnp.bfloat16)
        )
        grad_parts = lax.all_to_all(stacked, "seq", split_axis=1, concat_axis=3, tiled=True)
        grad_projected = grad_parts.reshape(IMG_MB, local_patches, 3 * model_width)
        grad_normed_one = jnp.einsum(
            "pte,de->ptd", grad_projected, w_qkv_full, preferred_element_type=jnp.float32
        )
        grad_from_one, grad_gain1, grad_bias1 = norm_one_back(grad_normed_one)
        grad_inputs.append((grad_residual + grad_from_one).astype(jnp.bfloat16))
        norm_grads = (grad_gain1, grad_bias1, grad_gain2, grad_bias2)
        norm_total = norm_grads if micro_idx == 0 else add_pairs(norm_total, norm_grads)
        kept.append(
            (
                normed_one_low,
                grad_projected,
                mixed_tokens,
                grad_attn_low,
                normed_two_low,
                grad_upward_low,
                activated_low,
                grad_branch,
            )
        )
    joined = [jnp.concatenate([item[index] for item in kept], axis=0) for index in range(8)]
    big = weight_grads(
        joined[0],
        joined[1],
        joined[2],
        joined[3],
        joined[4],
        joined[5],
        joined[6],
        joined[7],
        model_width,
    )
    owned = (
        lax.psum_scatter(big[0].astype(jnp.bfloat16), "dp", scatter_dimension=0, tiled=True).astype(
            jnp.float32
        ),
        lax.psum_scatter(big[1].astype(jnp.bfloat16), "dp", scatter_dimension=0, tiled=True).astype(
            jnp.float32
        ),
        lax.psum_scatter(big[2].astype(jnp.bfloat16), "dp", scatter_dimension=0, tiled=True).astype(
            jnp.float32
        ),
        lax.psum_scatter(big[3].astype(jnp.bfloat16), "dp", scatter_dimension=1, tiled=True).astype(
            jnp.float32
        ),
        lax.psum_scatter(big[4].astype(jnp.bfloat16), "dp", scatter_dimension=0, tiled=True).astype(
            jnp.float32
        ),
        lax.psum_scatter(big[5].astype(jnp.bfloat16), "dp", scatter_dimension=0, tiled=True).astype(
            jnp.float32
        ),
        lax.psum_scatter(big[6].astype(jnp.bfloat16), "dp", scatter_dimension=0, tiled=True).astype(
            jnp.float32
        ),
        lax.psum_scatter(big[7].astype(jnp.bfloat16), "dp", scatter_dimension=0, tiled=True).astype(
            jnp.float32
        ),
        lax.psum_scatter(big[8].astype(jnp.bfloat16), "dp", scatter_dimension=0, tiled=True).astype(
            jnp.float32
        ),
        lax.psum_scatter(
            norm_total[0].astype(jnp.bfloat16), "dp", scatter_dimension=0, tiled=True
        ).astype(jnp.float32),
        lax.psum_scatter(
            norm_total[1].astype(jnp.bfloat16), "dp", scatter_dimension=0, tiled=True
        ).astype(jnp.float32),
        lax.psum_scatter(
            norm_total[2].astype(jnp.bfloat16), "dp", scatter_dimension=0, tiled=True
        ).astype(jnp.float32),
        lax.psum_scatter(
            norm_total[3].astype(jnp.bfloat16), "dp", scatter_dimension=0, tiled=True
        ).astype(jnp.float32),
    )
    owned = (
        lax.psum(owned[0].astype(jnp.bfloat16), "seq").astype(jnp.float32),
        lax.psum(owned[1].astype(jnp.bfloat16), "seq").astype(jnp.float32),
        lax.psum(owned[2].astype(jnp.bfloat16), "seq").astype(jnp.float32),
        lax.psum(owned[3].astype(jnp.bfloat16), "seq").astype(jnp.float32),
        lax.psum(owned[4].astype(jnp.bfloat16), "seq").astype(jnp.float32),
        lax.psum(owned[5].astype(jnp.bfloat16), "seq").astype(jnp.float32),
        lax.psum(owned[6].astype(jnp.bfloat16), "seq").astype(jnp.float32),
        lax.psum(owned[7].astype(jnp.bfloat16), "seq").astype(jnp.float32),
        lax.psum(owned[8].astype(jnp.bfloat16), "seq").astype(jnp.float32),
        lax.psum(owned[9].astype(jnp.bfloat16), "seq").astype(jnp.float32),
        lax.psum(owned[10].astype(jnp.bfloat16), "seq").astype(jnp.float32),
        lax.psum(owned[11].astype(jnp.bfloat16), "seq").astype(jnp.float32),
        lax.psum(owned[12].astype(jnp.bfloat16), "seq").astype(jnp.float32),
    )
    return (
        jnp.concatenate(outputs, axis=0),
        jnp.concatenate(grad_inputs, axis=0),
        owned[0],
        owned[1],
        owned[2],
        owned[3],
        owned[4],
        owned[5],
        owned[6],
        owned[7],
        owned[8],
        owned[9],
        owned[10],
        owned[11],
        owned[12],
    )


F32=jnp.float32; BF16=jnp.bfloat16
NT=(((1,),(1,)),((),())); TN=(((0,),(0,)),((),())); NN=(((1,),(0,)),((),()))
def dg(a,b,dims): return lax.dot_general(a,b,dims,preferred_element_type=F32)

def attn_fwd_kernel(q_ref, ka_ref, kb_ref, va_ref, vb_ref, o_ref, l_ref):
    rows=q_ref.shape[0]
    lane=lax.broadcasted_iota(jnp.int32,(rows,128),1)
    q=q_ref[...]*jnp.asarray(0.125,BF16)
    outs=[]; ls=[]
    for h in range(2):
        qh=jnp.where((lane<64) if h==0 else (lane>=64), q, jnp.zeros_like(q))
        sa=dg(ka_ref[...],qh,NT); sb=dg(kb_ref[...],qh,NT)
        m=jnp.maximum(jnp.max(sa,axis=0,keepdims=True),jnp.max(sb,axis=0,keepdims=True))
        pa=jnp.exp(sa-m); pb=jnp.exp(sb-m)
        tot=jnp.sum(pa,axis=0,keepdims=True)+jnp.sum(pb,axis=0,keepdims=True)
        oT=dg(va_ref[...],pa.astype(BF16),TN)+dg(vb_ref[...],pb.astype(BF16),TN)
        outs.append(oT[64*h:64*h+64]*(1.0/tot))
        ls.append(m+jnp.log(tot))
    oT=jnp.concatenate(outs,axis=0)
    o_ref[...]=oT.T.astype(BF16)
    l_ref[0]=jnp.concatenate(ls+[jnp.zeros((6,rows),F32)],axis=0)

def attn_fwd(q,ka,kb,va,vb):
    rows,width=q.shape
    spec=pl.BlockSpec((rows,128),lambda i:(0,i))
    keys=ka.shape[0]
    ks=pl.BlockSpec((keys,128),lambda i:(0,i))
    return pl.pallas_call(attn_fwd_kernel,grid=(width//128,),
        in_specs=[spec,ks,ks,ks,ks],
        out_specs=[spec,pl.BlockSpec((1,8,rows),lambda i:(i,0,0))],
        out_shape=[jax.ShapeDtypeStruct((rows,width),BF16),jax.ShapeDtypeStruct((width//128,8,rows),F32)],
        compiler_params=pltpu.CompilerParams(vmem_limit_bytes=48<<20),name="attn_fwd",
        cost_estimate=pl.CostEstimate(flops=4*rows*2*keys*width,bytes_accessed=12*rows*width,transcendentals=rows*2*keys*width//64))(q,ka,kb,va,vb)

def attn_bwd_kernel(q_ref, ka_ref, kb_ref, va_ref, vb_ref, o_ref, do_ref, l_ref, dq_ref, dka_ref, dkb_ref, dva_ref, dvb_ref):
    rows=q_ref.shape[0]
    lane=lax.broadcasted_iota(jnp.int32,(rows,128),1)
    q=q_ref[...]*jnp.asarray(0.125,BF16)
    do=do_ref[...]
    t=(do.astype(F32)*o_ref[...].astype(F32)).T
    klane=lax.broadcasted_iota(jnp.int32,(ka_ref.shape[0],128),1)
    dq=None; dk=[None,None]; dv=[None,None]
    add=lambda a,b: b if a is None else a+b
    for h in range(2):
        sel=(lane<64) if h==0 else (lane>=64)
        ksel=(klane<64) if h==0 else (klane>=64)
        qh=jnp.where(sel,q,jnp.zeros_like(q)); doh=jnp.where(sel,do,jnp.zeros_like(do))
        delta=jnp.sum(t[64*h:64*h+64],axis=0,keepdims=True)
        lse=l_ref[0,h:h+1,:]
        for n,(k_ref,v_ref) in enumerate(((ka_ref,va_ref),(kb_ref,vb_ref))):
            s=dg(k_ref[...],qh,NT)
            p=jnp.exp(s-lse)
            dp=dg(v_ref[...],doh,NT)
            ds=(p*(dp-delta)).astype(BF16)
            dv[n]=add(dv[n],dg(p.astype(BF16),doh,NN))
            dk[n]=add(dk[n],dg(ds,qh,NN))
            kh=jnp.where(ksel,k_ref[...],jnp.zeros_like(k_ref[...]))
            dq=add(dq,dg(kh,ds,TN))
    dq_ref[...]=(dq*0.125).T.astype(BF16)
    dka_ref[...]=dk[0].astype(BF16); dkb_ref[...]=dk[1].astype(BF16)
    dva_ref[...]=dv[0].astype(BF16); dvb_ref[...]=dv[1].astype(BF16)

def attn_bwd(q,ka,kb,va,vb,o,do,l):
    rows,width=q.shape; keys=ka.shape[0]
    spec=pl.BlockSpec((rows,128),lambda i:(0,i))
    ks=pl.BlockSpec((keys,128),lambda i:(0,i))
    sh=jax.ShapeDtypeStruct((rows,width),BF16); kh=jax.ShapeDtypeStruct((keys,width),BF16)
    return pl.pallas_call(attn_bwd_kernel,grid=(width//128,),
        in_specs=[spec,ks,ks,ks,ks,spec,spec,pl.BlockSpec((1,8,rows),lambda i:(i,0,0))],
        out_specs=[spec,ks,ks,ks,ks],
        out_shape=[sh,kh,kh,kh,kh],
        compiler_params=pltpu.CompilerParams(vmem_limit_bytes=48<<20),name="attn_bwd",
        cost_estimate=pl.CostEstimate(flops=10*rows*2*keys*width,bytes_accessed=26*rows*width,transcendentals=rows*2*keys*width//64))(q,ka,kb,va,vb,o,do,l)


def image_moves(shift):
    pairs = []
    for p in range(4):
        for c in range(2):
            for z in range(4):
                to_core, to_z = z // 2, 2 * c + (shift ^ (z & 1))
                pairs.append(((2 * p + c) * 4 + z, (2 * p + to_core) * 4 + to_z))
    return pairs


def gather_image(blocks):
    odd = lax.axis_index("seq") % 2
    parts = []
    for shift in range(2):
        mine = lax.dynamic_index_in_dim(blocks, odd ^ shift, 0, keepdims=False)
        parts.append(lax.ppermute(mine, ("dp", "seq"), image_moves(shift)))
    rows = parts[0].shape[0]
    swapped = jnp.where(odd == 0, jnp.stack(parts), jnp.stack(parts[::-1]))
    return swapped.reshape(2 * rows, parts[0].shape[1])


def return_image(rows_all):
    odd = lax.axis_index("seq") % 2
    halves = rows_all.reshape(2, rows_all.shape[0] // 2, rows_all.shape[1])
    parts = []
    for shift in range(2):
        mine = lax.dynamic_index_in_dim(halves, odd ^ shift, 0, keepdims=False)
        back = [(to, start) for start, to in image_moves(shift)]
        parts.append(lax.ppermute(mine, ("dp", "seq"), back))
    return jnp.where(odd == 0, jnp.stack(parts), jnp.stack(parts[::-1]))


def other_core(value):
    return lax.ppermute(value, "dp", [(i, i ^ 1) for i in range(lax.axis_size("dp"))])


def dot_nn(left, right):
    return dg(left, right, NN)


def norm_parts(value):
    centre = jnp.mean(value, axis=-1, keepdims=True)
    spread = jnp.mean(jnp.square(value - centre), axis=-1, keepdims=True)
    rstd = lax.rsqrt(spread + norm_eps)
    return ((value - centre) * rstd, rstd)


def norm_back(xhat, rstd, grad, gain):
    e = grad * gain
    return rstd * (
        e - jnp.mean(e, axis=-1, keepdims=True) - xhat * jnp.mean(e * xhat, axis=-1, keepdims=True)
    )


MESH = pl.DeviceIdType.MESH
HBM = pltpu.MemorySpace.HBM


def flip(value, bits):
    return lax.ppermute(value, "dp", [(i, i ^ bits) for i in range(8)])


def flip_z(value, bits):
    return lax.ppermute(value, "seq", [(i, i ^ bits) for i in range(4)])


def after(value, *earlier):
    return lax.optimization_barrier((value,) + earlier)[0]


def finish_kernel(a01, a2, b01, b2, out, kept, in_sem, out_sem, send_sem, recv_sem):
    d, z = lax.axis_index("dp"), lax.axis_index("seq")
    core, x, y = lax.rem(d, 2), lax.rem(d // 2, 2), d // 4
    sibling = (d + 1 - 2 * core, z)
    half = a01.shape[2]
    barrier = pltpu.get_barrier_semaphore()
    pl.semaphore_signal(barrier, inc=1, device_id=sibling, device_id_type=MESH)
    pl.semaphore_wait(barrier, 1)
    pieces = (
        (a01.at[0], y, x, 0), (b01.at[0], y, x, 1),
        (a01.at[1], y, 1 - x, 0), (b01.at[1], 1 - y, x, 1),
        (a2.at[0], 1 - y, x, 0), (b2.at[0], y, 1 - x, 1),
        (a2.at[1], 1 - y, 1 - x, 0), (b2.at[1], 1 - y, 1 - x, 1),
    )
    sends, loads, stores = [], [], []
    for k, (piece, py, px, side) in enumerate(pieces):
        row = pl.multiple_of(((py * 2 + px) * 2 + core) * 128, 128)
        target = out.at[pl.ds(row, 128), pl.ds(side * half, half)]
        sends.append(
            pltpu.make_async_remote_copy(
                src_ref=piece, dst_ref=target, send_sem=send_sem.at[k], recv_sem=recv_sem.at[k],
                device_id=sibling, device_id_type=MESH,
            )
        )
        loads.append(pltpu.make_async_copy(piece, kept.at[k], in_sem.at[k]))
        stores.append(pltpu.make_async_copy(kept.at[k], target, out_sem.at[k]))
    for k in range(8):
        sends[k].start()
        loads[k].start()
    for k in range(8):
        loads[k].wait()
        stores[k].start()
    for k in range(8):
        stores[k].wait()
        sends[k].wait()


def finish(parts, ident):
    half = parts[0].shape[2]
    return pl.pallas_call(
        finish_kernel,
        in_specs=[pl.BlockSpec(memory_space=pl.ANY)] * 4,
        out_specs=pl.BlockSpec(memory_space=HBM),
        out_shape=jax.ShapeDtypeStruct((1024, 2 * half), BF16),
        scratch_shapes=[pltpu.VMEM((8, 128, half), BF16)] + [pltpu.SemaphoreType.DMA((8,))] * 4,
        compiler_params=pltpu.CompilerParams(collective_id=ident, has_side_effects=True),
        cost_estimate=pl.CostEstimate(flops=0, bytes_accessed=8192 * half, transcendentals=0),
        name="finish%d" % ident,
    )(*parts)


def first_hop(shard):
    half = shard.shape[1] // 2
    a, b = shard[:, :half], shard[:, half:]
    return jnp.stack([a, flip(a, 2)]), jnp.stack([b, flip(b, 4)])


def second_hop(first):
    return first[0], flip(first[0], 4), first[1], flip(first[1], 2)


def relative(value, order, me):
    return jnp.concatenate(
        [lax.dynamic_slice_in_dim(value, 128 * (me ^ r), 128, axis=1) for r in order], axis=1
    )


CHUNKS = 12


def gelu_slope(u):
    inner = 0.7978845608028654 * (u + 0.044715 * u * u * u)
    t = jnp.tanh(inner)
    return 0.5 * (1.0 + t) + 0.5 * u * (1.0 - t * t) * (0.7978845608028654 * (1.0 + 3 * 0.044715 * u * u))


def bwd_kernel(
    cot_hbm, cot_t_hbm, n2_t_hbm, act_hbm, up_hbm, wd_hbm, wu_hbm, wo_hbm, wq_hbm, att_t_hbm, n1_t_hbm,
    q_hbm, ka_hbm, kb_hbm, va_hbm, vb_hbm, att_hbm, lse_ref, res_hbm, x_hbm, gain1_ref, gain2_ref,
    gd_out, gu_out, go_out, gq_out, gin_out, sums_ref,
    so, sr, g, h1a, h1b, h2a, h2b, z1, z2, z3, fin, dkv_in, cot, gres,
    sib_s, sib_r, hop_s, hop_r, zs, zr, fin_sem, dkv_s, dkv_r, load,
):
    d, z = lax.axis_index("dp"), lax.axis_index("seq")
    core, x, y = lax.rem(d, 2), lax.rem(d // 2, 2), d // 4
    par = lax.rem(z, 2)
    sibling = (d + 1 - 2 * core, z)
    over_x = (d + 2 - 4 * x, z)
    over_y = (d + 4 - 8 * y, z)
    near_z = (d, z + 1 - 2 * par)
    far_z = (d, z + 2 - 4 * (z // 2))
    barrier = pltpu.get_barrier_semaphore()
    for to in (sibling, over_x, over_y, near_z, far_z):
        pl.semaphore_signal(barrier, inc=1, device_id=to, device_id_type=MESH)
    pl.semaphore_wait(barrier, 5)

    def remote(src, dst, send, recv, to):
        return pltpu.make_async_remote_copy(
            src_ref=src, dst_ref=dst, send_sem=send, recv_sem=recv, device_id=to, device_id_type=MESH
        )

    lo, hi = pl.ds(0, 512), pl.ds(512, 512)
    keep = pl.ds(pl.multiple_of(par * 512, 512), 512)
    give = pl.ds(pl.multiple_of((1 - par) * 512, 512), 512)

    def to_sib(k):
        return remote(so.at[lax.rem(k, 2)], sr.at[lax.rem(k, 2)], sib_s.at[k], sib_r.at[k], sibling)

    def hop(k, j):
        src, dst, to = (
            (g.at[k, 1, :, :, lo], h1a.at[k], over_y),
            (g.at[k, :, 1, :, hi], h1b.at[k], over_x),
            (g.at[k, 0, 1, :, lo], h2a.at[k], over_x),
            (g.at[k, 1, 0, :, hi], h2b.at[k], over_y),
        )[j]
        return remote(src, dst, hop_s.at[k, j], hop_r.at[k, j], to)

    def zhop(k, j):
        src, dst, to = (
            (g.at[k, 0, 0, :, give], z1.at[k], near_z),
            (g.at[k, 0, 0, :, keep], z2.at[k], far_z),
            (g.at[k, 0, 0, :, keep], z3.at[k], near_z),
        )[j]
        return remote(src, dst, zs.at[k, j], zr.at[k, j], to)

    def plus(a, b):
        return (a.astype(F32) + b.astype(F32)).astype(BF16)

    def out_copy(k):
        slot = lax.rem(k, 2)
        def with_target(run):
            col = lambda j: pl.ds(pl.multiple_of(j * 1024, 1024), 1024)
            sem = fin_sem.at[slot]
            @pl.when(jnp.logical_and(k < 8, lax.rem(k, 2) == 0))
            def _(): run(pltpu.make_async_copy(fin.at[slot], gd_out.at[:, col(k // 2)], sem))
            @pl.when(jnp.logical_and(k < 8, lax.rem(k, 2) == 1))
            def _(): run(pltpu.make_async_copy(fin.at[slot], gu_out.at[:, col(k // 2)], sem))
            @pl.when(k == 8)
            def _(): run(pltpu.make_async_copy(fin.at[slot], go_out, sem))
            @pl.when(k > 8)
            def _(): run(pltpu.make_async_copy(fin.at[slot], gq_out.at[:, col(k - 9)], sem))
        return with_target

    def tick(n):
        def stage(k, body):
            @pl.when(jnp.logical_and(k >= 0, k < CHUNKS))
            def _(): body(k)

        def c2(k):
            hop(k, 0).wait(); hop(k, 1).wait()
            g[k, 0, :, :, lo] = plus(g[k, 0, :, :, lo], h1a[k])
            g[k, :, 0, :, hi] = plus(g[k, :, 0, :, hi], h1b[k])
            hop(k, 2).start(); hop(k, 3).start()

        def c3(k):
            hop(k, 2).wait(); hop(k, 3).wait()
            g[k, 0, 0, :, lo] = plus(g[k, 0, 0, :, lo], h2a[k])
            g[k, 0, 0, :, hi] = plus(g[k, 0, 0, :, hi], h2b[k])
            zhop(k, 0).start()

        def c4(k):
            zhop(k, 0).wait()
            g[k, 0, 0, :, keep] = plus(g[k, 0, 0, :, keep], z1[k])
            zhop(k, 1).start()

        def c5(k):
            zhop(k, 1).wait()
            g[k, 0, 0, :, keep] = plus(g[k, 0, 0, :, keep], z2[k])
            zhop(k, 2).start()

        def c6(k):
            zhop(k, 2).wait()
            slot = lax.rem(k, 2)
            @pl.when(k >= 2)
            def _(): out_copy(k - 2)(lambda c: c.wait())
            fin[slot, :, keep] = g[k, 0, 0, :, keep].astype(F32)
            fin[slot, :, give] = z3[k].astype(F32)
            out_copy(k)(lambda c: c.start())

        stage(n, c2); stage(n - 1, c3); stage(n - 2, c4); stage(n - 3, c5); stage(n - 4, c6)

    def tiles(count, body, size=256):
        def step(i, carry):
            body(pl.ds(pl.multiple_of(i * size, size), size))
            return carry
        lax.fori_loop(0, count, step, 0)

    def send_odd(k, left, right):
        def one(cols):
            so[lax.rem(k, 2), :, cols] = dg(left[512:1024, :], right[:, cols], NN).astype(BF16)
        tiles(4, one)
        to_sib(k).start()

    def add_even(k, left, right):
        to_sib(k).wait()
        def one(cols):
            part = dg(left[0:512, :], right[:, cols], NN) + sr[lax.rem(k, 2), :, cols].astype(F32)
            g[k, :, :, :, cols] = part.astype(BF16).reshape(2, 2, 128, 256)
        tiles(4, one)
        hop(k, 0).start(); hop(k, 1).start()

    def fetch(src, dst, i):
        return pltpu.make_async_copy(src, dst, load.at[i])

    first = fetch(cot_hbm, cot, 0)
    first.start()
    sums_ref[...] = jnp.zeros_like(sums_ref)

    def mlp(cot_t, n2_t, actb, upb, wdb, wub, gub, gn2, resb):
        pieces = [fetch(cot_t_hbm, cot_t, 1), fetch(n2_t_hbm, n2_t, 2), fetch(res_hbm, resb, 3)]
        for c in pieces: c.start()
        def parts(j):
            cols = pl.ds(pl.multiple_of(j * 1024, 1024), 1024)
            s = lax.rem(j, 2)
            return [
                pltpu.make_async_copy(src.at[:, cols], dst.at[s], load.at[4 + 4 * s + i])
                for i, (src, dst) in enumerate(((act_hbm, actb), (up_hbm, upb), (wd_hbm, wdb), (wu_hbm, wub)))
            ]
        for c in parts(jnp.int32(0)): c.start()
        gn2[...] = jnp.zeros_like(gn2)
        first.wait()
        pieces[0].wait()
        pieces[1].wait()
        def block(j, carry):
            s = lax.rem(j, 2)
            for c in parts(j): c.wait()
            @pl.when(j < 3)
            def _():
                for c in parts(j + 1): c.start()
            kd, ku = 2 * j, 2 * j + 1
            send_odd(kd, cot_t, actb.at[s])
            def slope(cols):
                back = dg(cot[...], wdb[s, :, cols], NN)
                low = (back * gelu_slope(upb[s, :, cols])).astype(BF16)
                gub[:, cols] = low
                sums_ref[pl.ds(j, 1), cols] = jnp.sum(low.astype(F32), axis=0, keepdims=True)
            tiles(4, slope)
            add_even(kd, cot_t, actb.at[s])
            send_odd(ku, n2_t, gub)
            def down(cols):
                gn2[:, cols] += dg(gub[...], wub[s, cols, :], NT)
            tiles(4, down)
            add_even(ku, n2_t, gub)
            @pl.when(j > 0)
            def _(): tick(j - 1)
            return carry
        lax.fori_loop(0, 4, block, 0)
        pieces[2].wait()
        def rows(r):
            res = resb[r, :]
            centre = jnp.mean(res, axis=-1, keepdims=True)
            off = res - centre
            rstd = lax.rsqrt(jnp.mean(off * off, axis=-1, keepdims=True) + norm_eps)
            xhat = off * rstd
            grad = gn2[r, :]
            e = grad * gain2_ref[...]
            back = rstd * (e - jnp.mean(e, axis=-1, keepdims=True) - xhat * jnp.mean(e * xhat, axis=-1, keepdims=True))
            total = cot[r, :].astype(F32) + back
            gres[r, :] = total
            low = total.astype(BF16).astype(F32)
            add = lambda i, v: sums_ref.__setitem__((slice(i, i + 1), slice(None)), sums_ref[i : i + 1, :] + jnp.sum(v, axis=0, keepdims=True))
            add(4, low); add(5, grad * xhat); add(6, grad); add(7, cot[r, :].astype(F32))
        tiles(8, rows, 64)

    pl.run_scoped(
        mlp, pltpu.VMEM((1024, 512), BF16), pltpu.VMEM((1024, 512), BF16), pltpu.VMEM((2, 512, 1024), BF16),
        pltpu.VMEM((2, 512, 1024), F32), pltpu.VMEM((2, 1024, 1024), BF16), pltpu.VMEM((2, 1024, 1024), BF16),
        pltpu.VMEM((512, 1024), BF16), pltpu.VMEM((512, 1024), F32), pltpu.VMEM((512, 1024), F32),
    )

    def rest(dqkv, n1_t, xb):
        late = [fetch(n1_t_hbm, n1_t, 0), fetch(x_hbm, xb, 1)]
        for c in late: c.start()

        def attention(wo, att_t, ga, q, ka, kb, va, vb, att, do, dob):
            loads = [
                fetch(src, dst, 2 + i) for i, (src, dst) in enumerate((
                    (wo_hbm, wo), (att_t_hbm, att_t), (q_hbm, q), (ka_hbm, ka), (kb_hbm, kb), (va_hbm, va),
                    (vb_hbm, vb), (att_hbm, att),
                ))
            ]
            for c in loads: c.start()
            tick(jnp.int32(3))
            ga[...] = gres[...].astype(BF16)
            for c in loads: c.wait()
            send_odd(jnp.int32(8), att_t, ga)
            def mixed(cols):
                do[:, cols] = dg(ga[...], wo[cols, :], NT).astype(BF16)
            tiles(4, mixed)
            add_even(jnp.int32(8), att_t, ga)
            lane = lax.broadcasted_iota(jnp.int32, (512, 128), 1)
            def pair(i, carry):
                cols = pl.ds(pl.multiple_of(i * 128, 128), 128)
                qs = q[:, cols] * jnp.asarray(0.125, BF16)
                dos = do[:, cols]
                t = (dos.astype(F32) * att[:, cols].astype(F32)).T
                dq, dk, dv = None, [None, None], [None, None]
                plus_ = lambda a, b: b if a is None else a + b
                for h in range(2):
                    sel = (lane < 64) if h == 0 else (lane >= 64)
                    qh = jnp.where(sel, qs, jnp.zeros_like(qs))
                    doh = jnp.where(sel, dos, jnp.zeros_like(dos))
                    delta = jnp.sum(t[64 * h : 64 * h + 64], axis=0, keepdims=True)
                    lse = lse_ref[i, h : h + 1, :]
                    for n, (k_ref, v_ref) in enumerate(((ka, va), (kb, vb))):
                        kk = k_ref[:, cols]
                        s = dg(kk, qh, NT)
                        p = jnp.exp(s - lse)
                        dp = dg(v_ref[:, cols], doh, NT)
                        ds = (p * (dp - delta)).astype(BF16)
                        dv[n] = plus_(dv[n], dg(p.astype(BF16), doh, NN))
                        dk[n] = plus_(dk[n], dg(ds, qh, NN))
                        dq = plus_(dq, dg(jnp.where(sel, kk, jnp.zeros_like(kk)), ds, TN))
                at = lambda base: pl.ds(pl.multiple_of(base + i * 128, 128), 128)
                dqkv[:, at(0)] = (dq * 0.125).T.astype(BF16)
                dqkv[:, at(1024)] = dk[0].astype(BF16)
                dqkv[:, at(2048)] = dv[0].astype(BF16)
                dob[:, at(0)] = dk[1].astype(BF16)
                dob[:, at(1024)] = dv[1].astype(BF16)
                @pl.when(lax.rem(i, 3) == 1)
                def _(): tick(4 + i // 3)
                return carry
            lax.fori_loop(0, 8, pair, 0)
            swap = remote(dob, dkv_in, dkv_s, dkv_r, sibling)
            swap.start()
            late[0].wait()
            send_odd(jnp.int32(9), n1_t, dqkv.at[:, pl.ds(0, 1024)])
            swap.wait()

        pl.run_scoped(
            attention, pltpu.VMEM((1024, 1024), BF16), pltpu.VMEM((1024, 512), BF16),
            *[pltpu.VMEM((512, 1024), BF16)] * 8, pltpu.VMEM((512, 2048), BF16),
        )

        def last(wq, gn1):
            def wq_part(i):
                s = lax.rem(i, 2)
                return pltpu.make_async_copy(wq_hbm.at[pl.ds(pl.multiple_of(i * 256, 256), 256), :], wq.at[s], load.at[2 + s])
            wq_part(jnp.int32(0)).start()
            def join(cols):
                there = pl.ds(pl.multiple_of(1024 + cols.start, 256), 256)
                dqkv[:, there] = plus(dqkv[:, there], dkv_in[:, cols])
            tiles(8, join)
            add_even(jnp.int32(9), n1_t, dqkv.at[:, pl.ds(0, 1024)])
            for k in (10, 11):
                right = dqkv.at[:, pl.ds(1024 * (k - 9), 1024)]
                send_odd(jnp.int32(k), n1_t, right)
                if k == 10:
                    tick(jnp.int32(7))
                add_even(jnp.int32(k), n1_t, right)
            def back(i, carry):
                wq_part(i).wait()
                @pl.when(i < 3)
                def _(): wq_part(i + 1).start()
                gn1[:, pl.ds(pl.multiple_of(i * 256, 256), 256)] = dg(dqkv[...], wq[lax.rem(i, 2)], NT)
                return carry
            lax.fori_loop(0, 4, back, 0)
            tick(jnp.int32(8))
            late[1].wait()
            def rows(r):
                xx = xb[r, :].astype(F32)
                centre = jnp.mean(xx, axis=-1, keepdims=True)
                off = xx - centre
                rstd = lax.rsqrt(jnp.mean(off * off, axis=-1, keepdims=True) + norm_eps)
                xhat = off * rstd
                grad = gn1[r, :]
                e = grad * gain1_ref[...]
                back = rstd * (e - jnp.mean(e, axis=-1, keepdims=True) - xhat * jnp.mean(e * xhat, axis=-1, keepdims=True))
                xb[r, :] = (gres[r, :] + back).astype(BF16)
                add = lambda i, v: sums_ref.__setitem__((slice(i, i + 1), slice(None)), sums_ref[i : i + 1, :] + jnp.sum(v, axis=0, keepdims=True))
                add(8, grad * xhat); add(9, grad)
                add(10, dqkv[r, 0:1024].astype(F32)); add(11, dqkv[r, 2048:3072].astype(F32))
            tiles(8, rows, 64)
            given = fetch(xb, gin_out, 4)
            given.start()
            def drain(n, carry):
                tick(n)
                return carry
            lax.fori_loop(9, CHUNKS + 4, drain, 0)
            for k in (CHUNKS - 2, CHUNKS - 1):
                out_copy(jnp.int32(k))(lambda c: c.wait())
            given.wait()

        pl.run_scoped(last, pltpu.VMEM((2, 256, 3072), BF16), pltpu.VMEM((512, 1024), F32))

    pl.run_scoped(rest, pltpu.VMEM((512, 3072), BF16), pltpu.VMEM((1024, 512), BF16), pltpu.VMEM((512, 1024), BF16))


def backward(arrays, lse, residual, x, gain1, gain2):
    any_ = pl.BlockSpec(memory_space=pl.ANY)
    vmem = pl.BlockSpec(memory_space=pltpu.VMEM)
    hbm = pl.BlockSpec(memory_space=HBM)
    n = CHUNKS
    dma = pltpu.SemaphoreType.DMA
    return pl.pallas_call(
        bwd_kernel,
        in_specs=[any_] * len(arrays) + [vmem, any_, any_, vmem, vmem],
        out_specs=[hbm] * 5 + [vmem],
        out_shape=[jax.ShapeDtypeStruct((128, w), F32) for w in (4096, 4096, 1024, 3072)]
        + [jax.ShapeDtypeStruct((512, 1024), BF16), jax.ShapeDtypeStruct((16, 1024), F32)],
        scratch_shapes=[
            pltpu.VMEM((2, 512, 1024), BF16), pltpu.VMEM((2, 512, 1024), BF16), pltpu.VMEM((n, 2, 2, 128, 1024), BF16),
            pltpu.VMEM((n, 2, 128, 512), BF16), pltpu.VMEM((n, 2, 128, 512), BF16),
            pltpu.VMEM((n, 128, 512), BF16), pltpu.VMEM((n, 128, 512), BF16),
            pltpu.VMEM((n, 128, 512), BF16), pltpu.VMEM((n, 128, 512), BF16), pltpu.VMEM((n, 128, 512), BF16),
            pltpu.VMEM((2, 128, 1024), F32), pltpu.VMEM((512, 2048), BF16), pltpu.VMEM((512, 1024), BF16),
            pltpu.VMEM((512, 1024), F32),
            dma((n,)), dma((n,)), dma((n, 4)), dma((n, 4)), dma((n, 3)), dma((n, 3)), dma((2,)), dma, dma, dma((12,)),
        ],
        compiler_params=pltpu.CompilerParams(collective_id=8, has_side_effects=True, vmem_limit_bytes=67043328),
        cost_estimate=pl.CostEstimate(flops=40 * 10**9, bytes_accessed=60 << 20, transcendentals=10**7),
        name="backward",
    )(*arrays, lse, residual, x, gain1, gain2)


def local_fast(
    tokens, w_qkv, w_out, w_up, w_down, b_query, b_value, b_out, b_up, b_down,
    ln1_gain, ln1_bias, ln2_gain, ln2_bias, cotangent,
):
    d = tokens.shape[2]
    me = lax.axis_index("dp")
    small = (b_query, b_value, b_out, b_up, b_down, ln1_gain, ln1_bias, ln2_gain, ln2_bias)
    sizes = [item.shape[0] for item in small]

    x_low = gather_image(tokens)
    pack = jnp.concatenate(small).reshape(1, -1)
    for bits in (1, 2, 4):
        pack = jnp.concatenate([pack, flip(pack, bits)])
    packed = jnp.concatenate([lax.dynamic_slice_in_dim(pack, me ^ r, 1, axis=0) for r in range(8)])
    vectors, at = [], 0
    for size in sizes:
        vectors.append(packed[:, at : at + size].reshape(1, -1).astype(F32))
        at += size
    bias_query, bias_value, bias_out, bias_up, bias_down, gain1, shift1, gain2, shift2 = vectors

    qkv1 = first_hop(w_qkv)
    qkv2 = second_hop(qkv1)
    out1 = first_hop(after(w_out, *qkv1))
    out2 = second_hop(out1)
    up1 = first_hop(after(w_up, *qkv2))
    up2 = second_hop(up1)
    down1 = first_hop(after(w_down.T, *out2))
    down2 = second_hop(down1)
    wq = finish(qkv2, 0)
    cot_low = gather_image(after(cotangent, x_low))

    x = x_low.astype(F32)
    xhat1, rstd1 = norm_parts(x)
    n1 = (xhat1 * gain1 + shift1).astype(BF16)
    bias = jnp.concatenate([bias_query, jnp.zeros_like(bias_query), bias_value], axis=1)
    projected = (dot_nn(n1, wq) + bias).astype(BF16)
    q, k, v = (projected[:, i * d : (i + 1) * d] for i in range(3))
    kv_other = other_core(projected[:, d:])
    kb, vb = kv_other[:, :d], kv_other[:, d:]
    attended, lse = attn_fwd(q, k, kb, v, vb)
    wo = finish(out2, 1)
    residual = x + dot_nn(attended, wo) + bias_out
    xhat2, rstd2 = norm_parts(residual)
    n2 = (xhat2 * gain2 + shift2).astype(BF16)
    wu = finish(up2, 2)
    upward = dot_nn(n2, wu) + bias_up
    act = activate(upward).astype(BF16)
    wdt = finish(down2, 3)
    result = return_image((residual + dg(act, wdt, NT) + bias_down).astype(BF16))

    order = (0, 2, 4, 6, 1, 3, 5, 7)
    turned = lambda value: relative(value, order, me).T
    g_down, g_up, g_out, g_qkv, gin, rows = backward(
        (cot_low, turned(cot_low), turned(n2), act, upward, wdt, wu, wo, wq, turned(attended), turned(n1),
         q, k, kb, v, vb, attended), lse, residual, x_low, gain1, gain2)
    grad_input = return_image(gin)
    small_grads = (rows[10], rows[11], rows[4], rows[:4], rows[7], rows[8], rows[9], rows[5], rows[6])
    sums = jnp.concatenate([g.reshape(8, -1) for g in small_grads], axis=1)
    for bits in (1, 2, 4):
        sums = lax.optimization_barrier(sums + flip(sums, bits))
    for bits in (1, 2):
        sums = lax.optimization_barrier(sums + flip_z(sums, bits))
    mine = lax.dynamic_slice_in_dim(sums, me, 1, axis=0)[0]
    outs, at = [], 0
    for size in sizes:
        outs.append(mine[at : at + size])
        at += size
    return (result, grad_input, g_qkv, g_out, g_up, g_down.T, *outs)


def solution(mesh):
    in_specs = (
        P("dp", "seq", None),
        P("dp", None),
        P("dp", None),
        P("dp", None),
        P(None, "dp"),
        P("dp"),
        P("dp"),
        P("dp"),
        P("dp"),
        P("dp"),
        P("dp"),
        P("dp"),
        P("dp"),
        P("dp"),
        P("dp", "seq", None),
    )
    out_specs = (
        P("dp", "seq", None),
        P("dp", "seq", None),
        P("dp", None),
        P("dp", None),
        P("dp", None),
        P(None, "dp"),
        P("dp"),
        P("dp"),
        P("dp"),
        P("dp"),
        P("dp"),
        P("dp"),
        P("dp"),
        P("dp"),
        P("dp"),
    )
    fn = local_fast if dict(mesh.shape) == {"dp": 8, "seq": 4} else local
    return jax.shard_map(fn, mesh=mesh, in_specs=in_specs, out_specs=out_specs, check_vma=False)
```

```python
import functools

import jax
import jax.numpy as jnp
from jax import lax
from jax.experimental import pallas as pl
from jax.experimental.pallas import tpu as pltpu
from jax.sharding import PartitionSpec as P

H = 16
DH = 64
MICRO = 2
IMG_MB = 1


norm_eps = 1e-06


def normalize(inputs, ln_gain, ln_offset):
    centre = jnp.mean(inputs, axis=-1, keepdims=True)
    spread = jnp.mean(jnp.square(inputs - centre), axis=-1, keepdims=True)
    return (inputs - centre) * lax.rsqrt(spread + norm_eps) * ln_gain + ln_offset


def activate(upward):
    return jax.nn.gelu(upward, approximate=True)


def add_pairs(first_set, second_set):
    return tuple(
        (first_item + second_item for first_item, second_item in zip(first_set, second_set))
    )


def forward_heads(queries, keyed, valued, factor):
    images, length, head_count, head_size = queries.shape
    block_rows = min(512, length)
    blocks = length // block_rows
    query_blocks = queries.reshape(images, blocks, block_rows, head_count, head_size)

    def forward_per_image(element):
        q_image, k_image, v_image = element

        def forward_per_block(q_block):
            scores = (
                jnp.einsum("qhd,khd->hqk", q_block, k_image, preferred_element_type=jnp.float32)
                * factor
            )
            row_max = jnp.max(scores, axis=-1, keepdims=True)
            exponent = jnp.exp(scores - row_max)
            row_total = jnp.sum(exponent, axis=-1, keepdims=True)
            attn_probs = (exponent / row_total).astype(jnp.bfloat16)
            mixture = jnp.einsum(
                "hqk,khd->qhd", attn_probs, v_image, preferred_element_type=jnp.float32
            )
            return (mixture, row_max[..., 0] + jnp.log(row_total[..., 0]))

        return lax.map(forward_per_block, q_image)

    mixture, log_total = lax.map(forward_per_image, (query_blocks, keyed, valued))
    return (mixture.reshape(images, length, head_count * head_size), log_total)


def backward_heads(queries, keyed, valued, grad_mixed, log_total, factor):
    images, length, head_count, head_size = queries.shape
    block_rows = min(512, length)
    blocks = length // block_rows
    query_blocks = queries.reshape(images, blocks, block_rows, head_count, head_size)
    grad_blocks = grad_mixed.reshape(images, blocks, block_rows, head_count, head_size)

    def backward_per_image(element):
        q_image, k_image, v_image, g_image, l_image = element

        def backward_per_block(running, pieces):
            grad_key, grad_value = running
            q_block, g_block, l_block = pieces
            scores = (
                jnp.einsum("qhd,khd->hqk", q_block, k_image, preferred_element_type=jnp.float32)
                * factor
            )
            full_probs = jnp.exp(scores - l_block[..., None])
            grad_probs = jnp.einsum(
                "qhd,khd->hqk", g_block, v_image, preferred_element_type=jnp.float32
            )
            row_inner = jnp.sum(full_probs * grad_probs, axis=-1, keepdims=True)
            grad_scores = (full_probs * (grad_probs - row_inner)).astype(jnp.bfloat16)
            grad_query = (
                jnp.einsum("hqk,khd->qhd", grad_scores, k_image, preferred_element_type=jnp.float32)
                * factor
            )
            grad_key = (
                grad_key
                + jnp.einsum(
                    "hqk,qhd->khd", grad_scores, q_block, preferred_element_type=jnp.float32
                )
                * factor
            )
            grad_value = grad_value + jnp.einsum(
                "hqk,qhd->khd",
                full_probs.astype(jnp.bfloat16),
                g_block,
                preferred_element_type=jnp.float32,
            )
            return ((grad_key, grad_value), grad_query)

        empty_sum = jnp.zeros((length, head_count, head_size), jnp.float32)
        (grad_key, grad_value), grad_query = lax.scan(
            backward_per_block, (empty_sum, empty_sum), (q_image, g_image, l_image)
        )
        return (grad_query.reshape(length, head_count, head_size), grad_key, grad_value)

    return lax.map(backward_per_image, (query_blocks, keyed, valued, grad_blocks, log_total))


def weight_grads(
    normed_one_low,
    grad_projected,
    mixed_tokens,
    grad_attn_low,
    normed_two_low,
    grad_upward_low,
    activated_low,
    grad_branch,
    model_width,
):
    grad_qkv = jnp.einsum(
        "ptd,pte->de", normed_one_low, grad_projected, preferred_element_type=jnp.float32
    )
    grad_bquery = jnp.sum(grad_projected[:, :, :model_width], axis=(0, 1), dtype=jnp.float32)
    grad_bvalue = jnp.sum(grad_projected[:, :, 2 * model_width :], axis=(0, 1), dtype=jnp.float32)
    grad_wout = jnp.einsum(
        "pte,ptd->ed", mixed_tokens, grad_attn_low, preferred_element_type=jnp.float32
    )
    grad_bout = jnp.sum(grad_attn_low, axis=(0, 1), dtype=jnp.float32)
    grad_up = jnp.einsum(
        "ptd,ptf->df", normed_two_low, grad_upward_low, preferred_element_type=jnp.float32
    )
    grad_bup = jnp.sum(grad_upward_low, axis=(0, 1), dtype=jnp.float32)
    grad_down = jnp.einsum(
        "ptf,ptd->fd", activated_low, grad_branch, preferred_element_type=jnp.float32
    )
    grad_bdown = jnp.sum(grad_branch, axis=(0, 1), dtype=jnp.float32)
    return (
        grad_qkv,
        grad_wout,
        grad_up,
        grad_down,
        grad_bquery,
        grad_bvalue,
        grad_bout,
        grad_bup,
        grad_bdown,
    )


def local(
    tokens,
    w_qkv,
    w_out,
    w_up,
    w_down,
    b_query,
    b_value,
    b_out,
    b_up,
    b_down,
    ln1_gain,
    ln1_bias,
    ln2_gain,
    ln2_bias,
    cotangent,
):
    seq_count = lax.axis_size("seq")
    local_patches = tokens.shape[1]
    model_width = tokens.shape[2]
    patches = local_patches * seq_count
    head_local = H // seq_count
    factor = DH ** (-0.5)
    gathered = (
        lax.all_gather(w_qkv, "dp", axis=0, tiled=True),
        lax.all_gather(w_out, "dp", axis=0, tiled=True),
        lax.all_gather(w_up, "dp", axis=0, tiled=True),
        lax.all_gather(w_down, "dp", axis=1, tiled=True),
        lax.all_gather(b_query, "dp", axis=0, tiled=True),
        lax.all_gather(b_value, "dp", axis=0, tiled=True),
        lax.all_gather(b_out, "dp", axis=0, tiled=True),
        lax.all_gather(b_up, "dp", axis=0, tiled=True),
        lax.all_gather(b_down, "dp", axis=0, tiled=True),
        lax.all_gather(ln1_gain, "dp", axis=0, tiled=True),
        lax.all_gather(ln1_bias, "dp", axis=0, tiled=True),
        lax.all_gather(ln2_gain, "dp", axis=0, tiled=True),
        lax.all_gather(ln2_bias, "dp", axis=0, tiled=True),
    )
    outputs = []
    grad_inputs = []
    kept = []
    for micro_idx in range(MICRO):
        w_qkv_full, w_out_full, w_up_full, w_down_full = (
            gathered[0],
            gathered[1],
            gathered[2],
            gathered[3],
        )
        vectors = [piece.astype(jnp.float32) for piece in gathered[4:]]
        (
            bias_query,
            bias_value,
            bias_out,
            bias_up,
            bias_down,
            gain_one,
            offset_one,
            gain_two,
            offset_two,
        ) = vectors
        start = micro_idx * IMG_MB
        inputs = tokens[start : start + IMG_MB].astype(jnp.float32)
        normed_one, norm_one_back = jax.vjp(normalize, inputs, gain_one, offset_one)
        normed_one_low = normed_one.astype(jnp.bfloat16)
        qkv_bias = jnp.concatenate([bias_query, jnp.zeros_like(bias_query), bias_value])
        projected = (
            jnp.einsum(
                "ptd,de->pte", normed_one_low, w_qkv_full, preferred_element_type=jnp.float32
            )
            + qkv_bias
        )
        projected_low = projected.astype(jnp.bfloat16).reshape(
            IMG_MB, local_patches, 3, model_width
        )
        by_heads = lax.all_to_all(projected_low, "seq", split_axis=3, concat_axis=1, tiled=True)
        queries = by_heads[:, :, 0].reshape(IMG_MB, patches, head_local, DH)
        keyed = by_heads[:, :, 1].reshape(IMG_MB, patches, head_local, DH)
        valued = by_heads[:, :, 2].reshape(IMG_MB, patches, head_local, DH)
        attended, log_total = forward_heads(queries, keyed, valued, factor)
        attended_low = attended.astype(jnp.bfloat16)
        mixed_tokens = lax.all_to_all(attended_low, "seq", split_axis=1, concat_axis=2, tiled=True)
        residual = (
            inputs
            + jnp.einsum(
                "pte,ed->ptd", mixed_tokens, w_out_full, preferred_element_type=jnp.float32
            )
            + bias_out
        )
        normed_two, norm_two_back = jax.vjp(normalize, residual, gain_two, offset_two)
        normed_two_low = normed_two.astype(jnp.bfloat16)
        upward = (
            jnp.einsum("ptd,df->ptf", normed_two_low, w_up_full, preferred_element_type=jnp.float32)
            + bias_up
        )
        activated, activate_back = jax.vjp(activate, upward)
        activated_low = activated.astype(jnp.bfloat16)
        layer_out = (
            residual
            + jnp.einsum(
                "ptf,fd->ptd", activated_low, w_down_full, preferred_element_type=jnp.float32
            )
            + bias_down
        )
        outputs.append(layer_out.astype(jnp.bfloat16))
        grad_result = cotangent[start : start + IMG_MB].astype(jnp.float32)
        grad_branch = grad_result.astype(jnp.bfloat16)
        grad_active = jnp.einsum(
            "ptd,fd->ptf", grad_branch, w_down_full, preferred_element_type=jnp.float32
        )
        (grad_upward,) = activate_back(grad_active)
        grad_upward_low = grad_upward.astype(jnp.bfloat16)
        grad_normed_two = jnp.einsum(
            "ptf,df->ptd", grad_upward_low, w_up_full, preferred_element_type=jnp.float32
        )
        grad_from_two, grad_gain2, grad_bias2 = norm_two_back(grad_normed_two)
        grad_residual = grad_result + grad_from_two
        grad_attn_low = grad_residual.astype(jnp.bfloat16)
        grad_mixed = jnp.einsum(
            "ptd,ed->pte", grad_attn_low, w_out_full, preferred_element_type=jnp.float32
        ).astype(jnp.bfloat16)
        grad_heads = lax.all_to_all(grad_mixed, "seq", split_axis=2, concat_axis=1, tiled=True)
        grad_query, grad_key, grad_value = backward_heads(
            queries,
            keyed,
            valued,
            grad_heads.reshape(IMG_MB, patches, head_local, DH),
            log_total,
            factor,
        )
        stacked = (
            jnp.stack([grad_query, grad_key, grad_value], axis=2)
            .reshape(IMG_MB, patches, 3, head_local * DH)
            .astype(jnp.bfloat16)
        )
        grad_parts = lax.all_to_all(stacked, "seq", split_axis=1, concat_axis=3, tiled=True)
        grad_projected = grad_parts.reshape(IMG_MB, local_patches, 3 * model_width)
        grad_normed_one = jnp.einsum(
            "pte,de->ptd", grad_projected, w_qkv_full, preferred_element_type=jnp.float32
        )
        grad_from_one, grad_gain1, grad_bias1 = norm_one_back(grad_normed_one)
        grad_inputs.append((grad_residual + grad_from_one).astype(jnp.bfloat16))
        norm_grads = (grad_gain1, grad_bias1, grad_gain2, grad_bias2)
        norm_total = norm_grads if micro_idx == 0 else add_pairs(norm_total, norm_grads)
        kept.append(
            (
                normed_one_low,
                grad_projected,
                mixed_tokens,
                grad_attn_low,
                normed_two_low,
                grad_upward_low,
                activated_low,
                grad_branch,
            )
        )
    joined = [jnp.concatenate([item[index] for item in kept], axis=0) for index in range(8)]
    big = weight_grads(
        joined[0],
        joined[1],
        joined[2],
        joined[3],
        joined[4],
        joined[5],
        joined[6],
        joined[7],
        model_width,
    )
    owned = (
        lax.psum_scatter(big[0].astype(jnp.bfloat16), "dp", scatter_dimension=0, tiled=True).astype(
            jnp.float32
        ),
        lax.psum_scatter(big[1].astype(jnp.bfloat16), "dp", scatter_dimension=0, tiled=True).astype(
            jnp.float32
        ),
        lax.psum_scatter(big[2].astype(jnp.bfloat16), "dp", scatter_dimension=0, tiled=True).astype(
            jnp.float32
        ),
        lax.psum_scatter(big[3].astype(jnp.bfloat16), "dp", scatter_dimension=1, tiled=True).astype(
            jnp.float32
        ),
        lax.psum_scatter(big[4].astype(jnp.bfloat16), "dp", scatter_dimension=0, tiled=True).astype(
            jnp.float32
        ),
        lax.psum_scatter(big[5].astype(jnp.bfloat16), "dp", scatter_dimension=0, tiled=True).astype(
            jnp.float32
        ),
        lax.psum_scatter(big[6].astype(jnp.bfloat16), "dp", scatter_dimension=0, tiled=True).astype(
            jnp.float32
        ),
        lax.psum_scatter(big[7].astype(jnp.bfloat16), "dp", scatter_dimension=0, tiled=True).astype(
            jnp.float32
        ),
        lax.psum_scatter(big[8].astype(jnp.bfloat16), "dp", scatter_dimension=0, tiled=True).astype(
            jnp.float32
        ),
        lax.psum_scatter(
            norm_total[0].astype(jnp.bfloat16), "dp", scatter_dimension=0, tiled=True
        ).astype(jnp.float32),
        lax.psum_scatter(
            norm_total[1].astype(jnp.bfloat16), "dp", scatter_dimension=0, tiled=True
        ).astype(jnp.float32),
        lax.psum_scatter(
            norm_total[2].astype(jnp.bfloat16), "dp", scatter_dimension=0, tiled=True
        ).astype(jnp.float32),
        lax.psum_scatter(
            norm_total[3].astype(jnp.bfloat16), "dp", scatter_dimension=0, tiled=True
        ).astype(jnp.float32),
    )
    owned = (
        lax.psum(owned[0].astype(jnp.bfloat16), "seq").astype(jnp.float32),
        lax.psum(owned[1].astype(jnp.bfloat16), "seq").astype(jnp.float32),
        lax.psum(owned[2].astype(jnp.bfloat16), "seq").astype(jnp.float32),
        lax.psum(owned[3].astype(jnp.bfloat16), "seq").astype(jnp.float32),
        lax.psum(owned[4].astype(jnp.bfloat16), "seq").astype(jnp.float32),
        lax.psum(owned[5].astype(jnp.bfloat16), "seq").astype(jnp.float32),
        lax.psum(owned[6].astype(jnp.bfloat16), "seq").astype(jnp.float32),
        lax.psum(owned[7].astype(jnp.bfloat16), "seq").astype(jnp.float32),
        lax.psum(owned[8].astype(jnp.bfloat16), "seq").astype(jnp.float32),
        lax.psum(owned[9].astype(jnp.bfloat16), "seq").astype(jnp.float32),
        lax.psum(owned[10].astype(jnp.bfloat16), "seq").astype(jnp.float32),
        lax.psum(owned[11].astype(jnp.bfloat16), "seq").astype(jnp.float32),
        lax.psum(owned[12].astype(jnp.bfloat16), "seq").astype(jnp.float32),
    )
    return (
        jnp.concatenate(outputs, axis=0),
        jnp.concatenate(grad_inputs, axis=0),
        owned[0],
        owned[1],
        owned[2],
        owned[3],
        owned[4],
        owned[5],
        owned[6],
        owned[7],
        owned[8],
        owned[9],
        owned[10],
        owned[11],
        owned[12],
    )


F32=jnp.float32; BF16=jnp.bfloat16
NT=(((1,),(1,)),((),())); TN=(((0,),(0,)),((),())); NN=(((1,),(0,)),((),()))
def dg(a,b,dims): return lax.dot_general(a,b,dims,preferred_element_type=F32)

MESH = pl.DeviceIdType.MESH
HBM = pltpu.MemorySpace.HBM


def device_map():
    d, z = lax.axis_index("dp"), lax.axis_index("seq")
    core, x, y = lax.rem(d, 2), lax.rem(d // 2, 2), d // 4
    par = lax.rem(z, 2)
    return dict(
        d=d, z=z, core=core, x=x, y=y, par=par,
        sibling=(d + 1 - 2 * core, z), over_x=(d + 2 - 4 * x, z), over_y=(d + 4 - 8 * y, z),
        near_z=(d, z + 1 - 2 * par), far_z=(d, z + 2 - 4 * (z // 2)),
        image=[(d - core + z // 2, 2 * core + b) for b in range(2)],
        home=(z // 2) == core,
    )


def remote(src, dst, send, recv, to):
    return pltpu.make_async_remote_copy(
        src_ref=src, dst_ref=dst, send_sem=send, recv_sem=recv, device_id=to, device_id_type=MESH
    )


def greet(place, names):
    barrier = pltpu.get_barrier_semaphore()
    for name in names:
        pl.semaphore_signal(barrier, inc=1, device_id=place[name], device_id_type=MESH)
    for b in range(2):
        @pl.when(jnp.logical_not(jnp.logical_and(place["home"], place["par"] == b)))
        def _(): pl.semaphore_signal(barrier, inc=1, device_id=place["image"][b], device_id_type=MESH)
    pl.semaphore_wait(barrier, len(names) + 2 - place["home"].astype(jnp.int32))


class Move:
    def __init__(self, place, sources, target, sems):
        self.place, self.sources, self.target, self.sems = place, sources, target, sems
    def each(self, far, near):
        p = self.place
        for b in range(2):
            stays = jnp.logical_and(p["home"], p["par"] == b)
            target = self.target(p["par"])
            @pl.when(jnp.logical_not(stays))
            def _(): far(remote(self.sources[b], target, self.sems.at[0, b], self.sems.at[1, p["par"]], p["image"][b]))
            @pl.when(stays)
            def _(): near(pltpu.make_async_copy(self.sources[b], target, self.sems.at[2, 0]))
    def start(self):
        self.each(lambda c: c.start(), lambda c: c.start())
    def wait(self):
        p = self.place
        self.each(lambda c: c.wait_send(), lambda c: c.wait())
        for h in range(2):
            @pl.when(jnp.logical_not(jnp.logical_and(p["home"], p["par"] == h)))
            def _(): remote(self.sources[0], self.target(h), self.sems.at[0, 0], self.sems.at[1, h], p["image"][0]).wait_recv()


def tiles(count, body, size=256):
    def step(i, carry):
        body(pl.ds(pl.multiple_of(i * size, size), size))
        return carry
    lax.fori_loop(0, count, step, 0)


def turn(place, source, target):
    for j in range(8):
        jy, jx, jc = j // 4, (j // 2) % 2, j % 2
        differ = lambda a, b: (a + b) - 2 * a * b
        at = differ(place["core"], jc) * 4 + differ(place["y"], jy) * 2 + differ(place["x"], jx)
        target[pl.ds(pl.multiple_of(at * 128, 128), 128), :] = source[:, 128 * j : 128 * j + 128].T


def fwd_kernel(
    tok_hbm, cotg_hbm, wq_s, wo_s, wu_s, wd_s, pack,
    wq_o, wo_o, wu_o, wd_o, x_o, cot_o, cot_t_o, n1_t_o, n2_t_o, att_t_o, qkv_o, kv_o, att_o, act_o, up_o, res_o, out_o,
    lse, vec,
    wq, wo, wu, wd, wdn, pk, xb, cot, n1, n2, qkv, kv, att, act, upb, up_bias, res, cot_t, n1_t, n2_t, att_t,
    ws, wr, wl, ps, pr, ms, kvs, kvr, outs, ups,
):
    p = device_map()
    y, x, core, par = p["y"], p["x"], p["core"], p["par"]
    greet(p, ("sibling", "over_x", "over_y"))

    def rows(py, px):
        return pl.ds(pl.multiple_of(((py * 2 + px) * 2 + core) * 128, 128), 128)

    chunks = [(wq, wq_s, 0, 3072), (wo, wo_s, 0, 1024), (wu, wu_s, 0, 2048), (wu, wu_s, 2048, 2048),
              (wd, None, 0, 2048), (wd, None, 2048, 2048)]
    me, bx, by, diag = rows(y, x), rows(y, 1 - x), rows(1 - y, x), rows(1 - y, 1 - x)

    def copy(n, i):
        w, shard, at, size = chunks[n]
        lo, hi, full = pl.ds(at, size // 2), pl.ds(at + size // 2, size // 2), pl.ds(at, size)
        own = (lambda cols: w.at[me, cols]) if shard is None else (lambda cols: shard.at[:, cols])
        src, dst, to = (
            (own(lo), w.at[me, lo], "over_x"), (own(hi), w.at[me, hi], "over_y"),
            (own(hi), w.at[me, hi], "over_x"), (own(lo), w.at[me, lo], "over_y"),
            (own(full), w.at[me, full], "sibling"),
            (w.at[bx, lo], w.at[bx, lo], "over_y"), (w.at[by, hi], w.at[by, hi], "over_x"),
            (w.at[bx, full], w.at[bx, full], "sibling"), (w.at[by, full], w.at[by, full], "sibling"),
            (w.at[diag, lo], w.at[diag, lo], "sibling"), (w.at[diag, hi], w.at[diag, hi], "sibling"),
        )[i]
        return remote(src, dst, ws.at[n, i], wr.at[n, i], p[to])

    def start(n, *which):
        for i in which: copy(n, i).start()

    def wait(n, *which):
        for i in which: copy(n, i).wait()

    def local(n):
        w, shard, at, size = chunks[n]
        return pltpu.make_async_copy(shard.at[:, pl.ds(at, size)], w.at[me, pl.ds(at, size)], wl.at[n])

    def own(n):
        start(n, 0, 1, 2, 3, 4)
        if chunks[n][1] is not None: local(n).start()

    def mid(n):
        wait(n, 0, 1)
        start(n, 5, 6)
        if n < 5: own(n + 1)

    def late(n):
        wait(n, 2, 3)
        start(n, 7, 8)

    def end(n):
        wait(n, 5, 6)
        start(n, 9, 10)
        wait(n, 4, 7, 8, 9, 10)
        if chunks[n][1] is not None: local(n).wait()

    given, settled = [], []
    def give(src, dst):
        c = pltpu.make_async_copy(src, dst, outs.at[len(given)])
        c.start()
        given.append(c)
        return c

    def settle(c):
        c.wait()
        settled.append(c)

    own(0)
    pk[y, x, core] = pack[...]
    hop1 = remote(pk.at[y, x, core], pk.at[y, x, core], ps.at[0], pr.at[0], p["over_x"])
    hop1.start()
    half = lambda h: pl.ds(pl.multiple_of(h * 256, 256), 256)
    tok = Move(p, [tok_hbm.at[b] for b in range(2)], lambda h: xb.at[half(h)], ms.at[0])
    tok.start()
    cot_move = Move(p, [cotg_hbm.at[b] for b in range(2)], lambda h: cot.at[half(h)], ms.at[1])
    cot_move.start()
    down = pltpu.make_async_copy(wd_s, wdn, wl.at[5])
    down.start()
    hop1.wait()
    hop2 = remote(pk.at[y, :, core], pk.at[y, :, core], ps.at[1], pr.at[1], p["over_y"])
    hop2.start()
    down.wait()
    for j in range(8):
        wd[me, 512 * j : 512 * j + 512] = wdn[512 * j : 512 * j + 512, :].T
    hop2.wait()
    hop3 = remote(pk.at[:, :, core], pk.at[:, :, core], ps.at[2], pr.at[2], p["sibling"])
    hop3.start()
    mid(0)
    hop3.wait()
    for j in range(8):
        block = pk[j // 4, (j // 2) % 2, j % 2]
        for r in range(12):
            if 3 <= r < 7:
                at = 512 * j + 128 * (r - 3)
                up_bias[:, at : at + 128] = block[r : r + 1]
            else:
                to = {0: 4, 1: 5, 2: 6, 7: 7, 8: 8, 9: 9, 10: 10, 11: 11}[r]
                vec[to : to + 1, 128 * j : 128 * j + 128] = block[r : r + 1]
    vec[0:4, :] = jnp.zeros((4, 1024), F32)
    vec[12:16, :] = jnp.zeros((4, 1024), F32)
    tok.wait()

    def stats(value):
        off = value - jnp.mean(value, axis=-1, keepdims=True)
        return off * lax.rsqrt(jnp.mean(off * off, axis=-1, keepdims=True) + norm_eps)

    def norm_one(r):
        n1[r, :] = (stats(xb[r, :].astype(F32)) * vec[8:9, :] + vec[9:10, :]).astype(BF16)
    tiles(8, norm_one, 64)
    x_given = give(xb, x_o)
    late(0)
    turn(p, n1, n1_t)
    give(n1_t, n1_t_o)
    end(0)
    give(wq, wq_o)
    mid(1)

    def project(cols, bias):
        part = dg(n1[...], wq[:, cols], NN)
        qkv[:, cols] = (part if bias is None else part + bias).astype(BF16)
    def key_cols(c): project(pl.ds(pl.multiple_of(1024 + c.start, 256), 256), None)
    tiles(4, key_cols)
    def value_cols(c): project(pl.ds(pl.multiple_of(2048 + c.start, 256), 256), vec[5:6, c])
    tiles(4, value_cols)
    swap = remote(qkv.at[:, pl.ds(1024, 2048)], kv, kvs, kvr, p["sibling"])
    swap.start()
    def query_cols(c): project(c, vec[4:5, c])
    tiles(4, query_cols)
    swap.wait()
    give(qkv, qkv_o)
    give(kv, kv_o)

    lane = lax.broadcasted_iota(jnp.int32, (512, 128), 1)
    def pair(i, carry):
        at = lambda base: pl.ds(pl.multiple_of(base + i * 128, 128), 128)
        q = qkv[:, at(0)] * jnp.asarray(0.125, BF16)
        outs_, ls = [], []
        for h in range(2):
            qh = jnp.where((lane < 64) if h == 0 else (lane >= 64), q, jnp.zeros_like(q))
            sa, sb = dg(qkv[:, at(1024)], qh, NT), dg(kv[:, at(0)], qh, NT)
            m = jnp.maximum(jnp.max(sa, axis=0, keepdims=True), jnp.max(sb, axis=0, keepdims=True))
            pa, pb = jnp.exp(sa - m), jnp.exp(sb - m)
            total = jnp.sum(pa, axis=0, keepdims=True) + jnp.sum(pb, axis=0, keepdims=True)
            o = dg(qkv[:, at(2048)], pa.astype(BF16), TN) + dg(kv[:, at(1024)], pb.astype(BF16), TN)
            outs_.append(o[64 * h : 64 * h + 64] * (1.0 / total))
            ls.append(m + jnp.log(total))
        att[:, at(0)] = jnp.concatenate(outs_, axis=0).T.astype(BF16)
        lse[i] = jnp.concatenate(ls + [jnp.zeros((6, 512), F32)], axis=0)
        @pl.when(i == 2)
        def _():
            late(1)
            end(1)
            mid(2)
        return carry
    lax.fori_loop(0, 8, pair, 0)
    give(wo, wo_o)
    give(att, att_o)
    late(2)
    end(2)
    mid(3)

    def out_cols(c):
        res[:, c] = xb[:, c].astype(F32) + dg(att[...], wo[:, c], NN) + vec[6:7, c]
    tiles(4, out_cols)
    res_given = give(res, res_o)
    def norm_two(r):
        n2[r, :] = (stats(res[r, :]) * vec[10:11, :] + vec[11:12, :]).astype(BF16)
    tiles(8, norm_two, 64)

    def up_copy(i):
        return pltpu.make_async_copy(upb.at[lax.rem(i, 2)], up_o.at[:, pl.ds(pl.multiple_of(i * 512, 512), 512)], ups.at[lax.rem(i, 2)])
    def up_block(i, carry):
        @pl.when(i >= 2)
        def _(): up_copy(i - 2).wait()
        for t in range(2):
            c = pl.ds(pl.multiple_of(i * 512 + 256 * t, 256), 256)
            u = dg(n2[...], wu[:, c], NN) + up_bias[:, c]
            upb[lax.rem(i, 2), :, 256 * t : 256 * t + 256] = u
            act[:, c] = (0.5 * u * (1.0 + jnp.tanh(0.7978845608028654 * (u + 0.044715 * u * u * u)))).astype(BF16)
        up_copy(i).start()
        return carry
    lax.fori_loop(0, 4, up_block, 0)
    turn(p, n2, n2_t)
    give(n2_t, n2_t_o)
    turn(p, att, att_t)
    give(att_t, att_t_o)
    cot_move.wait()
    give(cot, cot_o)
    turn(p, cot, cot_t)
    give(cot_t, cot_t_o)
    late(3)
    end(3)
    give(wu, wu_o)
    mid(4)
    lax.fori_loop(4, 8, up_block, 0)
    give(act, act_o)
    late(4)
    end(4)
    settle(res_given)
    first, second = pl.ds(0, 2048), pl.ds(2048, 2048)
    def half_down(c):
        res[:, c] += dg(act[:, first], wd[c, first], NT)
    tiles(4, half_down)
    mid(5)
    late(5)
    end(5)
    give(wd, wd_o)
    settle(x_given)
    def finish_cols(c):
        xb[:, c] = (res[:, c] + dg(act[:, second], wd[c, second], NT) + vec[7:8, c]).astype(BF16)
    tiles(4, finish_cols)
    give(xb, out_o)
    for c in given:
        if not any(c is s for s in settled): c.wait()
    up_copy(jnp.int32(6)).wait()
    up_copy(jnp.int32(7)).wait()


def forward(tokens, cotangent, shards, pack):
    any_, vmem, hbm = (pl.BlockSpec(memory_space=s) for s in (pl.ANY, pltpu.VMEM, HBM))
    dma = pltpu.SemaphoreType.DMA
    wide = [((1024, 3072), BF16), ((1024, 1024), BF16), ((1024, 4096), BF16), ((1024, 4096), BF16)]
    rows, turned = ((512, 1024), BF16), ((1024, 512), BF16)
    shapes = wide + [rows, rows] + [turned] * 4 + [
        ((512, 3072), BF16), ((512, 2048), BF16), rows, ((512, 4096), BF16), ((512, 4096), F32), ((512, 1024), F32), rows]
    return pl.pallas_call(
        fwd_kernel,
        in_specs=[any_] * 6 + [vmem],
        out_specs=[hbm] * len(shapes) + [vmem, vmem],
        out_shape=[jax.ShapeDtypeStruct(*s) for s in shapes + [((8, 8, 512), F32), ((16, 1024), F32)]],
        scratch_shapes=[pltpu.VMEM(*s) for s in wide + [
            ((4096, 128), BF16), ((2, 2, 2, 12, 128), F32), rows, rows, rows, rows, ((512, 3072), BF16), ((512, 2048), BF16),
            rows, ((512, 4096), BF16), ((2, 512, 512), F32), ((1, 4096), F32), ((512, 1024), F32)] + [turned] * 4]
        + [dma((6, 11)), dma((6, 11)), dma((6,)), dma((3,)), dma((3,)), dma((2, 3, 2)), dma, dma, dma((20,)), dma((2,))],
        compiler_params=pltpu.CompilerParams(collective_id=7, has_side_effects=True, vmem_limit_bytes=67043328),
        cost_estimate=pl.CostEstimate(flops=20 * 10**9, bytes_accessed=60 << 20, transcendentals=10**7),
        name="forward",
    )(tokens, cotangent, *shards, pack)


CHUNKS = 12


def gelu_slope(u):
    inner = 0.7978845608028654 * (u + 0.044715 * u * u * u)
    t = jnp.tanh(inner)
    return 0.5 * (1.0 + t) + 0.5 * u * (1.0 - t * t) * (0.7978845608028654 * (1.0 + 3 * 0.044715 * u * u))


def bwd_kernel(
    cot_hbm, cot_t_hbm, n2_t_hbm, act_hbm, up_hbm, wd_hbm, wu_hbm, wo_hbm, wq_hbm, att_t_hbm, n1_t_hbm,
    qkv_hbm, kv_hbm, att_hbm, out_hbm, res_hbm, x_hbm, lse_ref, vec,
    gd_out, gu_out, go_out, gq_out, result_out, gin_out, small_out,
    sums_ref, sum_in, so, sr, g, h1a, h1b, h2a, h2b, z1, z2, z3, fin, dkv_in, cot, gres,
    sib_s, sib_r, hop_s, hop_r, zs, zr, fin_sem, dkv_s, dkv_r, load, ms, ss, sm,
):
    p = device_map()
    x, y, core, par, z = p["x"], p["y"], p["core"], p["par"], p["z"]
    sibling, over_x, over_y, near_z, far_z = (p[n] for n in ("sibling", "over_x", "over_y", "near_z", "far_z"))
    greet(p, ("sibling", "over_x", "over_y", "near_z", "far_z"))

    lo, hi = pl.ds(0, 512), pl.ds(512, 512)
    keep = pl.ds(pl.multiple_of(par * 512, 512), 512)
    give = pl.ds(pl.multiple_of((1 - par) * 512, 512), 512)

    def to_sib(k):
        return remote(so.at[lax.rem(k, 2)], sr.at[lax.rem(k, 2)], sib_s.at[k], sib_r.at[k], sibling)

    def hop(k, j):
        src, dst, to = (
            (g.at[k, 1, :, :, lo], h1a.at[k], over_y),
            (g.at[k, :, 1, :, hi], h1b.at[k], over_x),
            (g.at[k, 0, 1, :, lo], h2a.at[k], over_x),
            (g.at[k, 1, 0, :, hi], h2b.at[k], over_y),
        )[j]
        return remote(src, dst, hop_s.at[k, j], hop_r.at[k, j], to)

    def zhop(k, j):
        src, dst, to = (
            (g.at[k, 0, 0, :, give], z1.at[k], near_z),
            (g.at[k, 0, 0, :, keep], z2.at[k], far_z),
            (g.at[k, 0, 0, :, keep], z3.at[k], near_z),
        )[j]
        return remote(src, dst, zs.at[k, j], zr.at[k, j], to)

    def plus(a, b):
        return (a.astype(F32) + b.astype(F32)).astype(BF16)

    def out_copy(k):
        slot = lax.rem(k, 2)
        def with_target(run):
            col = lambda j: pl.ds(pl.multiple_of(j * 1024, 1024), 1024)
            sem = fin_sem.at[slot]
            @pl.when(jnp.logical_and(k < 8, lax.rem(k, 2) == 0))
            def _(): run(pltpu.make_async_copy(fin.at[slot], gd_out.at[:, col(k // 2)], sem))
            @pl.when(jnp.logical_and(k < 8, lax.rem(k, 2) == 1))
            def _(): run(pltpu.make_async_copy(fin.at[slot], gu_out.at[:, col(k // 2)], sem))
            @pl.when(k == 8)
            def _(): run(pltpu.make_async_copy(fin.at[slot], go_out, sem))
            @pl.when(k > 8)
            def _(): run(pltpu.make_async_copy(fin.at[slot], gq_out.at[:, col(k - 9)], sem))
        return with_target

    def tick(n):
        def stage(k, body):
            @pl.when(jnp.logical_and(k >= 0, k < CHUNKS))
            def _(): body(k)

        def c2(k):
            hop(k, 0).wait(); hop(k, 1).wait()
            g[k, 0, :, :, lo] = plus(g[k, 0, :, :, lo], h1a[k])
            g[k, :, 0, :, hi] = plus(g[k, :, 0, :, hi], h1b[k])
            hop(k, 2).start(); hop(k, 3).start()

        def c3(k):
            hop(k, 2).wait(); hop(k, 3).wait()
            g[k, 0, 0, :, lo] = plus(g[k, 0, 0, :, lo], h2a[k])
            g[k, 0, 0, :, hi] = plus(g[k, 0, 0, :, hi], h2b[k])
            zhop(k, 0).start()

        def c4(k):
            zhop(k, 0).wait()
            g[k, 0, 0, :, keep] = plus(g[k, 0, 0, :, keep], z1[k])
            zhop(k, 1).start()

        def c5(k):
            zhop(k, 1).wait()
            g[k, 0, 0, :, keep] = plus(g[k, 0, 0, :, keep], z2[k])
            zhop(k, 2).start()

        def c6(k):
            zhop(k, 2).wait()
            slot = lax.rem(k, 2)
            @pl.when(k >= 2)
            def _(): out_copy(k - 2)(lambda c: c.wait())
            fin[slot, :, keep] = g[k, 0, 0, :, keep].astype(F32)
            fin[slot, :, give] = z3[k].astype(F32)
            out_copy(k)(lambda c: c.start())

        stage(n, c2); stage(n - 1, c3); stage(n - 2, c4); stage(n - 3, c5); stage(n - 4, c6)

    def send_odd(k, left, right):
        def one(cols):
            so[lax.rem(k, 2), :, cols] = dg(left[512:1024, :], right[:, cols], NN).astype(BF16)
        tiles(4, one)
        to_sib(k).start()

    def add_even(k, left, right):
        to_sib(k).wait()
        def one(cols):
            part = dg(left[0:512, :], right[:, cols], NN) + sr[lax.rem(k, 2), :, cols].astype(F32)
            g[k, :, :, :, cols] = part.astype(BF16).reshape(2, 2, 128, 256)
        tiles(4, one)
        hop(k, 0).start(); hop(k, 1).start()

    def fetch(src, dst, i):
        return pltpu.make_async_copy(src, dst, load.at[i])

    first = fetch(cot_hbm, cot, 0)
    first.start()
    result = Move(p, [out_hbm.at[pl.ds(256 * h, 256)] for h in range(2)], lambda b: result_out.at[b], ms.at[0])
    result.start()
    sums_ref[...] = jnp.zeros_like(sums_ref)

    def mlp(cot_t, n2_t, actb, upb, wdb, wub, gub, gn2, resb):
        pieces = [fetch(cot_t_hbm, cot_t, 1), fetch(n2_t_hbm, n2_t, 2), fetch(res_hbm, resb, 3)]
        for c in pieces: c.start()
        def parts(j):
            cols = pl.ds(pl.multiple_of(j * 1024, 1024), 1024)
            s = lax.rem(j, 2)
            return [
                pltpu.make_async_copy(src.at[:, cols], dst.at[s], load.at[4 + 4 * s + i])
                for i, (src, dst) in enumerate(((act_hbm, actb), (up_hbm, upb), (wd_hbm, wdb), (wu_hbm, wub)))
            ]
        for c in parts(jnp.int32(0)): c.start()
        gn2[...] = jnp.zeros_like(gn2)
        first.wait()
        pieces[0].wait()
        pieces[1].wait()
        def block(j, carry):
            s = lax.rem(j, 2)
            for c in parts(j): c.wait()
            @pl.when(j < 3)
            def _():
                for c in parts(j + 1): c.start()
            kd, ku = 2 * j, 2 * j + 1
            send_odd(kd, cot_t, actb.at[s])
            def slope(cols):
                back = dg(cot[...], wdb[s, :, cols], NN)
                low = (back * gelu_slope(upb[s, :, cols])).astype(BF16)
                gub[:, cols] = low
                sums_ref[pl.ds(j, 1), cols] = jnp.sum(low.astype(F32), axis=0, keepdims=True)
            tiles(4, slope)
            add_even(kd, cot_t, actb.at[s])
            send_odd(ku, n2_t, gub)
            def down(cols):
                gn2[:, cols] += dg(gub[...], wub[s, cols, :], NT)
            tiles(4, down)
            add_even(ku, n2_t, gub)
            @pl.when(j > 0)
            def _(): tick(j - 1)
            return carry
        lax.fori_loop(0, 4, block, 0)
        pieces[2].wait()
        def rows(r):
            res = resb[r, :]
            centre = jnp.mean(res, axis=-1, keepdims=True)
            off = res - centre
            rstd = lax.rsqrt(jnp.mean(off * off, axis=-1, keepdims=True) + norm_eps)
            xhat = off * rstd
            grad = gn2[r, :]
            e = grad * vec[10:11, :]
            back = rstd * (e - jnp.mean(e, axis=-1, keepdims=True) - xhat * jnp.mean(e * xhat, axis=-1, keepdims=True))
            total = cot[r, :].astype(F32) + back
            gres[r, :] = total
            low = total.astype(BF16).astype(F32)
            add = lambda i, v: sums_ref.__setitem__((slice(i, i + 1), slice(None)), sums_ref[i : i + 1, :] + jnp.sum(v, axis=0, keepdims=True))
            add(4, low); add(5, grad * xhat); add(6, grad); add(7, cot[r, :].astype(F32))
        tiles(8, rows, 64)

    pl.run_scoped(
        mlp, pltpu.VMEM((1024, 512), BF16), pltpu.VMEM((1024, 512), BF16), pltpu.VMEM((2, 512, 1024), BF16),
        pltpu.VMEM((2, 512, 1024), F32), pltpu.VMEM((2, 1024, 1024), BF16), pltpu.VMEM((2, 1024, 1024), BF16),
        pltpu.VMEM((512, 1024), BF16), pltpu.VMEM((512, 1024), F32), pltpu.VMEM((512, 1024), F32),
    )

    def rest(dqkv, n1_t, xb):
        late = [fetch(n1_t_hbm, n1_t, 0), fetch(x_hbm, xb, 1)]
        for c in late: c.start()

        def attention(wo, att_t, ga, q, ka, kb, va, vb, att, do, dob):
            loads = [
                fetch(src, dst, 2 + i) for i, (src, dst) in enumerate((
                    (wo_hbm, wo), (att_t_hbm, att_t), (qkv_hbm.at[:, pl.ds(0, 1024)], q), (qkv_hbm.at[:, pl.ds(1024, 1024)], ka), (kv_hbm.at[:, pl.ds(0, 1024)], kb),
                    (qkv_hbm.at[:, pl.ds(2048, 1024)], va), (kv_hbm.at[:, pl.ds(1024, 1024)], vb), (att_hbm, att),
                ))
            ]
            for c in loads: c.start()
            tick(jnp.int32(3))
            ga[...] = gres[...].astype(BF16)
            for c in loads: c.wait()
            send_odd(jnp.int32(8), att_t, ga)
            def mixed(cols):
                do[:, cols] = dg(ga[...], wo[cols, :], NT).astype(BF16)
            tiles(4, mixed)
            add_even(jnp.int32(8), att_t, ga)
            lane = lax.broadcasted_iota(jnp.int32, (512, 128), 1)
            def pair(i, carry):
                cols = pl.ds(pl.multiple_of(i * 128, 128), 128)
                qs = q[:, cols] * jnp.asarray(0.125, BF16)
                dos = do[:, cols]
                t = (dos.astype(F32) * att[:, cols].astype(F32)).T
                dq, dk, dv = None, [None, None], [None, None]
                plus_ = lambda a, b: b if a is None else a + b
                for h in range(2):
                    sel = (lane < 64) if h == 0 else (lane >= 64)
                    qh = jnp.where(sel, qs, jnp.zeros_like(qs))
                    doh = jnp.where(sel, dos, jnp.zeros_like(dos))
                    delta = jnp.sum(t[64 * h : 64 * h + 64], axis=0, keepdims=True)
                    lse = lse_ref[i, h : h + 1, :]
                    for n, (k_ref, v_ref) in enumerate(((ka, va), (kb, vb))):
                        kk = k_ref[:, cols]
                        s = dg(kk, qh, NT)
                        p = jnp.exp(s - lse)
                        dp = dg(v_ref[:, cols], doh, NT)
                        ds = (p * (dp - delta)).astype(BF16)
                        dv[n] = plus_(dv[n], dg(p.astype(BF16), doh, NN))
                        dk[n] = plus_(dk[n], dg(ds, qh, NN))
                        dq = plus_(dq, dg(jnp.where(sel, kk, jnp.zeros_like(kk)), ds, TN))
                at = lambda base: pl.ds(pl.multiple_of(base + i * 128, 128), 128)
                dqkv[:, at(0)] = (dq * 0.125).T.astype(BF16)
                dqkv[:, at(1024)] = dk[0].astype(BF16)
                dqkv[:, at(2048)] = dv[0].astype(BF16)
                dob[:, at(0)] = dk[1].astype(BF16)
                dob[:, at(1024)] = dv[1].astype(BF16)
                @pl.when(lax.rem(i, 3) == 1)
                def _(): tick(4 + i // 3)
                return carry
            lax.fori_loop(0, 8, pair, 0)
            swap = remote(dob, dkv_in, dkv_s, dkv_r, sibling)
            swap.start()
            late[0].wait()
            send_odd(jnp.int32(9), n1_t, dqkv.at[:, pl.ds(0, 1024)])
            swap.wait()

        pl.run_scoped(
            attention, pltpu.VMEM((1024, 1024), BF16), pltpu.VMEM((1024, 512), BF16),
            *[pltpu.VMEM((512, 1024), BF16)] * 8, pltpu.VMEM((512, 2048), BF16),
        )

        def last(wq, gn1):
            def wq_part(i):
                s = lax.rem(i, 2)
                return pltpu.make_async_copy(wq_hbm.at[pl.ds(pl.multiple_of(i * 256, 256), 256), :], wq.at[s], load.at[2 + s])
            wq_part(jnp.int32(0)).start()
            def join(cols):
                there = pl.ds(pl.multiple_of(1024 + cols.start, 256), 256)
                dqkv[:, there] = plus(dqkv[:, there], dkv_in[:, cols])
            tiles(8, join)
            add_even(jnp.int32(9), n1_t, dqkv.at[:, pl.ds(0, 1024)])
            for k in (10, 11):
                right = dqkv.at[:, pl.ds(1024 * (k - 9), 1024)]
                send_odd(jnp.int32(k), n1_t, right)
                if k == 10:
                    tick(jnp.int32(7))
                add_even(jnp.int32(k), n1_t, right)
            def back(i, carry):
                wq_part(i).wait()
                @pl.when(i < 3)
                def _(): wq_part(i + 1).start()
                gn1[:, pl.ds(pl.multiple_of(i * 256, 256), 256)] = dg(dqkv[...], wq[lax.rem(i, 2)], NT)
                return carry
            lax.fori_loop(0, 4, back, 0)
            tick(jnp.int32(8))
            late[1].wait()
            def rows(r):
                xx = xb[r, :].astype(F32)
                centre = jnp.mean(xx, axis=-1, keepdims=True)
                off = xx - centre
                rstd = lax.rsqrt(jnp.mean(off * off, axis=-1, keepdims=True) + norm_eps)
                xhat = off * rstd
                grad = gn1[r, :]
                e = grad * vec[8:9, :]
                back = rstd * (e - jnp.mean(e, axis=-1, keepdims=True) - xhat * jnp.mean(e * xhat, axis=-1, keepdims=True))
                xb[r, :] = (gres[r, :] + back).astype(BF16)
                add = lambda i, v: sums_ref.__setitem__((slice(i, i + 1), slice(None)), sums_ref[i : i + 1, :] + jnp.sum(v, axis=0, keepdims=True))
                add(8, grad * xhat); add(9, grad)
                add(10, dqkv[r, 0:1024].astype(F32)); add(11, dqkv[r, 2048:3072].astype(F32))
            tiles(8, rows, 64)
            given = Move(p, [xb.at[pl.ds(256 * h, 256)] for h in range(2)], lambda b: gin_out.at[b], ms.at[1])
            given.start()
            steps = [
                remote(sums_ref, sum_in.at[i], ss.at[i], sm.at[i], to)
                for i, to in enumerate((sibling, over_x, over_y, near_z, far_z))
            ]
            steps[0].start()
            for i in range(7):
                tick(jnp.int32(9 + i))
                if i < 5:
                    steps[i].wait()
                    sums_ref[...] += sum_in[i]
                    if i < 4: steps[i + 1].start()
            d = p["d"]
            mine = pl.ds(pl.multiple_of(d * 128, 128), 128)
            for to, at in ((0, 10), (1, 11), (2, 4), (7, 7), (8, 8), (9, 9), (10, 5), (11, 6)):
                small_out[to : to + 1, :] = sums_ref[at : at + 1, mine]
            for t in range(4):
                lanes = pl.ds(pl.multiple_of(lax.rem(d, 2) * 512 + 128 * t, 128), 128)
                part = sums_ref[0:1, lanes]
                for r in range(1, 4):
                    part = jnp.where(d // 2 == r, sums_ref[r : r + 1, lanes], part)
                small_out[3 + t : 4 + t, :] = part
            for k in (CHUNKS - 2, CHUNKS - 1):
                out_copy(jnp.int32(k))(lambda c: c.wait())
            given.wait()
            result.wait()

        pl.run_scoped(last, pltpu.VMEM((2, 256, 3072), BF16), pltpu.VMEM((512, 1024), F32))

    pl.run_scoped(rest, pltpu.VMEM((512, 3072), BF16), pltpu.VMEM((1024, 512), BF16), pltpu.VMEM((512, 1024), BF16))


def backward(arrays, lse, vec):
    any_, vmem, hbm = (pl.BlockSpec(memory_space=s) for s in (pl.ANY, pltpu.VMEM, HBM))
    n = CHUNKS
    dma = pltpu.SemaphoreType.DMA
    return pl.pallas_call(
        bwd_kernel,
        in_specs=[any_] * len(arrays) + [vmem, vmem],
        out_specs=[hbm] * 6 + [vmem],
        out_shape=[jax.ShapeDtypeStruct((128, w), F32) for w in (4096, 4096, 1024, 3072)]
        + [jax.ShapeDtypeStruct((2, 256, 1024), BF16)] * 2 + [jax.ShapeDtypeStruct((12, 128), F32)],
        scratch_shapes=[
            pltpu.VMEM((16, 1024), F32), pltpu.VMEM((5, 16, 1024), F32),
            pltpu.VMEM((2, 512, 1024), BF16), pltpu.VMEM((2, 512, 1024), BF16), pltpu.VMEM((n, 2, 2, 128, 1024), BF16),
            pltpu.VMEM((n, 2, 128, 512), BF16), pltpu.VMEM((n, 2, 128, 512), BF16),
            pltpu.VMEM((n, 128, 512), BF16), pltpu.VMEM((n, 128, 512), BF16),
            pltpu.VMEM((n, 128, 512), BF16), pltpu.VMEM((n, 128, 512), BF16), pltpu.VMEM((n, 128, 512), BF16),
            pltpu.VMEM((2, 128, 1024), F32), pltpu.VMEM((512, 2048), BF16), pltpu.VMEM((512, 1024), BF16),
            pltpu.VMEM((512, 1024), F32),
            dma((n,)), dma((n,)), dma((n, 4)), dma((n, 4)), dma((n, 3)), dma((n, 3)), dma((2,)), dma, dma, dma((12,)),
            dma((2, 3, 2)), dma((5,)), dma((5,)),
        ],
        compiler_params=pltpu.CompilerParams(collective_id=8, has_side_effects=True, vmem_limit_bytes=67043328),
        cost_estimate=pl.CostEstimate(flops=40 * 10**9, bytes_accessed=60 << 20, transcendentals=10**7),
        name="backward",
    )(*arrays, lse, vec)


def local_fast(
    tokens, w_qkv, w_out, w_up, w_down, b_query, b_value, b_out, b_up, b_down,
    ln1_gain, ln1_bias, ln2_gain, ln2_bias, cotangent,
):
    small = (b_query, b_value, b_out, b_up, b_down, ln1_gain, ln1_bias, ln2_gain, ln2_bias)
    pack, at = jnp.zeros((12, 128), F32), 0
    for item in small:
        rows = item.shape[0] // 128
        pack = pack + jnp.pad(item.astype(F32).reshape(rows, 128), ((at, 12 - at - rows), (0, 0)))
        at += rows
    (wq, wo, wu, wd, x, cot, cot_t, n1_t, n2_t, att_t, qkv, kv, att, act, up, res, out, lse, vec) = forward(
        tokens, cotangent, (w_qkv, w_out, w_up, w_down), pack)
    g_down, g_up, g_out, g_qkv, result, grad_input, sums = backward(
        (cot, cot_t, n2_t, act, up, wd, wu, wo, wq, att_t, n1_t, qkv, kv, att, out, res, x), lse, vec)
    outs, at = [], 0
    for item in small:
        rows = item.shape[0] // 128
        outs.append(sums[at : at + rows].reshape(-1))
        at += rows
    return (result, grad_input, g_qkv, g_out, g_up, g_down.T, *outs)


def solution(mesh):
    in_specs = (
        P("dp", "seq", None),
        P("dp", None),
        P("dp", None),
        P("dp", None),
        P(None, "dp"),
        P("dp"),
        P("dp"),
        P("dp"),
        P("dp"),
        P("dp"),
        P("dp"),
        P("dp"),
        P("dp"),
        P("dp"),
        P("dp", "seq", None),
    )
    out_specs = (
        P("dp", "seq", None),
        P("dp", "seq", None),
        P("dp", None),
        P("dp", None),
        P("dp", None),
        P(None, "dp"),
        P("dp"),
        P("dp"),
        P("dp"),
        P("dp"),
        P("dp"),
        P("dp"),
        P("dp"),
        P("dp"),
        P("dp"),
    )
    fn = local_fast if dict(mesh.shape) == {"dp": 8, "seq": 4} else local
    return jax.shard_map(fn, mesh=mesh, in_specs=in_specs, out_specs=out_specs, check_vma=False)
```

```python
import functools

import jax
import jax.numpy as jnp
from jax import lax
from jax.experimental import pallas as pl
from jax.experimental.pallas import tpu as pltpu
from jax.sharding import PartitionSpec as P

H = 16
DH = 64
MICRO = 2
IMG_MB = 1


norm_eps = 1e-06


def normalize(inputs, ln_gain, ln_offset):
    centre = jnp.mean(inputs, axis=-1, keepdims=True)
    spread = jnp.mean(jnp.square(inputs - centre), axis=-1, keepdims=True)
    return (inputs - centre) * lax.rsqrt(spread + norm_eps) * ln_gain + ln_offset


def activate(upward):
    return jax.nn.gelu(upward, approximate=True)


def add_pairs(first_set, second_set):
    return tuple(
        (first_item + second_item for first_item, second_item in zip(first_set, second_set))
    )


def forward_heads(queries, keyed, valued, factor):
    images, length, head_count, head_size = queries.shape
    block_rows = min(512, length)
    blocks = length // block_rows
    query_blocks = queries.reshape(images, blocks, block_rows, head_count, head_size)

    def forward_per_image(element):
        q_image, k_image, v_image = element

        def forward_per_block(q_block):
            scores = (
                jnp.einsum("qhd,khd->hqk", q_block, k_image, preferred_element_type=jnp.float32)
                * factor
            )
            row_max = jnp.max(scores, axis=-1, keepdims=True)
            exponent = jnp.exp(scores - row_max)
            row_total = jnp.sum(exponent, axis=-1, keepdims=True)
            attn_probs = (exponent / row_total).astype(jnp.bfloat16)
            mixture = jnp.einsum(
                "hqk,khd->qhd", attn_probs, v_image, preferred_element_type=jnp.float32
            )
            return (mixture, row_max[..., 0] + jnp.log(row_total[..., 0]))

        return lax.map(forward_per_block, q_image)

    mixture, log_total = lax.map(forward_per_image, (query_blocks, keyed, valued))
    return (mixture.reshape(images, length, head_count * head_size), log_total)


def backward_heads(queries, keyed, valued, grad_mixed, log_total, factor):
    images, length, head_count, head_size = queries.shape
    block_rows = min(512, length)
    blocks = length // block_rows
    query_blocks = queries.reshape(images, blocks, block_rows, head_count, head_size)
    grad_blocks = grad_mixed.reshape(images, blocks, block_rows, head_count, head_size)

    def backward_per_image(element):
        q_image, k_image, v_image, g_image, l_image = element

        def backward_per_block(running, pieces):
            grad_key, grad_value = running
            q_block, g_block, l_block = pieces
            scores = (
                jnp.einsum("qhd,khd->hqk", q_block, k_image, preferred_element_type=jnp.float32)
                * factor
            )
            full_probs = jnp.exp(scores - l_block[..., None])
            grad_probs = jnp.einsum(
                "qhd,khd->hqk", g_block, v_image, preferred_element_type=jnp.float32
            )
            row_inner = jnp.sum(full_probs * grad_probs, axis=-1, keepdims=True)
            grad_scores = (full_probs * (grad_probs - row_inner)).astype(jnp.bfloat16)
            grad_query = (
                jnp.einsum("hqk,khd->qhd", grad_scores, k_image, preferred_element_type=jnp.float32)
                * factor
            )
            grad_key = (
                grad_key
                + jnp.einsum(
                    "hqk,qhd->khd", grad_scores, q_block, preferred_element_type=jnp.float32
                )
                * factor
            )
            grad_value = grad_value + jnp.einsum(
                "hqk,qhd->khd",
                full_probs.astype(jnp.bfloat16),
                g_block,
                preferred_element_type=jnp.float32,
            )
            return ((grad_key, grad_value), grad_query)

        empty_sum = jnp.zeros((length, head_count, head_size), jnp.float32)
        (grad_key, grad_value), grad_query = lax.scan(
            backward_per_block, (empty_sum, empty_sum), (q_image, g_image, l_image)
        )
        return (grad_query.reshape(length, head_count, head_size), grad_key, grad_value)

    return lax.map(backward_per_image, (query_blocks, keyed, valued, grad_blocks, log_total))


def weight_grads(
    normed_one_low,
    grad_projected,
    mixed_tokens,
    grad_attn_low,
    normed_two_low,
    grad_upward_low,
    activated_low,
    grad_branch,
    model_width,
):
    grad_qkv = jnp.einsum(
        "ptd,pte->de", normed_one_low, grad_projected, preferred_element_type=jnp.float32
    )
    grad_bquery = jnp.sum(grad_projected[:, :, :model_width], axis=(0, 1), dtype=jnp.float32)
    grad_bvalue = jnp.sum(grad_projected[:, :, 2 * model_width :], axis=(0, 1), dtype=jnp.float32)
    grad_wout = jnp.einsum(
        "pte,ptd->ed", mixed_tokens, grad_attn_low, preferred_element_type=jnp.float32
    )
    grad_bout = jnp.sum(grad_attn_low, axis=(0, 1), dtype=jnp.float32)
    grad_up = jnp.einsum(
        "ptd,ptf->df", normed_two_low, grad_upward_low, preferred_element_type=jnp.float32
    )
    grad_bup = jnp.sum(grad_upward_low, axis=(0, 1), dtype=jnp.float32)
    grad_down = jnp.einsum(
        "ptf,ptd->fd", activated_low, grad_branch, preferred_element_type=jnp.float32
    )
    grad_bdown = jnp.sum(grad_branch, axis=(0, 1), dtype=jnp.float32)
    return (
        grad_qkv,
        grad_wout,
        grad_up,
        grad_down,
        grad_bquery,
        grad_bvalue,
        grad_bout,
        grad_bup,
        grad_bdown,
    )


def local(
    tokens,
    w_qkv,
    w_out,
    w_up,
    w_down,
    b_query,
    b_value,
    b_out,
    b_up,
    b_down,
    ln1_gain,
    ln1_bias,
    ln2_gain,
    ln2_bias,
    cotangent,
):
    seq_count = lax.axis_size("seq")
    local_patches = tokens.shape[1]
    model_width = tokens.shape[2]
    patches = local_patches * seq_count
    head_local = H // seq_count
    factor = DH ** (-0.5)
    gathered = (
        lax.all_gather(w_qkv, "dp", axis=0, tiled=True),
        lax.all_gather(w_out, "dp", axis=0, tiled=True),
        lax.all_gather(w_up, "dp", axis=0, tiled=True),
        lax.all_gather(w_down, "dp", axis=1, tiled=True),
        lax.all_gather(b_query, "dp", axis=0, tiled=True),
        lax.all_gather(b_value, "dp", axis=0, tiled=True),
        lax.all_gather(b_out, "dp", axis=0, tiled=True),
        lax.all_gather(b_up, "dp", axis=0, tiled=True),
        lax.all_gather(b_down, "dp", axis=0, tiled=True),
        lax.all_gather(ln1_gain, "dp", axis=0, tiled=True),
        lax.all_gather(ln1_bias, "dp", axis=0, tiled=True),
        lax.all_gather(ln2_gain, "dp", axis=0, tiled=True),
        lax.all_gather(ln2_bias, "dp", axis=0, tiled=True),
    )
    outputs = []
    grad_inputs = []
    kept = []
    for micro_idx in range(MICRO):
        w_qkv_full, w_out_full, w_up_full, w_down_full = (
            gathered[0],
            gathered[1],
            gathered[2],
            gathered[3],
        )
        vectors = [piece.astype(jnp.float32) for piece in gathered[4:]]
        (
            bias_query,
            bias_value,
            bias_out,
            bias_up,
            bias_down,
            gain_one,
            offset_one,
            gain_two,
            offset_two,
        ) = vectors
        start = micro_idx * IMG_MB
        inputs = tokens[start : start + IMG_MB].astype(jnp.float32)
        normed_one, norm_one_back = jax.vjp(normalize, inputs, gain_one, offset_one)
        normed_one_low = normed_one.astype(jnp.bfloat16)
        qkv_bias = jnp.concatenate([bias_query, jnp.zeros_like(bias_query), bias_value])
        projected = (
            jnp.einsum(
                "ptd,de->pte", normed_one_low, w_qkv_full, preferred_element_type=jnp.float32
            )
            + qkv_bias
        )
        projected_low = projected.astype(jnp.bfloat16).reshape(
            IMG_MB, local_patches, 3, model_width
        )
        by_heads = lax.all_to_all(projected_low, "seq", split_axis=3, concat_axis=1, tiled=True)
        queries = by_heads[:, :, 0].reshape(IMG_MB, patches, head_local, DH)
        keyed = by_heads[:, :, 1].reshape(IMG_MB, patches, head_local, DH)
        valued = by_heads[:, :, 2].reshape(IMG_MB, patches, head_local, DH)
        attended, log_total = forward_heads(queries, keyed, valued, factor)
        attended_low = attended.astype(jnp.bfloat16)
        mixed_tokens = lax.all_to_all(attended_low, "seq", split_axis=1, concat_axis=2, tiled=True)
        residual = (
            inputs
            + jnp.einsum(
                "pte,ed->ptd", mixed_tokens, w_out_full, preferred_element_type=jnp.float32
            )
            + bias_out
        )
        normed_two, norm_two_back = jax.vjp(normalize, residual, gain_two, offset_two)
        normed_two_low = normed_two.astype(jnp.bfloat16)
        upward = (
            jnp.einsum("ptd,df->ptf", normed_two_low, w_up_full, preferred_element_type=jnp.float32)
            + bias_up
        )
        activated, activate_back = jax.vjp(activate, upward)
        activated_low = activated.astype(jnp.bfloat16)
        layer_out = (
            residual
            + jnp.einsum(
                "ptf,fd->ptd", activated_low, w_down_full, preferred_element_type=jnp.float32
            )
            + bias_down
        )
        outputs.append(layer_out.astype(jnp.bfloat16))
        grad_result = cotangent[start : start + IMG_MB].astype(jnp.float32)
        grad_branch = grad_result.astype(jnp.bfloat16)
        grad_active = jnp.einsum(
            "ptd,fd->ptf", grad_branch, w_down_full, preferred_element_type=jnp.float32
        )
        (grad_upward,) = activate_back(grad_active)
        grad_upward_low = grad_upward.astype(jnp.bfloat16)
        grad_normed_two = jnp.einsum(
            "ptf,df->ptd", grad_upward_low, w_up_full, preferred_element_type=jnp.float32
        )
        grad_from_two, grad_gain2, grad_bias2 = norm_two_back(grad_normed_two)
        grad_residual = grad_result + grad_from_two
        grad_attn_low = grad_residual.astype(jnp.bfloat16)
        grad_mixed = jnp.einsum(
            "ptd,ed->pte", grad_attn_low, w_out_full, preferred_element_type=jnp.float32
        ).astype(jnp.bfloat16)
        grad_heads = lax.all_to_all(grad_mixed, "seq", split_axis=2, concat_axis=1, tiled=True)
        grad_query, grad_key, grad_value = backward_heads(
            queries,
            keyed,
            valued,
            grad_heads.reshape(IMG_MB, patches, head_local, DH),
            log_total,
            factor,
        )
        stacked = (
            jnp.stack([grad_query, grad_key, grad_value], axis=2)
            .reshape(IMG_MB, patches, 3, head_local * DH)
            .astype(jnp.bfloat16)
        )
        grad_parts = lax.all_to_all(stacked, "seq", split_axis=1, concat_axis=3, tiled=True)
        grad_projected = grad_parts.reshape(IMG_MB, local_patches, 3 * model_width)
        grad_normed_one = jnp.einsum(
            "pte,de->ptd", grad_projected, w_qkv_full, preferred_element_type=jnp.float32
        )
        grad_from_one, grad_gain1, grad_bias1 = norm_one_back(grad_normed_one)
        grad_inputs.append((grad_residual + grad_from_one).astype(jnp.bfloat16))
        norm_grads = (grad_gain1, grad_bias1, grad_gain2, grad_bias2)
        norm_total = norm_grads if micro_idx == 0 else add_pairs(norm_total, norm_grads)
        kept.append(
            (
                normed_one_low,
                grad_projected,
                mixed_tokens,
                grad_attn_low,
                normed_two_low,
                grad_upward_low,
                activated_low,
                grad_branch,
            )
        )
    joined = [jnp.concatenate([item[index] for item in kept], axis=0) for index in range(8)]
    big = weight_grads(
        joined[0],
        joined[1],
        joined[2],
        joined[3],
        joined[4],
        joined[5],
        joined[6],
        joined[7],
        model_width,
    )
    owned = (
        lax.psum_scatter(big[0].astype(jnp.bfloat16), "dp", scatter_dimension=0, tiled=True).astype(
            jnp.float32
        ),
        lax.psum_scatter(big[1].astype(jnp.bfloat16), "dp", scatter_dimension=0, tiled=True).astype(
            jnp.float32
        ),
        lax.psum_scatter(big[2].astype(jnp.bfloat16), "dp", scatter_dimension=0, tiled=True).astype(
            jnp.float32
        ),
        lax.psum_scatter(big[3].astype(jnp.bfloat16), "dp", scatter_dimension=1, tiled=True).astype(
            jnp.float32
        ),
        lax.psum_scatter(big[4].astype(jnp.bfloat16), "dp", scatter_dimension=0, tiled=True).astype(
            jnp.float32
        ),
        lax.psum_scatter(big[5].astype(jnp.bfloat16), "dp", scatter_dimension=0, tiled=True).astype(
            jnp.float32
        ),
        lax.psum_scatter(big[6].astype(jnp.bfloat16), "dp", scatter_dimension=0, tiled=True).astype(
            jnp.float32
        ),
        lax.psum_scatter(big[7].astype(jnp.bfloat16), "dp", scatter_dimension=0, tiled=True).astype(
            jnp.float32
        ),
        lax.psum_scatter(big[8].astype(jnp.bfloat16), "dp", scatter_dimension=0, tiled=True).astype(
            jnp.float32
        ),
        lax.psum_scatter(
            norm_total[0].astype(jnp.bfloat16), "dp", scatter_dimension=0, tiled=True
        ).astype(jnp.float32),
        lax.psum_scatter(
            norm_total[1].astype(jnp.bfloat16), "dp", scatter_dimension=0, tiled=True
        ).astype(jnp.float32),
        lax.psum_scatter(
            norm_total[2].astype(jnp.bfloat16), "dp", scatter_dimension=0, tiled=True
        ).astype(jnp.float32),
        lax.psum_scatter(
            norm_total[3].astype(jnp.bfloat16), "dp", scatter_dimension=0, tiled=True
        ).astype(jnp.float32),
    )
    owned = (
        lax.psum(owned[0].astype(jnp.bfloat16), "seq").astype(jnp.float32),
        lax.psum(owned[1].astype(jnp.bfloat16), "seq").astype(jnp.float32),
        lax.psum(owned[2].astype(jnp.bfloat16), "seq").astype(jnp.float32),
        lax.psum(owned[3].astype(jnp.bfloat16), "seq").astype(jnp.float32),
        lax.psum(owned[4].astype(jnp.bfloat16), "seq").astype(jnp.float32),
        lax.psum(owned[5].astype(jnp.bfloat16), "seq").astype(jnp.float32),
        lax.psum(owned[6].astype(jnp.bfloat16), "seq").astype(jnp.float32),
        lax.psum(owned[7].astype(jnp.bfloat16), "seq").astype(jnp.float32),
        lax.psum(owned[8].astype(jnp.bfloat16), "seq").astype(jnp.float32),
        lax.psum(owned[9].astype(jnp.bfloat16), "seq").astype(jnp.float32),
        lax.psum(owned[10].astype(jnp.bfloat16), "seq").astype(jnp.float32),
        lax.psum(owned[11].astype(jnp.bfloat16), "seq").astype(jnp.float32),
        lax.psum(owned[12].astype(jnp.bfloat16), "seq").astype(jnp.float32),
    )
    return (
        jnp.concatenate(outputs, axis=0),
        jnp.concatenate(grad_inputs, axis=0),
        owned[0],
        owned[1],
        owned[2],
        owned[3],
        owned[4],
        owned[5],
        owned[6],
        owned[7],
        owned[8],
        owned[9],
        owned[10],
        owned[11],
        owned[12],
    )


F32=jnp.float32; BF16=jnp.bfloat16
NT=(((1,),(1,)),((),())); TN=(((0,),(0,)),((),())); NN=(((1,),(0,)),((),()))
def dg(a,b,dims): return lax.dot_general(a,b,dims,preferred_element_type=F32)

MESH = pl.DeviceIdType.MESH
HBM = pltpu.MemorySpace.HBM


def device_map():
    d, z = lax.axis_index("dp"), lax.axis_index("seq")
    core, x, y = lax.rem(d, 2), lax.rem(d // 2, 2), d // 4
    par = lax.rem(z, 2)
    return dict(
        d=d, z=z, core=core, x=x, y=y, par=par,
        sibling=(d + 1 - 2 * core, z), over_x=(d + 2 - 4 * x, z), over_y=(d + 4 - 8 * y, z),
        near_z=(d, z + 1 - 2 * par), far_z=(d, z + 2 - 4 * (z // 2)),
        across=(d, 3 - z), mid=z * (3 - z) > 0,
        image=[(d - core + z // 2, 2 * core + b) for b in range(2)],
        home=(z // 2) == core,
    )


def remote(src, dst, send, recv, to):
    return pltpu.make_async_remote_copy(
        src_ref=src, dst_ref=dst, send_sem=send, recv_sem=recv, device_id=to, device_id_type=MESH
    )


def greet(place, names, middle=False):
    barrier = pltpu.get_barrier_semaphore()
    if middle:
        @pl.when(place["mid"])
        def _(): pl.semaphore_signal(barrier, inc=1, device_id=place["across"], device_id_type=MESH)
    for name in names:
        pl.semaphore_signal(barrier, inc=1, device_id=place[name], device_id_type=MESH)
    for b in range(2):
        @pl.when(jnp.logical_not(jnp.logical_and(place["home"], place["par"] == b)))
        def _(): pl.semaphore_signal(barrier, inc=1, device_id=place["image"][b], device_id_type=MESH)
    extra = place["mid"].astype(jnp.int32) if middle else 0
    pl.semaphore_wait(barrier, len(names) + 2 - place["home"].astype(jnp.int32) + extra)


class Move:
    def __init__(self, place, sources, target, sems):
        self.place, self.sources, self.target, self.sems = place, sources, target, sems
    def each(self, far, near):
        p = self.place
        for b in range(2):
            stays = jnp.logical_and(p["home"], p["par"] == b)
            target = self.target(p["par"])
            @pl.when(jnp.logical_not(stays))
            def _(): far(remote(self.sources[b], target, self.sems.at[0, b], self.sems.at[1, p["par"]], p["image"][b]))
            @pl.when(stays)
            def _(): near(pltpu.make_async_copy(self.sources[b], target, self.sems.at[2, 0]))
    def start(self):
        self.each(lambda c: c.start(), lambda c: c.start())
    def wait(self):
        p = self.place
        self.each(lambda c: c.wait_send(), lambda c: c.wait())
        for h in range(2):
            @pl.when(jnp.logical_not(jnp.logical_and(p["home"], p["par"] == h)))
            def _(): remote(self.sources[0], self.target(h), self.sems.at[0, 0], self.sems.at[1, h], p["image"][0]).wait_recv()


def tiles(count, body, size=256):
    def step(i, carry):
        body(pl.ds(pl.multiple_of(i * size, size), size))
        return carry
    lax.fori_loop(0, count, step, 0)


def turn(place, source, target):
    for j in range(8):
        jy, jx, jc = j // 4, (j // 2) % 2, j % 2
        differ = lambda a, b: (a + b) - 2 * a * b
        at = differ(place["core"], jc) * 4 + differ(place["y"], jy) * 2 + differ(place["x"], jx)
        target[pl.ds(pl.multiple_of(at * 128, 128), 128), :] = source[:, 128 * j : 128 * j + 128].T


def fwd_kernel(
    tok_hbm, cotg_hbm, wq_s, wo_s, wu_s, wd_s, pack,
    wq_o, wo_o, wu_o, wd_o, x_o, cot_o, cot_t_o, n1_t_o, n2_t_o, att_t_o, qkv_o, kv_o, att_o, act_o, up_o, res_o, out_o,
    lse, vec,
    wq, wo, wu, wd, wdn, pk, xb, cot, n1, n2, qkv, kv, att, act, upb, up_bias, res, cot_t, n1_t, n2_t, att_t,
    ws, wr, wl, ps, pr, ms, kvs, kvr, outs, ups,
):
    p = device_map()
    y, x, core, par = p["y"], p["x"], p["core"], p["par"]
    greet(p, ("sibling", "over_x", "over_y"))

    def rows(py, px):
        return pl.ds(pl.multiple_of(((py * 2 + px) * 2 + core) * 128, 128), 128)

    chunks = [(wq, wq_s, 0, 3072), (wo, wo_s, 0, 1024), (wu, wu_s, 0, 2048), (wu, wu_s, 2048, 2048),
              (wd, None, 0, 2048), (wd, None, 2048, 2048)]
    me, bx, by, diag = rows(y, x), rows(y, 1 - x), rows(1 - y, x), rows(1 - y, 1 - x)

    def copy(n, i):
        w, shard, at, size = chunks[n]
        lo, hi, full = pl.ds(at, size // 2), pl.ds(at + size // 2, size // 2), pl.ds(at, size)
        own = (lambda cols: w.at[me, cols]) if shard is None else (lambda cols: shard.at[:, cols])
        src, dst, to = (
            (own(lo), w.at[me, lo], "over_x"), (own(hi), w.at[me, hi], "over_y"),
            (own(hi), w.at[me, hi], "over_x"), (own(lo), w.at[me, lo], "over_y"),
            (own(full), w.at[me, full], "sibling"),
            (w.at[bx, lo], w.at[bx, lo], "over_y"), (w.at[by, hi], w.at[by, hi], "over_x"),
            (w.at[bx, full], w.at[bx, full], "sibling"), (w.at[by, full], w.at[by, full], "sibling"),
            (w.at[diag, lo], w.at[diag, lo], "sibling"), (w.at[diag, hi], w.at[diag, hi], "sibling"),
        )[i]
        return remote(src, dst, ws.at[n, i], wr.at[n, i], p[to])

    def start(n, *which):
        for i in which: copy(n, i).start()

    def wait(n, *which):
        for i in which: copy(n, i).wait()

    def local(n):
        w, shard, at, size = chunks[n]
        return pltpu.make_async_copy(shard.at[:, pl.ds(at, size)], w.at[me, pl.ds(at, size)], wl.at[n])

    def own(n):
        start(n, 0, 1, 2, 3, 4)
        if chunks[n][1] is not None: local(n).start()

    def mid(n):
        wait(n, 0, 1)
        start(n, 5, 6)
        if n < 5: own(n + 1)

    def late(n):
        wait(n, 2, 3)
        start(n, 7, 8)

    def end(n):
        wait(n, 5, 6)
        start(n, 9, 10)
        wait(n, 4, 7, 8, 9, 10)
        if chunks[n][1] is not None: local(n).wait()

    given, settled = [], []
    def give(src, dst):
        c = pltpu.make_async_copy(src, dst, outs.at[len(given)])
        c.start()
        given.append(c)
        return c

    def settle(c):
        c.wait()
        settled.append(c)

    own(0)
    pk[y, x, core] = pack[...]
    hop1 = remote(pk.at[y, x, core], pk.at[y, x, core], ps.at[0], pr.at[0], p["over_x"])
    hop1.start()
    half = lambda h: pl.ds(pl.multiple_of(h * 256, 256), 256)
    tok = Move(p, [tok_hbm.at[b] for b in range(2)], lambda h: xb.at[half(h)], ms.at[0])
    tok.start()
    cot_move = Move(p, [cotg_hbm.at[b] for b in range(2)], lambda h: cot.at[half(h)], ms.at[1])
    cot_move.start()
    down = pltpu.make_async_copy(wd_s, wdn, wl.at[5])
    down.start()
    hop1.wait()
    hop2 = remote(pk.at[y, :, core], pk.at[y, :, core], ps.at[1], pr.at[1], p["over_y"])
    hop2.start()
    down.wait()
    for j in range(8):
        wd[me, 512 * j : 512 * j + 512] = wdn[512 * j : 512 * j + 512, :].T
    hop2.wait()
    hop3 = remote(pk.at[:, :, core], pk.at[:, :, core], ps.at[2], pr.at[2], p["sibling"])
    hop3.start()
    mid(0)
    hop3.wait()
    for j in range(8):
        block = pk[j // 4, (j // 2) % 2, j % 2]
        for r in range(12):
            if 3 <= r < 7:
                at = 512 * j + 128 * (r - 3)
                up_bias[:, at : at + 128] = block[r : r + 1]
            else:
                to = {0: 4, 1: 5, 2: 6, 7: 7, 8: 8, 9: 9, 10: 10, 11: 11}[r]
                vec[to : to + 1, 128 * j : 128 * j + 128] = block[r : r + 1]
    vec[0:4, :] = jnp.zeros((4, 1024), F32)
    vec[12:16, :] = jnp.zeros((4, 1024), F32)
    tok.wait()

    def stats(value):
        off = value - jnp.mean(value, axis=-1, keepdims=True)
        return off * lax.rsqrt(jnp.mean(off * off, axis=-1, keepdims=True) + norm_eps)

    def norm_one(r):
        n1[r, :] = (stats(xb[r, :].astype(F32)) * vec[8:9, :] + vec[9:10, :]).astype(BF16)
    tiles(8, norm_one, 64)
    x_given = give(xb, x_o)
    late(0)
    turn(p, n1, n1_t)
    give(n1_t, n1_t_o)
    end(0)
    give(wq, wq_o)
    mid(1)

    def project(cols, bias):
        part = dg(n1[...], wq[:, cols], NN)
        qkv[:, cols] = (part if bias is None else part + bias).astype(BF16)
    def key_cols(c): project(pl.ds(pl.multiple_of(1024 + c.start, 256), 256), None)
    tiles(4, key_cols)
    def value_cols(c): project(pl.ds(pl.multiple_of(2048 + c.start, 256), 256), vec[5:6, c])
    tiles(4, value_cols)
    swap = remote(qkv.at[:, pl.ds(1024, 2048)], kv, kvs, kvr, p["sibling"])
    swap.start()
    def query_cols(c): project(c, vec[4:5, c])
    tiles(4, query_cols)
    swap.wait()
    give(qkv, qkv_o)
    give(kv, kv_o)

    lane = lax.broadcasted_iota(jnp.int32, (512, 128), 1)
    def pair(i, carry):
        at = lambda base: pl.ds(pl.multiple_of(base + i * 128, 128), 128)
        q = qkv[:, at(0)] * jnp.asarray(0.125, BF16)
        outs_, ls = [], []
        for h in range(2):
            qh = jnp.where((lane < 64) if h == 0 else (lane >= 64), q, jnp.zeros_like(q))
            sa, sb = dg(qkv[:, at(1024)], qh, NT), dg(kv[:, at(0)], qh, NT)
            m = jnp.maximum(jnp.max(sa, axis=0, keepdims=True), jnp.max(sb, axis=0, keepdims=True))
            pa, pb = jnp.exp(sa - m), jnp.exp(sb - m)
            total = jnp.sum(pa, axis=0, keepdims=True) + jnp.sum(pb, axis=0, keepdims=True)
            o = dg(qkv[:, at(2048)], pa.astype(BF16), TN) + dg(kv[:, at(1024)], pb.astype(BF16), TN)
            outs_.append(o[64 * h : 64 * h + 64] * (1.0 / total))
            ls.append(m + jnp.log(total))
        att[:, at(0)] = jnp.concatenate(outs_, axis=0).T.astype(BF16)
        lse[i] = jnp.concatenate(ls + [jnp.zeros((6, 512), F32)], axis=0)
        @pl.when(i == 2)
        def _():
            late(1)
            end(1)
            mid(2)
        return carry
    lax.fori_loop(0, 8, pair, 0)
    give(wo, wo_o)
    give(att, att_o)
    late(2)
    end(2)
    mid(3)

    def out_cols(c):
        res[:, c] = xb[:, c].astype(F32) + dg(att[...], wo[:, c], NN) + vec[6:7, c]
    tiles(4, out_cols)
    res_given = give(res, res_o)
    def norm_two(r):
        n2[r, :] = (stats(res[r, :]) * vec[10:11, :] + vec[11:12, :]).astype(BF16)
    tiles(8, norm_two, 64)

    def up_copy(i):
        return pltpu.make_async_copy(upb.at[lax.rem(i, 2)], up_o.at[:, pl.ds(pl.multiple_of(i * 512, 512), 512)], ups.at[lax.rem(i, 2)])
    def up_block(i, carry):
        @pl.when(i >= 2)
        def _(): up_copy(i - 2).wait()
        for t in range(2):
            c = pl.ds(pl.multiple_of(i * 512 + 256 * t, 256), 256)
            u = dg(n2[...], wu[:, c], NN) + up_bias[:, c]
            upb[lax.rem(i, 2), :, 256 * t : 256 * t + 256] = u
            act[:, c] = (0.5 * u * (1.0 + jnp.tanh(0.7978845608028654 * (u + 0.044715 * u * u * u)))).astype(BF16)
        up_copy(i).start()
        return carry
    lax.fori_loop(0, 4, up_block, 0)
    turn(p, n2, n2_t)
    give(n2_t, n2_t_o)
    turn(p, att, att_t)
    give(att_t, att_t_o)
    cot_move.wait()
    give(cot, cot_o)
    turn(p, cot, cot_t)
    give(cot_t, cot_t_o)
    late(3)
    end(3)
    give(wu, wu_o)
    mid(4)
    lax.fori_loop(4, 8, up_block, 0)
    give(act, act_o)
    late(4)
    end(4)
    settle(res_given)
    first, second = pl.ds(0, 2048), pl.ds(2048, 2048)
    def half_down(c):
        res[:, c] += dg(act[:, first], wd[c, first], NT)
    tiles(4, half_down)
    mid(5)
    late(5)
    end(5)
    give(wd, wd_o)
    settle(x_given)
    def finish_cols(c):
        xb[:, c] = (res[:, c] + dg(act[:, second], wd[c, second], NT) + vec[7:8, c]).astype(BF16)
    tiles(4, finish_cols)
    give(xb, out_o)
    for c in given:
        if not any(c is s for s in settled): c.wait()
    up_copy(jnp.int32(6)).wait()
    up_copy(jnp.int32(7)).wait()


def forward(tokens, cotangent, shards, pack):
    any_, vmem, hbm = (pl.BlockSpec(memory_space=s) for s in (pl.ANY, pltpu.VMEM, HBM))
    dma = pltpu.SemaphoreType.DMA
    wide = [((1024, 3072), BF16), ((1024, 1024), BF16), ((1024, 4096), BF16), ((1024, 4096), BF16)]
    rows, turned = ((512, 1024), BF16), ((1024, 512), BF16)
    shapes = wide + [rows, rows] + [turned] * 4 + [
        ((512, 3072), BF16), ((512, 2048), BF16), rows, ((512, 4096), BF16), ((512, 4096), F32), ((512, 1024), F32), rows]
    return pl.pallas_call(
        fwd_kernel,
        in_specs=[any_] * 6 + [vmem],
        out_specs=[hbm] * len(shapes) + [vmem, vmem],
        out_shape=[jax.ShapeDtypeStruct(*s) for s in shapes + [((8, 8, 512), F32), ((16, 1024), F32)]],
        scratch_shapes=[pltpu.VMEM(*s) for s in wide + [
            ((4096, 128), BF16), ((2, 2, 2, 12, 128), F32), rows, rows, rows, rows, ((512, 3072), BF16), ((512, 2048), BF16),
            rows, ((512, 4096), BF16), ((2, 512, 512), F32), ((1, 4096), F32), ((512, 1024), F32)] + [turned] * 4]
        + [dma((6, 11)), dma((6, 11)), dma((6,)), dma((3,)), dma((3,)), dma((2, 3, 2)), dma, dma, dma((20,)), dma((2,))],
        compiler_params=pltpu.CompilerParams(collective_id=7, has_side_effects=True, vmem_limit_bytes=67043328),
        cost_estimate=pl.CostEstimate(flops=20 * 10**9, bytes_accessed=60 << 20, transcendentals=10**7),
        name="forward",
    )(tokens, cotangent, *shards, pack)


CHUNKS = 12
SLOTS = 10


def gelu_slope(u):
    inner = 0.7978845608028654 * (u + 0.044715 * u * u * u)
    t = jnp.tanh(inner)
    return 0.5 * (1.0 + t) + 0.5 * u * (1.0 - t * t) * (0.7978845608028654 * (1.0 + 3 * 0.044715 * u * u))


def bwd_kernel(
    cot_hbm, cot_t_hbm, n2_t_hbm, act_hbm, up_hbm, wd_hbm, wu_hbm, wo_hbm, wq_hbm, att_t_hbm, n1_t_hbm,
    qkv_hbm, kv_hbm, att_hbm, out_hbm, res_hbm, x_hbm, lse_ref, vec,
    gd_out, gu_out, go_out, gq_out, result_out, gin_out, small_out,
    sums_ref, sum_in, so, sr, g, h1a, h1b, h2a, h2b, z1, z2, fin, dkv_in, cot, gres, gub, n2_t,
    sib_s, sib_r, hop_s, hop_r, zs, zr, fin_sem, dkv_s, dkv_r, load, ms, ss, sm,
):
    p = device_map()
    x, y, core, par, z = p["x"], p["y"], p["core"], p["par"], p["z"]
    sibling, over_x, over_y, near_z, far_z = (p[n] for n in ("sibling", "over_x", "over_y", "near_z", "far_z"))
    greet(p, ("sibling", "over_x", "over_y", "near_z", "far_z"), True)
    mid, across = p["mid"], p["across"]

    lo, hi = pl.ds(0, 512), pl.ds(512, 512)
    def to_sib(k):
        return remote(so.at[lax.rem(k, 2)], sr.at[lax.rem(k, 2)], sib_s.at[k], sib_r.at[k], sibling)

    def hop(k, j):
        src, dst, to = (
            (g.at[lax.rem(k, SLOTS), 1, :, :, lo], h1a.at[k], over_y),
            (g.at[lax.rem(k, SLOTS), :, 1, :, hi], h1b.at[k], over_x),
            (g.at[lax.rem(k, SLOTS), 0, 1, :, lo], h2a.at[k], over_x),
            (g.at[lax.rem(k, SLOTS), 1, 0, :, hi], h2b.at[k], over_y),
        )[j]
        return remote(src, dst, hop_s.at[k, j], hop_r.at[k, j], to)

    def zhop(k, j, side):
        cols = (lo, hi)[side]
        dst, to = ((z1.at[k, :, cols], near_z), (z2.at[k, :, cols], across), (z2.at[k, :, cols], near_z))[j]
        return remote(g.at[lax.rem(k, SLOTS), 0, 0, :, cols], dst, zs.at[k, 2 * j + side], zr.at[k, 2 * j + side], to)

    def ends(run):
        pl.when(jnp.logical_not(mid))(run)

    def plus(a, b):
        return (a.astype(F32) + b.astype(F32)).astype(BF16)

    def out_copy(k):
        slot = lax.rem(k, 2)
        def with_target(run):
            col = lambda j: pl.ds(pl.multiple_of(j * 1024, 1024), 1024)
            sem = fin_sem.at[slot]
            @pl.when(k < 4)
            def _(): run(pltpu.make_async_copy(fin.at[slot], gd_out.at[:, col(k)], sem))
            @pl.when(jnp.logical_and(k >= 4, k < 8))
            def _(): run(pltpu.make_async_copy(fin.at[slot], gu_out.at[:, col(k - 4)], sem))
            @pl.when(k == 8)
            def _(): run(pltpu.make_async_copy(fin.at[slot], go_out, sem))
            @pl.when(k > 8)
            def _(): run(pltpu.make_async_copy(fin.at[slot], gq_out.at[:, col(k - 9)], sem))
        return with_target

    def tick(n):
        def stage(k, body):
            @pl.when(jnp.logical_and(k >= 0, k < CHUNKS))
            def _(): body(k)

        def c2(k):
            hop(k, 0).wait(); hop(k, 1).wait()
            g[lax.rem(k, SLOTS), 0, :, :, lo] = plus(g[lax.rem(k, SLOTS), 0, :, :, lo], h1a[k])
            g[lax.rem(k, SLOTS), :, 0, :, hi] = plus(g[lax.rem(k, SLOTS), :, 0, :, hi], h1b[k])
            hop(k, 2).start(); hop(k, 3).start()

        sides = ((0, lo), (1, hi))

        def c3(k):
            for side, cols in sides:
                hop(k, 2 + side).wait()
                mine = (lax.rem(k, SLOTS), 0, 0, slice(None), cols)
                g[mine] = plus(g[mine], (h2a, h2b)[side][k])
                ends(lambda: zhop(k, 0, side).start())

        def c4(k):
            @pl.when(mid)
            def _():
                for side, cols in sides:
                    zhop(k, 0, side).wait_recv()
                    mine = (lax.rem(k, SLOTS), 0, 0, slice(None), cols)
                    g[mine] = plus(g[mine], z1[k, :, cols])
                    zhop(k, 1, side).start()

        def c5(k):
            @pl.when(mid)
            def _():
                for side, cols in sides:
                    zhop(k, 1, side).wait()
                    mine = (lax.rem(k, SLOTS), 0, 0, slice(None), cols)
                    g[mine] = plus(g[mine], z2[k, :, cols])
                    zhop(k, 2, side).start()

        def c6(k):
            slot = lax.rem(k, 2)
            @pl.when(k >= 2)
            def _(): out_copy(k - 2)(lambda c: c.wait())
            @pl.when(mid)
            def _():
                fin[slot] = g[lax.rem(k, SLOTS), 0, 0].astype(F32)
                for side in range(2): zhop(k, 2, side).wait_send()
            def other():
                for side, cols in sides:
                    zhop(k, 0, side).wait_send()
                    zhop(k, 2, side).wait_recv()
                    fin[slot, :, cols] = z2[k, :, cols].astype(F32)
            ends(other)
            out_copy(k)(lambda c: c.start())

        stage(n, c2); stage(n - 1, c3); stage(n - 2, c4); stage(n - 3, c5); stage(n - 4, c6)

    def send_odd(k, left, right):
        def one(cols):
            so[lax.rem(k, 2), :, cols] = dg(left[512:1024, :], right[:, cols], NN).astype(BF16)
        tiles(2, one, 512)
        to_sib(k).start()

    def add_even(k, left, right):
        to_sib(k).wait()
        def one(cols):
            part = dg(left[0:512, :], right[:, cols], NN) + sr[lax.rem(k, 2), :, cols].astype(F32)
            g[lax.rem(k, SLOTS), :, :, :, cols] = part.astype(BF16).reshape(2, 2, 128, 512)
        tiles(2, one, 512)
        hop(k, 0).start(); hop(k, 1).start()

    def fetch(src, dst, i):
        return pltpu.make_async_copy(src, dst, load.at[i])

    first = fetch(cot_hbm, cot, 0)
    first.start()
    result = Move(p, [out_hbm.at[pl.ds(256 * h, 256)] for h in range(2)], lambda b: result_out.at[b], ms.at[0])
    result.start()
    sums_ref[...] = jnp.zeros_like(sums_ref)

    def mlp(cot_t, actb, upb, wdb, wub, gn2, resb):
        pieces = [fetch(cot_t_hbm, cot_t, 1), fetch(n2_t_hbm, n2_t, 2), fetch(res_hbm, resb, 3)]
        def part(i, j):
            src, dst = ((act_hbm, actb.at[lax.rem(j, 2)]), (up_hbm, upb), (wd_hbm, wdb), (wu_hbm, wub))[i]
            sem = load.at[4 + i] if i else load.at[8 + lax.rem(j, 2)]
            return pltpu.make_async_copy(src.at[:, pl.ds(pl.multiple_of(j * 1024, 1024), 1024)], dst, sem)
        pieces[0].start()
        for i in range(4): part(i, jnp.int32(0)).start()
        for c in pieces[1:]: c.start()
        gn2[...] = jnp.zeros_like(gn2)
        pieces[0].wait()
        def block(j, carry):
            acts = actb.at[lax.rem(j, 2)]
            def more(*which):
                @pl.when(j < 3)
                def _():
                    for i in which: part(i, j + 1).start()
            part(0, j).wait()
            more(0)
            send_odd(j, cot_t, acts)
            @pl.when(j == 0)
            def _(): first.wait()
            part(1, j).wait()
            part(2, j).wait()
            def slope(cols):
                back = dg(cot[...], wdb[:, cols], NN)
                low = (back * gelu_slope(upb[:, cols])).astype(BF16)
                gub[:, pl.ds(pl.multiple_of(j * 1024 + cols.start, 256), 256)] = low
                sums_ref[pl.ds(j, 1), cols] = jnp.sum(low.astype(F32), axis=0, keepdims=True)
            tiles(4, slope)
            more(1, 2)
            add_even(j, cot_t, acts)
            part(3, j).wait()
            here = pl.ds(pl.multiple_of(j * 1024, 1024), 1024)
            def down(cols):
                gn2[:, cols] += dg(gub[:, here], wub[cols, :], NT)
            tiles(4, down)
            more(3)
            @pl.when(j == 2)
            def _(): tick(jnp.int32(0))
            return carry
        lax.fori_loop(0, 4, block, 0)
        pieces[1].wait()
        pieces[2].wait()
        def rows(r):
            res = resb[r, :]
            centre = jnp.mean(res, axis=-1, keepdims=True)
            off = res - centre
            rstd = lax.rsqrt(jnp.mean(off * off, axis=-1, keepdims=True) + norm_eps)
            xhat = off * rstd
            grad = gn2[r, :]
            e = grad * vec[10:11, :]
            back = rstd * (e - jnp.mean(e, axis=-1, keepdims=True) - xhat * jnp.mean(e * xhat, axis=-1, keepdims=True))
            total = cot[r, :].astype(F32) + back
            gres[r, :] = total
            low = total.astype(BF16).astype(F32)
            add = lambda i, v: sums_ref.__setitem__((slice(i, i + 1), slice(None)), sums_ref[i : i + 1, :] + jnp.sum(v, axis=0, keepdims=True))
            add(4, low); add(5, grad * xhat); add(6, grad); add(7, cot[r, :].astype(F32))
        tiles(8, rows, 64)

    pl.run_scoped(
        mlp, pltpu.VMEM((1024, 512), BF16), pltpu.VMEM((2, 512, 1024), BF16), pltpu.VMEM((512, 1024), F32),
        pltpu.VMEM((1024, 1024), BF16), pltpu.VMEM((1024, 1024), BF16), pltpu.VMEM((512, 1024), F32),
        pltpu.VMEM((512, 1024), F32),
    )

    def rest(dqkv, n1_t, xb):
        late = [fetch(n1_t_hbm, n1_t, 0), fetch(x_hbm, xb, 1)]

        def attention(wo, att_t, ga, kv, att, do):
            loads = [
                fetch(src, dst, 2 + i) for i, (src, dst) in enumerate((
                    (wo_hbm, wo), (qkv_hbm, dqkv), (kv_hbm, kv), (att_hbm, att), (att_t_hbm, att_t),
                ))
            ]
            for c in loads + late: c.start()
            ga[...] = gres[...].astype(BF16)
            tick(jnp.int32(1))
            loads[0].wait()
            def mixed(cols):
                do[:, cols] = dg(ga[...], wo[cols, :], NT).astype(BF16)
            tiles(4, mixed)
            for c in loads[1:4]: c.wait()
            lane = lax.broadcasted_iota(jnp.int32, (512, 128), 1)
            def up_grad(m):
                return gub.at[:, pl.ds(pl.multiple_of(m * 1024, 1024), 1024)]
            def pair(i, carry):
                at = lambda base: pl.ds(pl.multiple_of(base + i * 128, 128), 128)
                cols = at(0)
                qs = dqkv[:, cols] * jnp.asarray(0.125, BF16)
                dos = do[:, cols]
                t = (dos.astype(F32) * att[:, cols].astype(F32)).T
                dq, dk, dv = None, [None, None], [None, None]
                plus_ = lambda a, b: b if a is None else a + b
                sides = ((dqkv, at(1024), at(2048)), (kv, at(0), at(1024)))
                for h in range(2):
                    sel = (lane < 64) if h == 0 else (lane >= 64)
                    qh = jnp.where(sel, qs, jnp.zeros_like(qs))
                    doh = jnp.where(sel, dos, jnp.zeros_like(dos))
                    delta = jnp.sum(t[64 * h : 64 * h + 64], axis=0, keepdims=True)
                    lse = lse_ref[i, h : h + 1, :]
                    for n, (ref, k_at, v_at) in enumerate(sides):
                        kk = ref[:, k_at]
                        s = dg(kk, qh, NT)
                        p_ = jnp.exp(s - lse)
                        dp = dg(ref[:, v_at], doh, NT)
                        ds = (p_ * (dp - delta)).astype(BF16)
                        dv[n] = plus_(dv[n], dg(p_.astype(BF16), doh, NN))
                        dk[n] = plus_(dk[n], dg(ds, qh, NN))
                        dq = plus_(dq, dg(jnp.where(sel, kk, jnp.zeros_like(kk)), ds, TN))
                dqkv[:, cols] = (dq * 0.125).T.astype(BF16)
                for n, (ref, k_at, v_at) in enumerate(sides):
                    ref[:, k_at] = dk[n].astype(BF16)
                    ref[:, v_at] = dv[n].astype(BF16)
                m = i // 2
                @pl.when(lax.rem(i, 2) == 1)
                def _():
                    send_odd(4 + m, n2_t, up_grad(m))
                    tick(2 + m)
                @pl.when(jnp.logical_and(lax.rem(i, 2) == 0, i > 0))
                def _(): add_even(3 + m, n2_t, up_grad(m - 1))
                return carry
            lax.fori_loop(0, 8, pair, 0)
            swap = remote(kv, dkv_in, dkv_s, dkv_r, sibling)
            swap.start()
            add_even(jnp.int32(7), n2_t, up_grad(jnp.int32(3)))
            late[0].wait()
            loads[4].wait()
            send_odd(jnp.int32(8), att_t, ga)
            tick(jnp.int32(6))
            add_even(jnp.int32(8), att_t, ga)
            send_odd(jnp.int32(9), n1_t, dqkv.at[:, pl.ds(0, 1024)])
            swap.wait()

        pl.run_scoped(
            attention, pltpu.VMEM((1024, 1024), BF16), pltpu.VMEM((1024, 512), BF16), pltpu.VMEM((512, 1024), BF16),
            pltpu.VMEM((512, 2048), BF16), pltpu.VMEM((512, 1024), BF16), pltpu.VMEM((512, 1024), BF16),
        )

        def last(wq, gn1):
            def wq_part(i):
                s = lax.rem(i, 2)
                return pltpu.make_async_copy(wq_hbm.at[pl.ds(pl.multiple_of(i * 256, 256), 256), :], wq.at[s], load.at[2 + s])
            wq_part(jnp.int32(0)).start()
            def join(cols):
                there = pl.ds(pl.multiple_of(1024 + cols.start, 256), 256)
                dqkv[:, there] = plus(dqkv[:, there], dkv_in[:, cols])
            tiles(8, join)
            add_even(jnp.int32(9), n1_t, dqkv.at[:, pl.ds(0, 1024)])
            def back(i, carry):
                wq_part(i).wait()
                @pl.when(i < 3)
                def _(): wq_part(i + 1).start()
                gn1[:, pl.ds(pl.multiple_of(i * 256, 256), 256)] = dg(dqkv[...], wq[lax.rem(i, 2)], NT)
                return carry
            lax.fori_loop(0, 4, back, 0)
            late[1].wait()
            def rows(r):
                xx = xb[r, :].astype(F32)
                centre = jnp.mean(xx, axis=-1, keepdims=True)
                off = xx - centre
                rstd = lax.rsqrt(jnp.mean(off * off, axis=-1, keepdims=True) + norm_eps)
                xhat = off * rstd
                grad = gn1[r, :]
                e = grad * vec[8:9, :]
                back = rstd * (e - jnp.mean(e, axis=-1, keepdims=True) - xhat * jnp.mean(e * xhat, axis=-1, keepdims=True))
                xb[r, :] = (gres[r, :] + back).astype(BF16)
                add = lambda i, v: sums_ref.__setitem__((slice(i, i + 1), slice(None)), sums_ref[i : i + 1, :] + jnp.sum(v, axis=0, keepdims=True))
                add(8, grad * xhat); add(9, grad)
                add(10, dqkv[r, 0:1024].astype(F32)); add(11, dqkv[r, 2048:3072].astype(F32))
            tiles(8, rows, 64)
            given = [
                Move(p, [xb.at[pl.ds(256 * h + 64 * i, 64)] for h in range(2)],
                     lambda b, i=i: gin_out.at[b, pl.ds(64 * i, 64)], ms.at[1 + i])
                for i in range(4)
            ]
            steps = [
                remote(sums_ref, sum_in.at[i], ss.at[i], sm.at[i], to)
                for i, to in enumerate((sibling, over_x, over_y, near_z, far_z))
            ]
            steps[0].start()
            tick(jnp.int32(7))
            given[0].start()
            for k in (10, 11):
                right = dqkv.at[:, pl.ds(1024 * (k - 9), 1024)]
                send_odd(jnp.int32(k), n1_t, right)
                if k == 10: tick(jnp.int32(8))
                add_even(jnp.int32(k), n1_t, right)
                if k == 10: given[1].start()
            for i in range(7):
                tick(jnp.int32(9 + i))
                if i < 2: given[2 + i].start()
                if i < 5:
                    steps[i].wait()
                    sums_ref[...] += sum_in[i]
                    if i < 4: steps[i + 1].start()
            d = p["d"]
            mine = pl.ds(pl.multiple_of(d * 128, 128), 128)
            for to, at in ((0, 10), (1, 11), (2, 4), (7, 7), (8, 8), (9, 9), (10, 5), (11, 6)):
                small_out[to : to + 1, :] = sums_ref[at : at + 1, mine]
            for t in range(4):
                lanes = pl.ds(pl.multiple_of(lax.rem(d, 2) * 512 + 128 * t, 128), 128)
                part = sums_ref[0:1, lanes]
                for r in range(1, 4):
                    part = jnp.where(d // 2 == r, sums_ref[r : r + 1, lanes], part)
                small_out[3 + t : 4 + t, :] = part
            for k in (CHUNKS - 2, CHUNKS - 1):
                out_copy(jnp.int32(k))(lambda c: c.wait())
            for move in given: move.wait()
            result.wait()

        pl.run_scoped(last, pltpu.VMEM((2, 256, 3072), BF16), pltpu.VMEM((512, 1024), F32))

    pl.run_scoped(rest, pltpu.VMEM((512, 3072), BF16), pltpu.VMEM((1024, 512), BF16), pltpu.VMEM((512, 1024), BF16))


def backward(arrays, lse, vec):
    any_, vmem, hbm = (pl.BlockSpec(memory_space=s) for s in (pl.ANY, pltpu.VMEM, HBM))
    n = CHUNKS
    dma = pltpu.SemaphoreType.DMA
    return pl.pallas_call(
        bwd_kernel,
        in_specs=[any_] * len(arrays) + [vmem, vmem],
        out_specs=[hbm] * 6 + [vmem],
        out_shape=[jax.ShapeDtypeStruct((128, w), F32) for w in (4096, 4096, 1024, 3072)]
        + [jax.ShapeDtypeStruct((2, 256, 1024), BF16)] * 2 + [jax.ShapeDtypeStruct((12, 128), F32)],
        scratch_shapes=[
            pltpu.VMEM((16, 1024), F32), pltpu.VMEM((5, 16, 1024), F32),
            pltpu.VMEM((2, 512, 1024), BF16), pltpu.VMEM((2, 512, 1024), BF16), pltpu.VMEM((SLOTS, 2, 2, 128, 1024), BF16),
            pltpu.VMEM((n, 2, 128, 512), BF16), pltpu.VMEM((n, 2, 128, 512), BF16),
            pltpu.VMEM((n, 128, 512), BF16), pltpu.VMEM((n, 128, 512), BF16),
            pltpu.VMEM((n, 128, 1024), BF16), pltpu.VMEM((n, 128, 1024), BF16),
            pltpu.VMEM((2, 128, 1024), F32), pltpu.VMEM((512, 2048), BF16), pltpu.VMEM((512, 1024), BF16),
            pltpu.VMEM((512, 1024), F32), pltpu.VMEM((512, 4096), BF16), pltpu.VMEM((1024, 512), BF16),
            dma((n,)), dma((n,)), dma((n, 4)), dma((n, 4)), dma((n, 6)), dma((n, 6)), dma((2,)), dma, dma, dma((12,)),
            dma((5, 3, 2)), dma((5,)), dma((5,)),
        ],
        compiler_params=pltpu.CompilerParams(collective_id=8, has_side_effects=True, vmem_limit_bytes=67043328),
        cost_estimate=pl.CostEstimate(flops=40 * 10**9, bytes_accessed=60 << 20, transcendentals=10**7),
        name="backward",
    )(*arrays, lse, vec)


def local_fast(
    tokens, w_qkv, w_out, w_up, w_down, b_query, b_value, b_out, b_up, b_down,
    ln1_gain, ln1_bias, ln2_gain, ln2_bias, cotangent,
):
    small = (b_query, b_value, b_out, b_up, b_down, ln1_gain, ln1_bias, ln2_gain, ln2_bias)
    pack, at = jnp.zeros((12, 128), F32), 0
    for item in small:
        rows = item.shape[0] // 128
        pack = pack + jnp.pad(item.astype(F32).reshape(rows, 128), ((at, 12 - at - rows), (0, 0)))
        at += rows
    (wq, wo, wu, wd, x, cot, cot_t, n1_t, n2_t, att_t, qkv, kv, att, act, up, res, out, lse, vec) = forward(
        tokens, cotangent, (w_qkv, w_out, w_up, w_down), pack)
    g_down, g_up, g_out, g_qkv, result, grad_input, sums = backward(
        (cot, cot_t, n2_t, act, up, wd, wu, wo, wq, att_t, n1_t, qkv, kv, att, out, res, x), lse, vec)
    outs, at = [], 0
    for item in small:
        rows = item.shape[0] // 128
        outs.append(sums[at : at + rows].reshape(-1))
        at += rows
    return (result, grad_input, g_qkv, g_out, g_up, g_down.T, *outs)


def solution(mesh):
    in_specs = (
        P("dp", "seq", None),
        P("dp", None),
        P("dp", None),
        P("dp", None),
        P(None, "dp"),
        P("dp"),
        P("dp"),
        P("dp"),
        P("dp"),
        P("dp"),
        P("dp"),
        P("dp"),
        P("dp"),
        P("dp"),
        P("dp", "seq", None),
    )
    out_specs = (
        P("dp", "seq", None),
        P("dp", "seq", None),
        P("dp", None),
        P("dp", None),
        P("dp", None),
        P(None, "dp"),
        P("dp"),
        P("dp"),
        P("dp"),
        P("dp"),
        P("dp"),
        P("dp"),
        P("dp"),
        P("dp"),
        P("dp"),
    )
    fn = local_fast if dict(mesh.shape) == {"dp": 8, "seq": 4} else local
    return jax.shard_map(fn, mesh=mesh, in_specs=in_specs, out_specs=out_specs, check_vma=False)
```

```python
import functools

import jax
import jax.numpy as jnp
from jax import lax
from jax.experimental import pallas as pl
from jax.experimental.pallas import tpu as pltpu
from jax.sharding import PartitionSpec as P

H = 16
DH = 64
MICRO = 2
IMG_MB = 1


norm_eps = 1e-06


def normalize(inputs, ln_gain, ln_offset):
    centre = jnp.mean(inputs, axis=-1, keepdims=True)
    spread = jnp.mean(jnp.square(inputs - centre), axis=-1, keepdims=True)
    return (inputs - centre) * lax.rsqrt(spread + norm_eps) * ln_gain + ln_offset


def activate(upward):
    return jax.nn.gelu(upward, approximate=True)


def add_pairs(first_set, second_set):
    return tuple(
        (first_item + second_item for first_item, second_item in zip(first_set, second_set))
    )


def forward_heads(queries, keyed, valued, factor):
    images, length, head_count, head_size = queries.shape
    block_rows = min(512, length)
    blocks = length // block_rows
    query_blocks = queries.reshape(images, blocks, block_rows, head_count, head_size)

    def forward_per_image(element):
        q_image, k_image, v_image = element

        def forward_per_block(q_block):
            scores = (
                jnp.einsum("qhd,khd->hqk", q_block, k_image, preferred_element_type=jnp.float32)
                * factor
            )
            row_max = jnp.max(scores, axis=-1, keepdims=True)
            exponent = jnp.exp(scores - row_max)
            row_total = jnp.sum(exponent, axis=-1, keepdims=True)
            attn_probs = (exponent / row_total).astype(jnp.bfloat16)
            mixture = jnp.einsum(
                "hqk,khd->qhd", attn_probs, v_image, preferred_element_type=jnp.float32
            )
            return (mixture, row_max[..., 0] + jnp.log(row_total[..., 0]))

        return lax.map(forward_per_block, q_image)

    mixture, log_total = lax.map(forward_per_image, (query_blocks, keyed, valued))
    return (mixture.reshape(images, length, head_count * head_size), log_total)


def backward_heads(queries, keyed, valued, grad_mixed, log_total, factor):
    images, length, head_count, head_size = queries.shape
    block_rows = min(512, length)
    blocks = length // block_rows
    query_blocks = queries.reshape(images, blocks, block_rows, head_count, head_size)
    grad_blocks = grad_mixed.reshape(images, blocks, block_rows, head_count, head_size)

    def backward_per_image(element):
        q_image, k_image, v_image, g_image, l_image = element

        def backward_per_block(running, pieces):
            grad_key, grad_value = running
            q_block, g_block, l_block = pieces
            scores = (
                jnp.einsum("qhd,khd->hqk", q_block, k_image, preferred_element_type=jnp.float32)
                * factor
            )
            full_probs = jnp.exp(scores - l_block[..., None])
            grad_probs = jnp.einsum(
                "qhd,khd->hqk", g_block, v_image, preferred_element_type=jnp.float32
            )
            row_inner = jnp.sum(full_probs * grad_probs, axis=-1, keepdims=True)
            grad_scores = (full_probs * (grad_probs - row_inner)).astype(jnp.bfloat16)
            grad_query = (
                jnp.einsum("hqk,khd->qhd", grad_scores, k_image, preferred_element_type=jnp.float32)
                * factor
            )
            grad_key = (
                grad_key
                + jnp.einsum(
                    "hqk,qhd->khd", grad_scores, q_block, preferred_element_type=jnp.float32
                )
                * factor
            )
            grad_value = grad_value + jnp.einsum(
                "hqk,qhd->khd",
                full_probs.astype(jnp.bfloat16),
                g_block,
                preferred_element_type=jnp.float32,
            )
            return ((grad_key, grad_value), grad_query)

        empty_sum = jnp.zeros((length, head_count, head_size), jnp.float32)
        (grad_key, grad_value), grad_query = lax.scan(
            backward_per_block, (empty_sum, empty_sum), (q_image, g_image, l_image)
        )
        return (grad_query.reshape(length, head_count, head_size), grad_key, grad_value)

    return lax.map(backward_per_image, (query_blocks, keyed, valued, grad_blocks, log_total))


def weight_grads(
    normed_one_low,
    grad_projected,
    mixed_tokens,
    grad_attn_low,
    normed_two_low,
    grad_upward_low,
    activated_low,
    grad_branch,
    model_width,
):
    grad_qkv = jnp.einsum(
        "ptd,pte->de", normed_one_low, grad_projected, preferred_element_type=jnp.float32
    )
    grad_bquery = jnp.sum(grad_projected[:, :, :model_width], axis=(0, 1), dtype=jnp.float32)
    grad_bvalue = jnp.sum(grad_projected[:, :, 2 * model_width :], axis=(0, 1), dtype=jnp.float32)
    grad_wout = jnp.einsum(
        "pte,ptd->ed", mixed_tokens, grad_attn_low, preferred_element_type=jnp.float32
    )
    grad_bout = jnp.sum(grad_attn_low, axis=(0, 1), dtype=jnp.float32)
    grad_up = jnp.einsum(
        "ptd,ptf->df", normed_two_low, grad_upward_low, preferred_element_type=jnp.float32
    )
    grad_bup = jnp.sum(grad_upward_low, axis=(0, 1), dtype=jnp.float32)
    grad_down = jnp.einsum(
        "ptf,ptd->fd", activated_low, grad_branch, preferred_element_type=jnp.float32
    )
    grad_bdown = jnp.sum(grad_branch, axis=(0, 1), dtype=jnp.float32)
    return (
        grad_qkv,
        grad_wout,
        grad_up,
        grad_down,
        grad_bquery,
        grad_bvalue,
        grad_bout,
        grad_bup,
        grad_bdown,
    )


def local(
    tokens,
    w_qkv,
    w_out,
    w_up,
    w_down,
    b_query,
    b_value,
    b_out,
    b_up,
    b_down,
    ln1_gain,
    ln1_bias,
    ln2_gain,
    ln2_bias,
    cotangent,
):
    seq_count = lax.axis_size("seq")
    local_patches = tokens.shape[1]
    model_width = tokens.shape[2]
    patches = local_patches * seq_count
    head_local = H // seq_count
    factor = DH ** (-0.5)
    gathered = (
        lax.all_gather(w_qkv, "dp", axis=0, tiled=True),
        lax.all_gather(w_out, "dp", axis=0, tiled=True),
        lax.all_gather(w_up, "dp", axis=0, tiled=True),
        lax.all_gather(w_down, "dp", axis=1, tiled=True),
        lax.all_gather(b_query, "dp", axis=0, tiled=True),
        lax.all_gather(b_value, "dp", axis=0, tiled=True),
        lax.all_gather(b_out, "dp", axis=0, tiled=True),
        lax.all_gather(b_up, "dp", axis=0, tiled=True),
        lax.all_gather(b_down, "dp", axis=0, tiled=True),
        lax.all_gather(ln1_gain, "dp", axis=0, tiled=True),
        lax.all_gather(ln1_bias, "dp", axis=0, tiled=True),
        lax.all_gather(ln2_gain, "dp", axis=0, tiled=True),
        lax.all_gather(ln2_bias, "dp", axis=0, tiled=True),
    )
    outputs = []
    grad_inputs = []
    kept = []
    for micro_idx in range(MICRO):
        w_qkv_full, w_out_full, w_up_full, w_down_full = (
            gathered[0],
            gathered[1],
            gathered[2],
            gathered[3],
        )
        vectors = [piece.astype(jnp.float32) for piece in gathered[4:]]
        (
            bias_query,
            bias_value,
            bias_out,
            bias_up,
            bias_down,
            gain_one,
            offset_one,
            gain_two,
            offset_two,
        ) = vectors
        start = micro_idx * IMG_MB
        inputs = tokens[start : start + IMG_MB].astype(jnp.float32)
        normed_one, norm_one_back = jax.vjp(normalize, inputs, gain_one, offset_one)
        normed_one_low = normed_one.astype(jnp.bfloat16)
        qkv_bias = jnp.concatenate([bias_query, jnp.zeros_like(bias_query), bias_value])
        projected = (
            jnp.einsum(
                "ptd,de->pte", normed_one_low, w_qkv_full, preferred_element_type=jnp.float32
            )
            + qkv_bias
        )
        projected_low = projected.astype(jnp.bfloat16).reshape(
            IMG_MB, local_patches, 3, model_width
        )
        by_heads = lax.all_to_all(projected_low, "seq", split_axis=3, concat_axis=1, tiled=True)
        queries = by_heads[:, :, 0].reshape(IMG_MB, patches, head_local, DH)
        keyed = by_heads[:, :, 1].reshape(IMG_MB, patches, head_local, DH)
        valued = by_heads[:, :, 2].reshape(IMG_MB, patches, head_local, DH)
        attended, log_total = forward_heads(queries, keyed, valued, factor)
        attended_low = attended.astype(jnp.bfloat16)
        mixed_tokens = lax.all_to_all(attended_low, "seq", split_axis=1, concat_axis=2, tiled=True)
        residual = (
            inputs
            + jnp.einsum(
                "pte,ed->ptd", mixed_tokens, w_out_full, preferred_element_type=jnp.float32
            )
            + bias_out
        )
        normed_two, norm_two_back = jax.vjp(normalize, residual, gain_two, offset_two)
        normed_two_low = normed_two.astype(jnp.bfloat16)
        upward = (
            jnp.einsum("ptd,df->ptf", normed_two_low, w_up_full, preferred_element_type=jnp.float32)
            + bias_up
        )
        activated, activate_back = jax.vjp(activate, upward)
        activated_low = activated.astype(jnp.bfloat16)
        layer_out = (
            residual
            + jnp.einsum(
                "ptf,fd->ptd", activated_low, w_down_full, preferred_element_type=jnp.float32
            )
            + bias_down
        )
        outputs.append(layer_out.astype(jnp.bfloat16))
        grad_result = cotangent[start : start + IMG_MB].astype(jnp.float32)
        grad_branch = grad_result.astype(jnp.bfloat16)
        grad_active = jnp.einsum(
            "ptd,fd->ptf", grad_branch, w_down_full, preferred_element_type=jnp.float32
        )
        (grad_upward,) = activate_back(grad_active)
        grad_upward_low = grad_upward.astype(jnp.bfloat16)
        grad_normed_two = jnp.einsum(
            "ptf,df->ptd", grad_upward_low, w_up_full, preferred_element_type=jnp.float32
        )
        grad_from_two, grad_gain2, grad_bias2 = norm_two_back(grad_normed_two)
        grad_residual = grad_result + grad_from_two
        grad_attn_low = grad_residual.astype(jnp.bfloat16)
        grad_mixed = jnp.einsum(
            "ptd,ed->pte", grad_attn_low, w_out_full, preferred_element_type=jnp.float32
        ).astype(jnp.bfloat16)
        grad_heads = lax.all_to_all(grad_mixed, "seq", split_axis=2, concat_axis=1, tiled=True)
        grad_query, grad_key, grad_value = backward_heads(
            queries,
            keyed,
            valued,
            grad_heads.reshape(IMG_MB, patches, head_local, DH),
            log_total,
            factor,
        )
        stacked = (
            jnp.stack([grad_query, grad_key, grad_value], axis=2)
            .reshape(IMG_MB, patches, 3, head_local * DH)
            .astype(jnp.bfloat16)
        )
        grad_parts = lax.all_to_all(stacked, "seq", split_axis=1, concat_axis=3, tiled=True)
        grad_projected = grad_parts.reshape(IMG_MB, local_patches, 3 * model_width)
        grad_normed_one = jnp.einsum(
            "pte,de->ptd", grad_projected, w_qkv_full, preferred_element_type=jnp.float32
        )
        grad_from_one, grad_gain1, grad_bias1 = norm_one_back(grad_normed_one)
        grad_inputs.append((grad_residual + grad_from_one).astype(jnp.bfloat16))
        norm_grads = (grad_gain1, grad_bias1, grad_gain2, grad_bias2)
        norm_total = norm_grads if micro_idx == 0 else add_pairs(norm_total, norm_grads)
        kept.append(
            (
                normed_one_low,
                grad_projected,
                mixed_tokens,
                grad_attn_low,
                normed_two_low,
                grad_upward_low,
                activated_low,
                grad_branch,
            )
        )
    joined = [jnp.concatenate([item[index] for item in kept], axis=0) for index in range(8)]
    big = weight_grads(
        joined[0],
        joined[1],
        joined[2],
        joined[3],
        joined[4],
        joined[5],
        joined[6],
        joined[7],
        model_width,
    )
    owned = (
        lax.psum_scatter(big[0].astype(jnp.bfloat16), "dp", scatter_dimension=0, tiled=True).astype(
            jnp.float32
        ),
        lax.psum_scatter(big[1].astype(jnp.bfloat16), "dp", scatter_dimension=0, tiled=True).astype(
            jnp.float32
        ),
        lax.psum_scatter(big[2].astype(jnp.bfloat16), "dp", scatter_dimension=0, tiled=True).astype(
            jnp.float32
        ),
        lax.psum_scatter(big[3].astype(jnp.bfloat16), "dp", scatter_dimension=1, tiled=True).astype(
            jnp.float32
        ),
        lax.psum_scatter(big[4].astype(jnp.bfloat16), "dp", scatter_dimension=0, tiled=True).astype(
            jnp.float32
        ),
        lax.psum_scatter(big[5].astype(jnp.bfloat16), "dp", scatter_dimension=0, tiled=True).astype(
            jnp.float32
        ),
        lax.psum_scatter(big[6].astype(jnp.bfloat16), "dp", scatter_dimension=0, tiled=True).astype(
            jnp.float32
        ),
        lax.psum_scatter(big[7].astype(jnp.bfloat16), "dp", scatter_dimension=0, tiled=True).astype(
            jnp.float32
        ),
        lax.psum_scatter(big[8].astype(jnp.bfloat16), "dp", scatter_dimension=0, tiled=True).astype(
            jnp.float32
        ),
        lax.psum_scatter(
            norm_total[0].astype(jnp.bfloat16), "dp", scatter_dimension=0, tiled=True
        ).astype(jnp.float32),
        lax.psum_scatter(
            norm_total[1].astype(jnp.bfloat16), "dp", scatter_dimension=0, tiled=True
        ).astype(jnp.float32),
        lax.psum_scatter(
            norm_total[2].astype(jnp.bfloat16), "dp", scatter_dimension=0, tiled=True
        ).astype(jnp.float32),
        lax.psum_scatter(
            norm_total[3].astype(jnp.bfloat16), "dp", scatter_dimension=0, tiled=True
        ).astype(jnp.float32),
    )
    owned = (
        lax.psum(owned[0].astype(jnp.bfloat16), "seq").astype(jnp.float32),
        lax.psum(owned[1].astype(jnp.bfloat16), "seq").astype(jnp.float32),
        lax.psum(owned[2].astype(jnp.bfloat16), "seq").astype(jnp.float32),
        lax.psum(owned[3].astype(jnp.bfloat16), "seq").astype(jnp.float32),
        lax.psum(owned[4].astype(jnp.bfloat16), "seq").astype(jnp.float32),
        lax.psum(owned[5].astype(jnp.bfloat16), "seq").astype(jnp.float32),
        lax.psum(owned[6].astype(jnp.bfloat16), "seq").astype(jnp.float32),
        lax.psum(owned[7].astype(jnp.bfloat16), "seq").astype(jnp.float32),
        lax.psum(owned[8].astype(jnp.bfloat16), "seq").astype(jnp.float32),
        lax.psum(owned[9].astype(jnp.bfloat16), "seq").astype(jnp.float32),
        lax.psum(owned[10].astype(jnp.bfloat16), "seq").astype(jnp.float32),
        lax.psum(owned[11].astype(jnp.bfloat16), "seq").astype(jnp.float32),
        lax.psum(owned[12].astype(jnp.bfloat16), "seq").astype(jnp.float32),
    )
    return (
        jnp.concatenate(outputs, axis=0),
        jnp.concatenate(grad_inputs, axis=0),
        owned[0],
        owned[1],
        owned[2],
        owned[3],
        owned[4],
        owned[5],
        owned[6],
        owned[7],
        owned[8],
        owned[9],
        owned[10],
        owned[11],
        owned[12],
    )


F32=jnp.float32; BF16=jnp.bfloat16
NT=(((1,),(1,)),((),())); TN=(((0,),(0,)),((),())); NN=(((1,),(0,)),((),()))
def dg(a,b,dims): return lax.dot_general(a,b,dims,preferred_element_type=F32)

MESH = pl.DeviceIdType.MESH
HBM = pltpu.MemorySpace.HBM


def device_map():
    d, z = lax.axis_index("dp"), lax.axis_index("seq")
    core, x, y = lax.rem(d, 2), lax.rem(d // 2, 2), d // 4
    par = lax.rem(z, 2)
    return dict(
        d=d, z=z, core=core, x=x, y=y, par=par,
        sibling=(d + 1 - 2 * core, z), over_x=(d + 2 - 4 * x, z), over_y=(d + 4 - 8 * y, z),
        near_z=(d, z + 1 - 2 * par), far_z=(d, z + 2 - 4 * (z // 2)),
        across=(d, 3 - z), mid=z * (3 - z) > 0,
        image=[(d - core + z // 2, 2 * core + b) for b in range(2)],
        home=(z // 2) == core,
    )


def remote(src, dst, send, recv, to):
    return pltpu.make_async_remote_copy(
        src_ref=src, dst_ref=dst, send_sem=send, recv_sem=recv, device_id=to, device_id_type=MESH
    )


def greet(place, names, middle=False):
    barrier = pltpu.get_barrier_semaphore()
    if middle:
        @pl.when(place["mid"])
        def _(): pl.semaphore_signal(barrier, inc=1, device_id=place["across"], device_id_type=MESH)
    for name in names:
        pl.semaphore_signal(barrier, inc=1, device_id=place[name], device_id_type=MESH)
    for b in range(2):
        @pl.when(jnp.logical_not(jnp.logical_and(place["home"], place["par"] == b)))
        def _(): pl.semaphore_signal(barrier, inc=1, device_id=place["image"][b], device_id_type=MESH)
    extra = place["mid"].astype(jnp.int32) if middle else 0
    pl.semaphore_wait(barrier, len(names) + 2 - place["home"].astype(jnp.int32) + extra)


class Move:
    def __init__(self, place, sources, target, sems):
        self.place, self.sources, self.target, self.sems = place, sources, target, sems
    def each(self, far, near):
        p = self.place
        for b in range(2):
            stays = jnp.logical_and(p["home"], p["par"] == b)
            target = self.target(p["par"])
            @pl.when(jnp.logical_not(stays))
            def _(): far(remote(self.sources[b], target, self.sems.at[0, b], self.sems.at[1, p["par"]], p["image"][b]))
            @pl.when(stays)
            def _(): near(pltpu.make_async_copy(self.sources[b], target, self.sems.at[2, 0]))
    def start(self):
        self.each(lambda c: c.start(), lambda c: c.start())
    def wait(self):
        p = self.place
        self.each(lambda c: c.wait_send(), lambda c: c.wait())
        for h in range(2):
            @pl.when(jnp.logical_not(jnp.logical_and(p["home"], p["par"] == h)))
            def _(): remote(self.sources[0], self.target(h), self.sems.at[0, 0], self.sems.at[1, h], p["image"][0]).wait_recv()


def tiles(count, body, size=256):
    def step(i, carry):
        body(pl.ds(pl.multiple_of(i * size, size), size))
        return carry
    lax.fori_loop(0, count, step, 0)


def turn(place, source, target):
    for j in range(8):
        jy, jx, jc = j // 4, (j // 2) % 2, j % 2
        differ = lambda a, b: (a + b) - 2 * a * b
        at = differ(place["core"], jc) * 4 + differ(place["y"], jy) * 2 + differ(place["x"], jx)
        target[pl.ds(pl.multiple_of(at * 128, 128), 128), :] = source[:, 128 * j : 128 * j + 128].T


def fwd_kernel(
    tok_hbm, cotg_hbm, wq_s, wo_s, wu_s, wd_s, pack,
    wq_o, wo_o, wu_o, wd_o, x_o, cot_o, n1_t_o, n2_t_o, att_t_o, qkv_o, kv_o, att_o, up_o, res_o, out_o, gd_o,
    lse, vec,
    wq, wo, wu, wd, wdn, pk, xb, cot, n1, n2, qkv, kv, att, act, upb, up_bias, res, cot_t, n1_t, n2_t, att_t, so, sr, gs,
    sib_s, sib_r, ws, wr, wl, ps, pr, ms, kvs, kvr, outs, ups,
):
    p = device_map()
    y, x, core, par = p["y"], p["x"], p["core"], p["par"]
    greet(p, ("sibling", "over_x", "over_y", "near_z"))

    def rows(py, px):
        return pl.ds(pl.multiple_of(((py * 2 + px) * 2 + core) * 128, 128), 128)

    chunks = [(wq, wq_s, 0, 3072), (wo, wo_s, 0, 1024), (wu, wu_s, 0, 2048), (wu, wu_s, 2048, 2048),
              (wd, None, 0, 2048), (wd, None, 2048, 2048)]
    me, bx, by, diag = rows(y, x), rows(y, 1 - x), rows(1 - y, x), rows(1 - y, 1 - x)

    shared = (2, 3)

    def copy(n, i):
        w, shard, at, size = chunks[n]
        full = part = pl.ds(at, size)
        lo, hi = pl.ds(at, size // 2), pl.ds(at + size // 2, size // 2)
        rest = None
        if n in shared:
            start_at = lambda by: pl.multiple_of(at + by, 512)
            part, rest = pl.ds(start_at(par * 1024), 1024), pl.ds(start_at((1 - par) * 1024), 1024)
            lo, hi = pl.ds(start_at(par * 1024), 512), pl.ds(start_at(par * 1024 + 512), 512)
        own = (lambda cols: w.at[me, cols]) if shard is None else (lambda cols: shard.at[:, cols])
        src, dst, to = (
            (own(lo), w.at[me, lo], "over_x"), (own(hi), w.at[me, hi], "over_y"),
            (own(hi), w.at[me, hi], "over_x"), (own(lo), w.at[me, lo], "over_y"),
            (own(full), w.at[me, full], "sibling"),
            (w.at[bx, lo], w.at[bx, lo], "over_y"), (w.at[by, hi], w.at[by, hi], "over_x"),
            (w.at[bx, part], w.at[bx, part], "sibling"), (w.at[by, part], w.at[by, part], "sibling"),
            (w.at[diag, lo], w.at[diag, lo], "sibling"), (w.at[diag, hi], w.at[diag, hi], "sibling"),
        )[i] if i < 11 else (
            (w.at[bx, part], w.at[bx, part], "near_z"), (w.at[by, part], w.at[by, part], "near_z"),
            (w.at[diag, part], w.at[diag, part], "near_z"),
            (w.at[bx, rest], w.at[bx, rest], "sibling"), (w.at[by, rest], w.at[by, rest], "sibling"),
            (w.at[diag, rest], w.at[diag, rest], "sibling"),
        )[i - 11]
        return remote(src, dst, ws.at[n, i], wr.at[n, i], p[to])

    def start(n, *which):
        for i in which: copy(n, i).start()

    def wait(n, *which):
        for i in which: copy(n, i).wait()

    def local(n):
        w, shard, at, size = chunks[n]
        return pltpu.make_async_copy(shard.at[:, pl.ds(at, size)], w.at[me, pl.ds(at, size)], wl.at[n])

    def own(n):
        start(n, 0, 1, 2, 3, 4)
        if chunks[n][1] is not None: local(n).start()

    def mid(n):
        wait(n, 0, 1)
        start(n, 5, 6)
        if n < 5: own(n + 1)

    def late(n):
        wait(n, 2, 3)
        start(n, 7, 8)
        if n in shared: start(n, 11, 12)

    def end(n):
        wait(n, 5, 6)
        start(n, 9, 10)
        if n in shared: start(n, 13)
        else: settle_chunk(n)

    def settle_chunk(n):
        if n in shared:
            wait(n, 11, 12, 13)
            start(n, 14, 15, 16)
            wait(n, 14, 15, 16)
        wait(n, 4, 7, 8, 9, 10)
        if chunks[n][1] is not None: local(n).wait()

    given, settled = [], []
    def give(src, dst):
        c = pltpu.make_async_copy(src, dst, outs.at[len(given)])
        c.start()
        given.append(c)
        return c

    def settle(c):
        c.wait()
        settled.append(c)

    own(0)
    pk[y, x, core] = pack[...]
    hop1 = remote(pk.at[y, x, core], pk.at[y, x, core], ps.at[0], pr.at[0], p["over_x"])
    hop1.start()
    half = lambda h: pl.ds(pl.multiple_of(h * 256, 256), 256)
    tok = Move(p, [tok_hbm.at[b] for b in range(2)], lambda h: xb.at[half(h)], ms.at[0])
    tok.start()
    cot_move = Move(p, [cotg_hbm.at[b] for b in range(2)], lambda h: cot.at[half(h)], ms.at[1])
    cot_move.start()
    down = pltpu.make_async_copy(wd_s, wdn, wl.at[5])
    down.start()
    hop1.wait()
    hop2 = remote(pk.at[y, :, core], pk.at[y, :, core], ps.at[1], pr.at[1], p["over_y"])
    hop2.start()
    down.wait()
    for j in range(8):
        wd[me, 512 * j : 512 * j + 512] = wdn[512 * j : 512 * j + 512, :].T
    hop2.wait()
    hop3 = remote(pk.at[:, :, core], pk.at[:, :, core], ps.at[2], pr.at[2], p["sibling"])
    hop3.start()
    mid(0)
    hop3.wait()
    for j in range(8):
        block = pk[j // 4, (j // 2) % 2, j % 2]
        for r in range(12):
            if 3 <= r < 7:
                at = 512 * j + 128 * (r - 3)
                up_bias[:, at : at + 128] = block[r : r + 1]
            else:
                to = {0: 4, 1: 5, 2: 6, 7: 7, 8: 8, 9: 9, 10: 10, 11: 11}[r]
                vec[to : to + 1, 128 * j : 128 * j + 128] = block[r : r + 1]
    vec[0:4, :] = jnp.zeros((4, 1024), F32)
    vec[12:16, :] = jnp.zeros((4, 1024), F32)
    tok.wait()

    def stats(value):
        off = value - jnp.mean(value, axis=-1, keepdims=True)
        return off * lax.rsqrt(jnp.mean(off * off, axis=-1, keepdims=True) + norm_eps)

    def norm_one(r):
        n1[r, :] = (stats(xb[r, :].astype(F32)) * vec[8:9, :] + vec[9:10, :]).astype(BF16)
    tiles(8, norm_one, 64)
    x_given = give(xb, x_o)
    late(0)
    turn(p, n1, n1_t)
    give(n1_t, n1_t_o)
    end(0)
    give(wq, wq_o)
    mid(1)

    def project(cols, bias):
        part = dg(n1[...], wq[:, cols], NN)
        qkv[:, cols] = (part if bias is None else part + bias).astype(BF16)
    def key_cols(c): project(pl.ds(pl.multiple_of(1024 + c.start, 256), 256), None)
    tiles(4, key_cols)
    def value_cols(c): project(pl.ds(pl.multiple_of(2048 + c.start, 256), 256), vec[5:6, c])
    tiles(4, value_cols)
    swap = remote(qkv.at[:, pl.ds(1024, 2048)], kv, kvs, kvr, p["sibling"])
    swap.start()
    def query_cols(c): project(c, vec[4:5, c])
    tiles(4, query_cols)
    swap.wait()
    give(qkv, qkv_o)
    give(kv, kv_o)

    lane = lax.broadcasted_iota(jnp.int32, (512, 128), 1)
    def pair(i, carry):
        at = lambda base: pl.ds(pl.multiple_of(base + i * 128, 128), 128)
        q = qkv[:, at(0)] * jnp.asarray(0.125, BF16)
        outs_, ls = [], []
        for h in range(2):
            qh = jnp.where((lane < 64) if h == 0 else (lane >= 64), q, jnp.zeros_like(q))
            sa, sb = dg(qkv[:, at(1024)], qh, NT), dg(kv[:, at(0)], qh, NT)
            m = jnp.maximum(jnp.max(sa, axis=0, keepdims=True), jnp.max(sb, axis=0, keepdims=True))
            pa, pb = jnp.exp(sa - m), jnp.exp(sb - m)
            total = jnp.sum(pa, axis=0, keepdims=True) + jnp.sum(pb, axis=0, keepdims=True)
            o = dg(qkv[:, at(2048)], pa.astype(BF16), TN) + dg(kv[:, at(1024)], pb.astype(BF16), TN)
            outs_.append(o[64 * h : 64 * h + 64] * (1.0 / total))
            ls.append(m + jnp.log(total))
        att[:, at(0)] = jnp.concatenate(outs_, axis=0).T.astype(BF16)
        lse[i] = jnp.concatenate(ls + [jnp.zeros((6, 512), F32)], axis=0)
        @pl.when(i == 1)
        def _():
            late(1)
            end(1)
            late(2)
        @pl.when(i == 3)
        def _():
            end(2)
            mid(3)
        @pl.when(i == 6)
        def _():
            late(3)
            end(3)
        return carry
    mid(2)
    lax.fori_loop(0, 8, pair, 0)
    mid(4)
    give(wo, wo_o)
    give(att, att_o)
    def out_cols(c):
        res[:, c] = xb[:, c].astype(F32) + dg(att[...], wo[:, c], NN) + vec[6:7, c]
    tiles(4, out_cols)
    res_given = give(res, res_o)
    def norm_two(r):
        n2[r, :] = (stats(res[r, :]) * vec[10:11, :] + vec[11:12, :]).astype(BF16)
    tiles(8, norm_two, 64)

    def up_copy(i):
        return pltpu.make_async_copy(upb.at[lax.rem(i, 2)], up_o.at[:, pl.ds(pl.multiple_of(i * 512, 512), 512)], ups.at[lax.rem(i, 2)])
    def up_block(i, carry):
        @pl.when(i >= 2)
        def _(): up_copy(i - 2).wait()
        for t in range(2):
            c = pl.ds(pl.multiple_of(i * 512 + 256 * t, 256), 256)
            u = dg(n2[...], wu[:, c], NN) + up_bias[:, c]
            upb[lax.rem(i, 2), :, 256 * t : 256 * t + 256] = u
            act[:, c] = (0.5 * u * (1.0 + jnp.tanh(0.7978845608028654 * (u + 0.044715 * u * u * u)))).astype(BF16)
        up_copy(i).start()
        return carry
    def to_sib(k):
        return remote(so.at[k % 2], sr.at[k % 2], sib_s.at[k], sib_r.at[k], p["sibling"])

    def down_odd(k):
        def one(cols):
            so[k % 2, :, cols] = dg(cot_t[512:1024, :], act[:, pl.ds(pl.multiple_of(1024 * k + cols.start, 512), 512)], NN).astype(BF16)
        tiles(2, one, 512)
        to_sib(k).start()

    def down_even(k):
        to_sib(k).wait()
        def one(cols):
            part = dg(cot_t[0:512, :], act[:, pl.ds(pl.multiple_of(1024 * k + cols.start, 512), 512)], NN)
            gs[k, :, :, :, cols] = (part + sr[k % 2, :, cols].astype(F32)).astype(BF16).reshape(2, 2, 128, 512)
        tiles(2, one, 512)
        give(gs.at[k], gd_o.at[k])

    turn(p, n2, n2_t)
    give(n2_t, n2_t_o)
    settle_chunk(2)
    lax.fori_loop(0, 4, up_block, 0)
    cot_move.wait()
    turn(p, cot, cot_t)
    give(cot, cot_o)
    late(4)
    down_odd(0)
    end(4)
    down_even(0)
    down_odd(1)
    settle(res_given)
    first, second = pl.ds(0, 2048), pl.ds(2048, 2048)
    def half_down(c):
        res[:, c] += dg(act[:, first], wd[c, first], NT)
    tiles(4, half_down)
    mid(5)
    down_even(1)
    turn(p, att, att_t)
    give(att_t, att_t_o)
    settle_chunk(3)
    give(wu, wu_o)
    lax.fori_loop(4, 8, up_block, 0)
    late(5)
    down_odd(2)
    end(5)
    give(wd, wd_o)
    settle(x_given)
    down_even(2)
    down_odd(3)
    def finish_cols(c):
        xb[:, c] = (res[:, c] + dg(act[:, second], wd[c, second], NT) + vec[7:8, c]).astype(BF16)
    tiles(4, finish_cols)
    give(xb, out_o)
    down_even(3)
    for c in given:
        if not any(c is s for s in settled): c.wait()
    up_copy(jnp.int32(6)).wait()
    up_copy(jnp.int32(7)).wait()


def forward(tokens, cotangent, shards, pack):
    any_, vmem, hbm = (pl.BlockSpec(memory_space=s) for s in (pl.ANY, pltpu.VMEM, HBM))
    dma = pltpu.SemaphoreType.DMA
    wide = [((1024, 3072), BF16), ((1024, 1024), BF16), ((1024, 4096), BF16), ((1024, 4096), BF16)]
    rows, turned = ((512, 1024), BF16), ((1024, 512), BF16)
    shapes = wide + [rows, rows] + [turned] * 3 + [
        ((512, 3072), BF16), ((512, 2048), BF16), rows, ((512, 4096), F32), ((512, 1024), F32), rows, ((4, 2, 2, 128, 1024), BF16)]
    return pl.pallas_call(
        fwd_kernel,
        in_specs=[any_] * 6 + [vmem],
        out_specs=[hbm] * len(shapes) + [vmem, vmem],
        out_shape=[jax.ShapeDtypeStruct(*s) for s in shapes + [((8, 8, 512), F32), ((16, 1024), F32)]],
        scratch_shapes=[pltpu.VMEM(*s) for s in wide + [
            ((4096, 128), BF16), ((2, 2, 2, 12, 128), F32), rows, rows, rows, rows, ((512, 3072), BF16), ((512, 2048), BF16),
            rows, ((512, 4096), BF16), ((2, 512, 512), F32), ((1, 4096), F32), ((512, 1024), F32)] + [turned] * 4 + [
            ((2, 512, 1024), BF16), ((2, 512, 1024), BF16), ((4, 2, 2, 128, 1024), BF16)]]
        + [dma((4,)), dma((4,)), dma((6, 17)), dma((6, 17)), dma((6,)), dma((3,)), dma((3,)), dma((2, 3, 2)), dma, dma, dma((20,)), dma((2,))],
        compiler_params=pltpu.CompilerParams(collective_id=7, has_side_effects=True, vmem_limit_bytes=67043328),
        cost_estimate=pl.CostEstimate(flops=20 * 10**9, bytes_accessed=60 << 20, transcendentals=10**7),
        name="forward",
    )(tokens, cotangent, *shards, pack)


CHUNKS = 12
SLOTS = 10


def gelu_slope(u):
    inner = 0.7978845608028654 * (u + 0.044715 * u * u * u)
    t = jnp.tanh(inner)
    return 0.5 * (1.0 + t) + 0.5 * u * (1.0 - t * t) * (0.7978845608028654 * (1.0 + 3 * 0.044715 * u * u))


def bwd_kernel(
    cot_hbm, gd_hbm, n2_t_hbm, up_hbm, wd_hbm, wu_hbm, wo_hbm, wq_hbm, att_t_hbm, n1_t_hbm,
    qkv_hbm, kv_hbm, att_hbm, out_hbm, res_hbm, x_hbm, lse_ref, vec,
    gd_out, gu_out, go_out, gq_out, result_out, gin_out, small_out,
    sums_ref, sum_in, so, sr, g, h1a, h1b, h2a, h2b, z1, z2, fin, dkv_in, cot, gres, gub, n2_t,
    sib_s, sib_r, hop_s, hop_r, zs, zr, fin_sem, dkv_s, dkv_r, load, ms, ss, sm,
):
    p = device_map()
    x, y, core, par, z = p["x"], p["y"], p["core"], p["par"], p["z"]
    sibling, over_x, over_y, near_z, far_z = (p[n] for n in ("sibling", "over_x", "over_y", "near_z", "far_z"))
    greet(p, ("sibling", "over_x", "over_y", "near_z", "far_z"), True)
    mid, across = p["mid"], p["across"]

    lo, hi = pl.ds(0, 512), pl.ds(512, 512)
    def to_sib(k):
        return remote(so.at[lax.rem(k, 2)], sr.at[lax.rem(k, 2)], sib_s.at[k], sib_r.at[k], sibling)

    def hop(k, j):
        src, dst, to = (
            (g.at[lax.rem(k, SLOTS), 1, :, :, lo], h1a.at[k], over_y),
            (g.at[lax.rem(k, SLOTS), :, 1, :, hi], h1b.at[k], over_x),
            (g.at[lax.rem(k, SLOTS), 0, 1, :, lo], h2a.at[k], over_x),
            (g.at[lax.rem(k, SLOTS), 1, 0, :, hi], h2b.at[k], over_y),
        )[j]
        return remote(src, dst, hop_s.at[k, j], hop_r.at[k, j], to)

    def zhop(k, j, side):
        cols = (lo, hi)[side]
        dst, to = ((z1.at[k, :, cols], near_z), (z2.at[k, :, cols], across), (z2.at[k, :, cols], near_z))[j]
        return remote(g.at[lax.rem(k, SLOTS), 0, 0, :, cols], dst, zs.at[k, 2 * j + side], zr.at[k, 2 * j + side], to)

    def ends(run):
        pl.when(jnp.logical_not(mid))(run)

    def plus(a, b):
        return (a.astype(F32) + b.astype(F32)).astype(BF16)

    def out_copy(k):
        slot = lax.rem(k, 2)
        def with_target(run):
            col = lambda j: pl.ds(pl.multiple_of(j * 1024, 1024), 1024)
            sem = fin_sem.at[slot]
            @pl.when(k < 4)
            def _(): run(pltpu.make_async_copy(fin.at[slot], gd_out.at[:, col(k)], sem))
            @pl.when(jnp.logical_and(k >= 4, k < 8))
            def _(): run(pltpu.make_async_copy(fin.at[slot], gu_out.at[:, col(k - 4)], sem))
            @pl.when(k == 8)
            def _(): run(pltpu.make_async_copy(fin.at[slot], go_out, sem))
            @pl.when(k > 8)
            def _(): run(pltpu.make_async_copy(fin.at[slot], gq_out.at[:, col(k - 9)], sem))
        return with_target

    def tick(n):
        def stage(k, body):
            @pl.when(jnp.logical_and(k >= 0, k < CHUNKS))
            def _(): body(k)

        def c2(k):
            hop(k, 0).wait(); hop(k, 1).wait()
            g[lax.rem(k, SLOTS), 0, :, :, lo] = plus(g[lax.rem(k, SLOTS), 0, :, :, lo], h1a[k])
            g[lax.rem(k, SLOTS), :, 0, :, hi] = plus(g[lax.rem(k, SLOTS), :, 0, :, hi], h1b[k])
            hop(k, 2).start(); hop(k, 3).start()
            @pl.when(k == 0)
            def _():
                hop(k + 3, 0).start(); hop(k + 3, 1).start()

        sides = ((0, lo), (1, hi))

        def c3(k):
            for side, cols in sides:
                hop(k, 2 + side).wait()
                mine = (lax.rem(k, SLOTS), 0, 0, slice(None), cols)
                g[mine] = plus(g[mine], (h2a, h2b)[side][k])
                ends(lambda: zhop(k, 0, side).start())

        def c4(k):
            @pl.when(mid)
            def _():
                for side, cols in sides:
                    zhop(k, 0, side).wait_recv()
                    mine = (lax.rem(k, SLOTS), 0, 0, slice(None), cols)
                    g[mine] = plus(g[mine], z1[k, :, cols])
                    zhop(k, 1, side).start()

        def c5(k):
            @pl.when(mid)
            def _():
                for side, cols in sides:
                    zhop(k, 1, side).wait()
                    mine = (lax.rem(k, SLOTS), 0, 0, slice(None), cols)
                    g[mine] = plus(g[mine], z2[k, :, cols])
                    zhop(k, 2, side).start()

        def c6(k):
            slot = lax.rem(k, 2)
            @pl.when(k >= 2)
            def _(): out_copy(k - 2)(lambda c: c.wait())
            @pl.when(mid)
            def _():
                fin[slot] = g[lax.rem(k, SLOTS), 0, 0].astype(F32)
                for side in range(2): zhop(k, 2, side).wait_send()
            def other():
                for side, cols in sides:
                    zhop(k, 0, side).wait_send()
                    zhop(k, 2, side).wait_recv()
                    fin[slot, :, cols] = z2[k, :, cols].astype(F32)
            ends(other)
            out_copy(k)(lambda c: c.start())

        stage(n, c2); stage(n - 1, c3); stage(n - 2, c4); stage(n - 3, c5); stage(n - 4, c6)

    def send_odd(k, left, right):
        def one(cols):
            so[lax.rem(k, 2), :, cols] = dg(left[512:1024, :], right[:, cols], NN).astype(BF16)
        tiles(2, one, 512)
        to_sib(k).start()

    def add_even(k, left, right):
        to_sib(k).wait()
        def one(cols):
            part = dg(left[0:512, :], right[:, cols], NN) + sr[lax.rem(k, 2), :, cols].astype(F32)
            g[lax.rem(k, SLOTS), :, :, :, cols] = part.astype(BF16).reshape(2, 2, 128, 512)
        tiles(2, one, 512)
        hop(k, 0).start(); hop(k, 1).start()

    def fetch(src, dst, i):
        return pltpu.make_async_copy(src, dst, load.at[i])

    first = fetch(cot_hbm, cot, 0)
    first.start()
    result = Move(p, [out_hbm.at[pl.ds(256 * h, 256)] for h in range(2)], lambda b: result_out.at[b], ms.at[0])
    result.start()
    sums_ref[...] = jnp.zeros_like(sums_ref)

    def mlp(upb, wdb, wub, gn2, resb):
        sums4 = fetch(gd_hbm, g.at[pl.ds(0, 4)], 1)
        pieces = [fetch(n2_t_hbm, n2_t, 2), fetch(res_hbm, resb, 3)]
        def part(i, j):
            src, dst = ((up_hbm, upb), (wd_hbm, wdb), (wu_hbm, wub))[i]
            return pltpu.make_async_copy(src.at[:, pl.ds(pl.multiple_of(j * 1024, 1024), 1024)], dst, load.at[4 + i])
        sums4.start()
        for i in range(3): part(i, jnp.int32(0)).start()
        for c in pieces: c.start()
        sums4.wait()
        for k in range(3):
            hop(jnp.int32(k), 0).start()
            hop(jnp.int32(k), 1).start()
        gn2[...] = jnp.zeros_like(gn2)
        first.wait()
        def block(j, carry):
            def more(*which):
                @pl.when(j < 3)
                def _():
                    for i in which: part(i, j + 1).start()
            part(0, j).wait()
            part(1, j).wait()
            def slope(cols):
                back = dg(cot[...], wdb[:, cols], NN)
                low = (back * gelu_slope(upb[:, cols])).astype(BF16)
                gub[:, pl.ds(pl.multiple_of(j * 1024 + cols.start, 256), 256)] = low
                sums_ref[pl.ds(j, 1), cols] = jnp.sum(low.astype(F32), axis=0, keepdims=True)
            tiles(4, slope)
            more(0, 1)
            part(2, j).wait()
            here = pl.ds(pl.multiple_of(j * 1024, 1024), 1024)
            def down(cols):
                gn2[:, cols] += dg(gub[:, here], wub[cols, :], NT)
            tiles(4, down)
            more(2)
            @pl.when(j == 2)
            def _(): tick(jnp.int32(0))
            return carry
        lax.fori_loop(0, 4, block, 0)
        for c in pieces: c.wait()
        def rows(r):
            res = resb[r, :]
            centre = jnp.mean(res, axis=-1, keepdims=True)
            off = res - centre
            rstd = lax.rsqrt(jnp.mean(off * off, axis=-1, keepdims=True) + norm_eps)
            xhat = off * rstd
            grad = gn2[r, :]
            e = grad * vec[10:11, :]
            back = rstd * (e - jnp.mean(e, axis=-1, keepdims=True) - xhat * jnp.mean(e * xhat, axis=-1, keepdims=True))
            total = cot[r, :].astype(F32) + back
            gres[r, :] = total
            low = total.astype(BF16).astype(F32)
            add = lambda i, v: sums_ref.__setitem__((slice(i, i + 1), slice(None)), sums_ref[i : i + 1, :] + jnp.sum(v, axis=0, keepdims=True))
            add(4, low); add(5, grad * xhat); add(6, grad); add(7, cot[r, :].astype(F32))
        tiles(8, rows, 64)

    pl.run_scoped(
        mlp, pltpu.VMEM((512, 1024), F32),
        pltpu.VMEM((1024, 1024), BF16), pltpu.VMEM((1024, 1024), BF16), pltpu.VMEM((512, 1024), F32),
        pltpu.VMEM((512, 1024), F32),
    )

    def rest(dqkv, n1_t, xb):
        late = [fetch(n1_t_hbm, n1_t, 0), fetch(x_hbm, xb, 1)]

        def attention(wo, att_t, ga, kv, att, do):
            loads = [
                fetch(src, dst, 2 + i) for i, (src, dst) in enumerate((
                    (wo_hbm, wo), (qkv_hbm, dqkv), (kv_hbm, kv), (att_hbm, att), (att_t_hbm, att_t),
                ))
            ]
            for c in loads + late: c.start()
            ga[...] = gres[...].astype(BF16)
            tick(jnp.int32(1))
            loads[0].wait()
            def mixed(cols):
                do[:, cols] = dg(ga[...], wo[cols, :], NT).astype(BF16)
            tiles(4, mixed)
            for c in loads[1:4]: c.wait()
            lane = lax.broadcasted_iota(jnp.int32, (512, 128), 1)
            def up_grad(m):
                return gub.at[:, pl.ds(pl.multiple_of(m * 1024, 1024), 1024)]
            def pair(i, carry):
                at = lambda base: pl.ds(pl.multiple_of(base + i * 128, 128), 128)
                cols = at(0)
                qs = dqkv[:, cols] * jnp.asarray(0.125, BF16)
                dos = do[:, cols]
                t = (dos.astype(F32) * att[:, cols].astype(F32)).T
                dq, dk, dv = None, [None, None], [None, None]
                plus_ = lambda a, b: b if a is None else a + b
                sides = ((dqkv, at(1024), at(2048)), (kv, at(0), at(1024)))
                for h in range(2):
                    sel = (lane < 64) if h == 0 else (lane >= 64)
                    qh = jnp.where(sel, qs, jnp.zeros_like(qs))
                    doh = jnp.where(sel, dos, jnp.zeros_like(dos))
                    delta = jnp.sum(t[64 * h : 64 * h + 64], axis=0, keepdims=True)
                    lse = lse_ref[i, h : h + 1, :]
                    for n, (ref, k_at, v_at) in enumerate(sides):
                        kk = ref[:, k_at]
                        s = dg(kk, qh, NT)
                        p_ = jnp.exp(s - lse)
                        dp = dg(ref[:, v_at], doh, NT)
                        ds = (p_ * (dp - delta)).astype(BF16)
                        dv[n] = plus_(dv[n], dg(p_.astype(BF16), doh, NN))
                        dk[n] = plus_(dk[n], dg(ds, qh, NN))
                        dq = plus_(dq, dg(jnp.where(sel, kk, jnp.zeros_like(kk)), ds, TN))
                dqkv[:, cols] = (dq * 0.125).T.astype(BF16)
                for n, (ref, k_at, v_at) in enumerate(sides):
                    ref[:, k_at] = dk[n].astype(BF16)
                    ref[:, v_at] = dv[n].astype(BF16)
                m = i // 2
                @pl.when(lax.rem(i, 2) == 1)
                def _():
                    send_odd(4 + m, n2_t, up_grad(m))
                    tick(2 + m)
                @pl.when(jnp.logical_and(lax.rem(i, 2) == 0, i > 0))
                def _(): add_even(3 + m, n2_t, up_grad(m - 1))
                return carry
            lax.fori_loop(0, 8, pair, 0)
            swap = remote(kv, dkv_in, dkv_s, dkv_r, sibling)
            swap.start()
            add_even(jnp.int32(7), n2_t, up_grad(jnp.int32(3)))
            late[0].wait()
            loads[4].wait()
            send_odd(jnp.int32(8), att_t, ga)
            tick(jnp.int32(6))
            add_even(jnp.int32(8), att_t, ga)
            send_odd(jnp.int32(9), n1_t, dqkv.at[:, pl.ds(0, 1024)])
            swap.wait()

        pl.run_scoped(
            attention, pltpu.VMEM((1024, 1024), BF16), pltpu.VMEM((1024, 512), BF16), pltpu.VMEM((512, 1024), BF16),
            pltpu.VMEM((512, 2048), BF16), pltpu.VMEM((512, 1024), BF16), pltpu.VMEM((512, 1024), BF16),
        )

        def last(wq, gn1):
            def wq_part(i):
                s = lax.rem(i, 2)
                return pltpu.make_async_copy(wq_hbm.at[pl.ds(pl.multiple_of(i * 256, 256), 256), :], wq.at[s], load.at[2 + s])
            wq_part(jnp.int32(0)).start()
            def join(cols):
                there = pl.ds(pl.multiple_of(1024 + cols.start, 256), 256)
                dqkv[:, there] = plus(dqkv[:, there], dkv_in[:, cols])
            tiles(8, join)
            add_even(jnp.int32(9), n1_t, dqkv.at[:, pl.ds(0, 1024)])
            def back(i, carry):
                wq_part(i).wait()
                @pl.when(i < 3)
                def _(): wq_part(i + 1).start()
                gn1[:, pl.ds(pl.multiple_of(i * 256, 256), 256)] = dg(dqkv[...], wq[lax.rem(i, 2)], NT)
                return carry
            lax.fori_loop(0, 4, back, 0)
            late[1].wait()
            def rows(r):
                xx = xb[r, :].astype(F32)
                centre = jnp.mean(xx, axis=-1, keepdims=True)
                off = xx - centre
                rstd = lax.rsqrt(jnp.mean(off * off, axis=-1, keepdims=True) + norm_eps)
                xhat = off * rstd
                grad = gn1[r, :]
                e = grad * vec[8:9, :]
                back = rstd * (e - jnp.mean(e, axis=-1, keepdims=True) - xhat * jnp.mean(e * xhat, axis=-1, keepdims=True))
                xb[r, :] = (gres[r, :] + back).astype(BF16)
                add = lambda i, v: sums_ref.__setitem__((slice(i, i + 1), slice(None)), sums_ref[i : i + 1, :] + jnp.sum(v, axis=0, keepdims=True))
                add(8, grad * xhat); add(9, grad)
                add(10, dqkv[r, 0:1024].astype(F32)); add(11, dqkv[r, 2048:3072].astype(F32))
            tiles(8, rows, 64)
            given = [
                Move(p, [xb.at[pl.ds(256 * h + 64 * i, 64)] for h in range(2)],
                     lambda b, i=i: gin_out.at[b, pl.ds(64 * i, 64)], ms.at[1 + i])
                for i in range(4)
            ]
            steps = [
                remote(sums_ref, sum_in.at[i], ss.at[i], sm.at[i], to)
                for i, to in enumerate((sibling, over_x, over_y, near_z, far_z))
            ]
            steps[0].start()
            tick(jnp.int32(7))
            given[0].start()
            for k in (10, 11):
                right = dqkv.at[:, pl.ds(1024 * (k - 9), 1024)]
                send_odd(jnp.int32(k), n1_t, right)
                if k == 10: tick(jnp.int32(8))
                add_even(jnp.int32(k), n1_t, right)
                if k == 10: given[1].start()
            for i in range(7):
                tick(jnp.int32(9 + i))
                if i < 2: given[2 + i].start()
                if i < 5:
                    steps[i].wait()
                    sums_ref[...] += sum_in[i]
                    if i < 4: steps[i + 1].start()
            d = p["d"]
            mine = pl.ds(pl.multiple_of(d * 128, 128), 128)
            for to, at in ((0, 10), (1, 11), (2, 4), (7, 7), (8, 8), (9, 9), (10, 5), (11, 6)):
                small_out[to : to + 1, :] = sums_ref[at : at + 1, mine]
            for t in range(4):
                lanes = pl.ds(pl.multiple_of(lax.rem(d, 2) * 512 + 128 * t, 128), 128)
                part = sums_ref[0:1, lanes]
                for r in range(1, 4):
                    part = jnp.where(d // 2 == r, sums_ref[r : r + 1, lanes], part)
                small_out[3 + t : 4 + t, :] = part
            for k in (CHUNKS - 2, CHUNKS - 1):
                out_copy(jnp.int32(k))(lambda c: c.wait())
            for move in given: move.wait()
            result.wait()

        pl.run_scoped(last, pltpu.VMEM((2, 256, 3072), BF16), pltpu.VMEM((512, 1024), F32))

    pl.run_scoped(rest, pltpu.VMEM((512, 3072), BF16), pltpu.VMEM((1024, 512), BF16), pltpu.VMEM((512, 1024), BF16))


def backward(arrays, lse, vec):
    any_, vmem, hbm = (pl.BlockSpec(memory_space=s) for s in (pl.ANY, pltpu.VMEM, HBM))
    n = CHUNKS
    dma = pltpu.SemaphoreType.DMA
    return pl.pallas_call(
        bwd_kernel,
        in_specs=[any_] * len(arrays) + [vmem, vmem],
        out_specs=[hbm] * 6 + [vmem],
        out_shape=[jax.ShapeDtypeStruct((128, w), F32) for w in (4096, 4096, 1024, 3072)]
        + [jax.ShapeDtypeStruct((2, 256, 1024), BF16)] * 2 + [jax.ShapeDtypeStruct((12, 128), F32)],
        scratch_shapes=[
            pltpu.VMEM((16, 1024), F32), pltpu.VMEM((5, 16, 1024), F32),
            pltpu.VMEM((2, 512, 1024), BF16), pltpu.VMEM((2, 512, 1024), BF16), pltpu.VMEM((SLOTS, 2, 2, 128, 1024), BF16),
            pltpu.VMEM((n, 2, 128, 512), BF16), pltpu.VMEM((n, 2, 128, 512), BF16),
            pltpu.VMEM((n, 128, 512), BF16), pltpu.VMEM((n, 128, 512), BF16),
            pltpu.VMEM((n, 128, 1024), BF16), pltpu.VMEM((n, 128, 1024), BF16),
            pltpu.VMEM((2, 128, 1024), F32), pltpu.VMEM((512, 2048), BF16), pltpu.VMEM((512, 1024), BF16),
            pltpu.VMEM((512, 1024), F32), pltpu.VMEM((512, 4096), BF16), pltpu.VMEM((1024, 512), BF16),
            dma((n,)), dma((n,)), dma((n, 4)), dma((n, 4)), dma((n, 6)), dma((n, 6)), dma((2,)), dma, dma, dma((12,)),
            dma((5, 3, 2)), dma((5,)), dma((5,)),
        ],
        compiler_params=pltpu.CompilerParams(collective_id=8, has_side_effects=True, vmem_limit_bytes=67043328),
        cost_estimate=pl.CostEstimate(flops=40 * 10**9, bytes_accessed=60 << 20, transcendentals=10**7),
        name="backward",
    )(*arrays, lse, vec)


def local_fast(
    tokens, w_qkv, w_out, w_up, w_down, b_query, b_value, b_out, b_up, b_down,
    ln1_gain, ln1_bias, ln2_gain, ln2_bias, cotangent,
):
    small = (b_query, b_value, b_out, b_up, b_down, ln1_gain, ln1_bias, ln2_gain, ln2_bias)
    pack, at = jnp.zeros((12, 128), F32), 0
    for item in small:
        rows = item.shape[0] // 128
        pack = pack + jnp.pad(item.astype(F32).reshape(rows, 128), ((at, 12 - at - rows), (0, 0)))
        at += rows
    (wq, wo, wu, wd, x, cot, n1_t, n2_t, att_t, qkv, kv, att, up, res, out, gd, lse, vec) = forward(
        tokens, cotangent, (w_qkv, w_out, w_up, w_down), pack)
    g_down, g_up, g_out, g_qkv, result, grad_input, sums = backward(
        (cot, gd, n2_t, up, wd, wu, wo, wq, att_t, n1_t, qkv, kv, att, out, res, x), lse, vec)
    outs, at = [], 0
    for item in small:
        rows = item.shape[0] // 128
        outs.append(sums[at : at + rows].reshape(-1))
        at += rows
    return (result, grad_input, g_qkv, g_out, g_up, g_down.T, *outs)


def solution(mesh):
    in_specs = (
        P("dp", "seq", None),
        P("dp", None),
        P("dp", None),
        P("dp", None),
        P(None, "dp"),
        P("dp"),
        P("dp"),
        P("dp"),
        P("dp"),
        P("dp"),
        P("dp"),
        P("dp"),
        P("dp"),
        P("dp"),
        P("dp", "seq", None),
    )
    out_specs = (
        P("dp", "seq", None),
        P("dp", "seq", None),
        P("dp", None),
        P("dp", None),
        P("dp", None),
        P(None, "dp"),
        P("dp"),
        P("dp"),
        P("dp"),
        P("dp"),
        P("dp"),
        P("dp"),
        P("dp"),
        P("dp"),
        P("dp"),
    )
    fn = local_fast if dict(mesh.shape) == {"dp": 8, "seq": 4} else local
    return jax.shard_map(fn, mesh=mesh, in_specs=in_specs, out_specs=out_specs, check_vma=False)
```

```python
import functools

import jax
import jax.numpy as jnp
from jax import lax
from jax.experimental import pallas as pl
from jax.experimental.pallas import tpu as pltpu
from jax.sharding import PartitionSpec as P

H = 16
DH = 64
MICRO = 2
IMG_MB = 1


norm_eps = 1e-06


def normalize(inputs, ln_gain, ln_offset):
    centre = jnp.mean(inputs, axis=-1, keepdims=True)
    spread = jnp.mean(jnp.square(inputs - centre), axis=-1, keepdims=True)
    return (inputs - centre) * lax.rsqrt(spread + norm_eps) * ln_gain + ln_offset


def activate(upward):
    return jax.nn.gelu(upward, approximate=True)


def add_pairs(first_set, second_set):
    return tuple(
        (first_item + second_item for first_item, second_item in zip(first_set, second_set))
    )


def forward_heads(queries, keyed, valued, factor):
    images, length, head_count, head_size = queries.shape
    block_rows = min(512, length)
    blocks = length // block_rows
    query_blocks = queries.reshape(images, blocks, block_rows, head_count, head_size)

    def forward_per_image(element):
        q_image, k_image, v_image = element

        def forward_per_block(q_block):
            scores = (
                jnp.einsum("qhd,khd->hqk", q_block, k_image, preferred_element_type=jnp.float32)
                * factor
            )
            row_max = jnp.max(scores, axis=-1, keepdims=True)
            exponent = jnp.exp(scores - row_max)
            row_total = jnp.sum(exponent, axis=-1, keepdims=True)
            attn_probs = (exponent / row_total).astype(jnp.bfloat16)
            mixture = jnp.einsum(
                "hqk,khd->qhd", attn_probs, v_image, preferred_element_type=jnp.float32
            )
            return (mixture, row_max[..., 0] + jnp.log(row_total[..., 0]))

        return lax.map(forward_per_block, q_image)

    mixture, log_total = lax.map(forward_per_image, (query_blocks, keyed, valued))
    return (mixture.reshape(images, length, head_count * head_size), log_total)


def backward_heads(queries, keyed, valued, grad_mixed, log_total, factor):
    images, length, head_count, head_size = queries.shape
    block_rows = min(512, length)
    blocks = length // block_rows
    query_blocks = queries.reshape(images, blocks, block_rows, head_count, head_size)
    grad_blocks = grad_mixed.reshape(images, blocks, block_rows, head_count, head_size)

    def backward_per_image(element):
        q_image, k_image, v_image, g_image, l_image = element

        def backward_per_block(running, pieces):
            grad_key, grad_value = running
            q_block, g_block, l_block = pieces
            scores = (
                jnp.einsum("qhd,khd->hqk", q_block, k_image, preferred_element_type=jnp.float32)
                * factor
            )
            full_probs = jnp.exp(scores - l_block[..., None])
            grad_probs = jnp.einsum(
                "qhd,khd->hqk", g_block, v_image, preferred_element_type=jnp.float32
            )
            row_inner = jnp.sum(full_probs * grad_probs, axis=-1, keepdims=True)
            grad_scores = (full_probs * (grad_probs - row_inner)).astype(jnp.bfloat16)
            grad_query = (
                jnp.einsum("hqk,khd->qhd", grad_scores, k_image, preferred_element_type=jnp.float32)
                * factor
            )
            grad_key = (
                grad_key
                + jnp.einsum(
                    "hqk,qhd->khd", grad_scores, q_block, preferred_element_type=jnp.float32
                )
                * factor
            )
            grad_value = grad_value + jnp.einsum(
                "hqk,qhd->khd",
                full_probs.astype(jnp.bfloat16),
                g_block,
                preferred_element_type=jnp.float32,
            )
            return ((grad_key, grad_value), grad_query)

        empty_sum = jnp.zeros((length, head_count, head_size), jnp.float32)
        (grad_key, grad_value), grad_query = lax.scan(
            backward_per_block, (empty_sum, empty_sum), (q_image, g_image, l_image)
        )
        return (grad_query.reshape(length, head_count, head_size), grad_key, grad_value)

    return lax.map(backward_per_image, (query_blocks, keyed, valued, grad_blocks, log_total))


def weight_grads(
    normed_one_low,
    grad_projected,
    mixed_tokens,
    grad_attn_low,
    normed_two_low,
    grad_upward_low,
    activated_low,
    grad_branch,
    model_width,
):
    grad_qkv = jnp.einsum(
        "ptd,pte->de", normed_one_low, grad_projected, preferred_element_type=jnp.float32
    )
    grad_bquery = jnp.sum(grad_projected[:, :, :model_width], axis=(0, 1), dtype=jnp.float32)
    grad_bvalue = jnp.sum(grad_projected[:, :, 2 * model_width :], axis=(0, 1), dtype=jnp.float32)
    grad_wout = jnp.einsum(
        "pte,ptd->ed", mixed_tokens, grad_attn_low, preferred_element_type=jnp.float32
    )
    grad_bout = jnp.sum(grad_attn_low, axis=(0, 1), dtype=jnp.float32)
    grad_up = jnp.einsum(
        "ptd,ptf->df", normed_two_low, grad_upward_low, preferred_element_type=jnp.float32
    )
    grad_bup = jnp.sum(grad_upward_low, axis=(0, 1), dtype=jnp.float32)
    grad_down = jnp.einsum(
        "ptf,ptd->fd", activated_low, grad_branch, preferred_element_type=jnp.float32
    )
    grad_bdown = jnp.sum(grad_branch, axis=(0, 1), dtype=jnp.float32)
    return (
        grad_qkv,
        grad_wout,
        grad_up,
        grad_down,
        grad_bquery,
        grad_bvalue,
        grad_bout,
        grad_bup,
        grad_bdown,
    )


def local(
    tokens,
    w_qkv,
    w_out,
    w_up,
    w_down,
    b_query,
    b_value,
    b_out,
    b_up,
    b_down,
    ln1_gain,
    ln1_bias,
    ln2_gain,
    ln2_bias,
    cotangent,
):
    seq_count = lax.axis_size("seq")
    local_patches = tokens.shape[1]
    model_width = tokens.shape[2]
    patches = local_patches * seq_count
    head_local = H // seq_count
    factor = DH ** (-0.5)
    gathered = (
        lax.all_gather(w_qkv, "dp", axis=0, tiled=True),
        lax.all_gather(w_out, "dp", axis=0, tiled=True),
        lax.all_gather(w_up, "dp", axis=0, tiled=True),
        lax.all_gather(w_down, "dp", axis=1, tiled=True),
        lax.all_gather(b_query, "dp", axis=0, tiled=True),
        lax.all_gather(b_value, "dp", axis=0, tiled=True),
        lax.all_gather(b_out, "dp", axis=0, tiled=True),
        lax.all_gather(b_up, "dp", axis=0, tiled=True),
        lax.all_gather(b_down, "dp", axis=0, tiled=True),
        lax.all_gather(ln1_gain, "dp", axis=0, tiled=True),
        lax.all_gather(ln1_bias, "dp", axis=0, tiled=True),
        lax.all_gather(ln2_gain, "dp", axis=0, tiled=True),
        lax.all_gather(ln2_bias, "dp", axis=0, tiled=True),
    )
    outputs = []
    grad_inputs = []
    kept = []
    for micro_idx in range(MICRO):
        w_qkv_full, w_out_full, w_up_full, w_down_full = (
            gathered[0],
            gathered[1],
            gathered[2],
            gathered[3],
        )
        vectors = [piece.astype(jnp.float32) for piece in gathered[4:]]
        (
            bias_query,
            bias_value,
            bias_out,
            bias_up,
            bias_down,
            gain_one,
            offset_one,
            gain_two,
            offset_two,
        ) = vectors
        start = micro_idx * IMG_MB
        inputs = tokens[start : start + IMG_MB].astype(jnp.float32)
        normed_one, norm_one_back = jax.vjp(normalize, inputs, gain_one, offset_one)
        normed_one_low = normed_one.astype(jnp.bfloat16)
        qkv_bias = jnp.concatenate([bias_query, jnp.zeros_like(bias_query), bias_value])
        projected = (
            jnp.einsum(
                "ptd,de->pte", normed_one_low, w_qkv_full, preferred_element_type=jnp.float32
            )
            + qkv_bias
        )
        projected_low = projected.astype(jnp.bfloat16).reshape(
            IMG_MB, local_patches, 3, model_width
        )
        by_heads = lax.all_to_all(projected_low, "seq", split_axis=3, concat_axis=1, tiled=True)
        queries = by_heads[:, :, 0].reshape(IMG_MB, patches, head_local, DH)
        keyed = by_heads[:, :, 1].reshape(IMG_MB, patches, head_local, DH)
        valued = by_heads[:, :, 2].reshape(IMG_MB, patches, head_local, DH)
        attended, log_total = forward_heads(queries, keyed, valued, factor)
        attended_low = attended.astype(jnp.bfloat16)
        mixed_tokens = lax.all_to_all(attended_low, "seq", split_axis=1, concat_axis=2, tiled=True)
        residual = (
            inputs
            + jnp.einsum(
                "pte,ed->ptd", mixed_tokens, w_out_full, preferred_element_type=jnp.float32
            )
            + bias_out
        )
        normed_two, norm_two_back = jax.vjp(normalize, residual, gain_two, offset_two)
        normed_two_low = normed_two.astype(jnp.bfloat16)
        upward = (
            jnp.einsum("ptd,df->ptf", normed_two_low, w_up_full, preferred_element_type=jnp.float32)
            + bias_up
        )
        activated, activate_back = jax.vjp(activate, upward)
        activated_low = activated.astype(jnp.bfloat16)
        layer_out = (
            residual
            + jnp.einsum(
                "ptf,fd->ptd", activated_low, w_down_full, preferred_element_type=jnp.float32
            )
            + bias_down
        )
        outputs.append(layer_out.astype(jnp.bfloat16))
        grad_result = cotangent[start : start + IMG_MB].astype(jnp.float32)
        grad_branch = grad_result.astype(jnp.bfloat16)
        grad_active = jnp.einsum(
            "ptd,fd->ptf", grad_branch, w_down_full, preferred_element_type=jnp.float32
        )
        (grad_upward,) = activate_back(grad_active)
        grad_upward_low = grad_upward.astype(jnp.bfloat16)
        grad_normed_two = jnp.einsum(
            "ptf,df->ptd", grad_upward_low, w_up_full, preferred_element_type=jnp.float32
        )
        grad_from_two, grad_gain2, grad_bias2 = norm_two_back(grad_normed_two)
        grad_residual = grad_result + grad_from_two
        grad_attn_low = grad_residual.astype(jnp.bfloat16)
        grad_mixed = jnp.einsum(
            "ptd,ed->pte", grad_attn_low, w_out_full, preferred_element_type=jnp.float32
        ).astype(jnp.bfloat16)
        grad_heads = lax.all_to_all(grad_mixed, "seq", split_axis=2, concat_axis=1, tiled=True)
        grad_query, grad_key, grad_value = backward_heads(
            queries,
            keyed,
            valued,
            grad_heads.reshape(IMG_MB, patches, head_local, DH),
            log_total,
            factor,
        )
        stacked = (
            jnp.stack([grad_query, grad_key, grad_value], axis=2)
            .reshape(IMG_MB, patches, 3, head_local * DH)
            .astype(jnp.bfloat16)
        )
        grad_parts = lax.all_to_all(stacked, "seq", split_axis=1, concat_axis=3, tiled=True)
        grad_projected = grad_parts.reshape(IMG_MB, local_patches, 3 * model_width)
        grad_normed_one = jnp.einsum(
            "pte,de->ptd", grad_projected, w_qkv_full, preferred_element_type=jnp.float32
        )
        grad_from_one, grad_gain1, grad_bias1 = norm_one_back(grad_normed_one)
        grad_inputs.append((grad_residual + grad_from_one).astype(jnp.bfloat16))
        norm_grads = (grad_gain1, grad_bias1, grad_gain2, grad_bias2)
        norm_total = norm_grads if micro_idx == 0 else add_pairs(norm_total, norm_grads)
        kept.append(
            (
                normed_one_low,
                grad_projected,
                mixed_tokens,
                grad_attn_low,
                normed_two_low,
                grad_upward_low,
                activated_low,
                grad_branch,
            )
        )
    joined = [jnp.concatenate([item[index] for item in kept], axis=0) for index in range(8)]
    big = weight_grads(
        joined[0],
        joined[1],
        joined[2],
        joined[3],
        joined[4],
        joined[5],
        joined[6],
        joined[7],
        model_width,
    )
    owned = (
        lax.psum_scatter(big[0].astype(jnp.bfloat16), "dp", scatter_dimension=0, tiled=True).astype(
            jnp.float32
        ),
        lax.psum_scatter(big[1].astype(jnp.bfloat16), "dp", scatter_dimension=0, tiled=True).astype(
            jnp.float32
        ),
        lax.psum_scatter(big[2].astype(jnp.bfloat16), "dp", scatter_dimension=0, tiled=True).astype(
            jnp.float32
        ),
        lax.psum_scatter(big[3].astype(jnp.bfloat16), "dp", scatter_dimension=1, tiled=True).astype(
            jnp.float32
        ),
        lax.psum_scatter(big[4].astype(jnp.bfloat16), "dp", scatter_dimension=0, tiled=True).astype(
            jnp.float32
        ),
        lax.psum_scatter(big[5].astype(jnp.bfloat16), "dp", scatter_dimension=0, tiled=True).astype(
            jnp.float32
        ),
        lax.psum_scatter(big[6].astype(jnp.bfloat16), "dp", scatter_dimension=0, tiled=True).astype(
            jnp.float32
        ),
        lax.psum_scatter(big[7].astype(jnp.bfloat16), "dp", scatter_dimension=0, tiled=True).astype(
            jnp.float32
        ),
        lax.psum_scatter(big[8].astype(jnp.bfloat16), "dp", scatter_dimension=0, tiled=True).astype(
            jnp.float32
        ),
        lax.psum_scatter(
            norm_total[0].astype(jnp.bfloat16), "dp", scatter_dimension=0, tiled=True
        ).astype(jnp.float32),
        lax.psum_scatter(
            norm_total[1].astype(jnp.bfloat16), "dp", scatter_dimension=0, tiled=True
        ).astype(jnp.float32),
        lax.psum_scatter(
            norm_total[2].astype(jnp.bfloat16), "dp", scatter_dimension=0, tiled=True
        ).astype(jnp.float32),
        lax.psum_scatter(
            norm_total[3].astype(jnp.bfloat16), "dp", scatter_dimension=0, tiled=True
        ).astype(jnp.float32),
    )
    owned = (
        lax.psum(owned[0].astype(jnp.bfloat16), "seq").astype(jnp.float32),
        lax.psum(owned[1].astype(jnp.bfloat16), "seq").astype(jnp.float32),
        lax.psum(owned[2].astype(jnp.bfloat16), "seq").astype(jnp.float32),
        lax.psum(owned[3].astype(jnp.bfloat16), "seq").astype(jnp.float32),
        lax.psum(owned[4].astype(jnp.bfloat16), "seq").astype(jnp.float32),
        lax.psum(owned[5].astype(jnp.bfloat16), "seq").astype(jnp.float32),
        lax.psum(owned[6].astype(jnp.bfloat16), "seq").astype(jnp.float32),
        lax.psum(owned[7].astype(jnp.bfloat16), "seq").astype(jnp.float32),
        lax.psum(owned[8].astype(jnp.bfloat16), "seq").astype(jnp.float32),
        lax.psum(owned[9].astype(jnp.bfloat16), "seq").astype(jnp.float32),
        lax.psum(owned[10].astype(jnp.bfloat16), "seq").astype(jnp.float32),
        lax.psum(owned[11].astype(jnp.bfloat16), "seq").astype(jnp.float32),
        lax.psum(owned[12].astype(jnp.bfloat16), "seq").astype(jnp.float32),
    )
    return (
        jnp.concatenate(outputs, axis=0),
        jnp.concatenate(grad_inputs, axis=0),
        owned[0],
        owned[1],
        owned[2],
        owned[3],
        owned[4],
        owned[5],
        owned[6],
        owned[7],
        owned[8],
        owned[9],
        owned[10],
        owned[11],
        owned[12],
    )


F32=jnp.float32; BF16=jnp.bfloat16
NT=(((1,),(1,)),((),())); TN=(((0,),(0,)),((),())); NN=(((1,),(0,)),((),()))
def dg(a,b,dims): return lax.dot_general(a,b,dims,preferred_element_type=F32)

MESH = pl.DeviceIdType.MESH
HBM = pltpu.MemorySpace.HBM


def device_map():
    d, z = lax.axis_index("dp"), lax.axis_index("seq")
    core, x, y = lax.rem(d, 2), lax.rem(d // 2, 2), d // 4
    par = lax.rem(z, 2)
    return dict(
        d=d, z=z, core=core, x=x, y=y, par=par,
        sibling=(d + 1 - 2 * core, z), over_x=(d + 2 - 4 * x, z), over_y=(d + 4 - 8 * y, z),
        near_z=(d, z + 1 - 2 * par), far_z=(d, z + 2 - 4 * (z // 2)),
        across=(d, 3 - z), mid=z * (3 - z) > 0,
        image=[(d - core + z // 2, 2 * core + b) for b in range(2)],
        home=(z // 2) == core,
    )


def remote(src, dst, send, recv, to):
    return pltpu.make_async_remote_copy(
        src_ref=src, dst_ref=dst, send_sem=send, recv_sem=recv, device_id=to, device_id_type=MESH
    )


def greet(place, names, middle=False):
    barrier = pltpu.get_barrier_semaphore()
    if middle:
        @pl.when(place["mid"])
        def _(): pl.semaphore_signal(barrier, inc=1, device_id=place["across"], device_id_type=MESH)
    for name in names:
        pl.semaphore_signal(barrier, inc=1, device_id=place[name], device_id_type=MESH)
    for b in range(2):
        @pl.when(jnp.logical_not(jnp.logical_and(place["home"], place["par"] == b)))
        def _(): pl.semaphore_signal(barrier, inc=1, device_id=place["image"][b], device_id_type=MESH)
    extra = place["mid"].astype(jnp.int32) if middle else 0
    pl.semaphore_wait(barrier, len(names) + 2 - place["home"].astype(jnp.int32) + extra)


class Move:
    def __init__(self, place, sources, target, sems):
        self.place, self.sources, self.target, self.sems = place, sources, target, sems
    def each(self, far, near):
        p = self.place
        for b in range(2):
            stays = jnp.logical_and(p["home"], p["par"] == b)
            target = self.target(p["par"])
            @pl.when(jnp.logical_not(stays))
            def _(): far(remote(self.sources[b], target, self.sems.at[0, b], self.sems.at[1, p["par"]], p["image"][b]))
            @pl.when(stays)
            def _(): near(pltpu.make_async_copy(self.sources[b], target, self.sems.at[2, 0]))
    def start(self):
        self.each(lambda c: c.start(), lambda c: c.start())
    def wait(self):
        p = self.place
        self.each(lambda c: c.wait_send(), lambda c: c.wait())
        for h in range(2):
            @pl.when(jnp.logical_not(jnp.logical_and(p["home"], p["par"] == h)))
            def _(): remote(self.sources[0], self.target(h), self.sems.at[0, 0], self.sems.at[1, h], p["image"][0]).wait_recv()


def tiles(count, body, size=256):
    def step(i, carry):
        body(pl.ds(pl.multiple_of(i * size, size), size))
        return carry
    lax.fori_loop(0, count, step, 0)


def turn(place, source, target):
    for j in range(8):
        jy, jx, jc = j // 4, (j // 2) % 2, j % 2
        differ = lambda a, b: (a + b) - 2 * a * b
        at = differ(place["core"], jc) * 4 + differ(place["y"], jy) * 2 + differ(place["x"], jx)
        target[pl.ds(pl.multiple_of(at * 128, 128), 128), :] = source[:, 128 * j : 128 * j + 128].T


def fwd_kernel(
    tok_hbm, cotg_hbm, wq_s, wo_s, wu_s, wd_s, pack,
    wq_o, wo_o, wu_o, wd_o, x_o, cot_o, n1_t_o, n2_t_o, att_t_o, qkv_o, kv_o, att_o, up_o, res_o, out_o, gd_o,
    lse, vec,
    wq, wo, wu, wd, wdn, pk, xb, cot, n1, n2, qkv, kv, att, act, upb, up_bias, res, cot_t, n1_t, n2_t, att_t, so, sr, gs,
    sib_s, sib_r, ws, wr, wl, ps, pr, ms, kvs, kvr, outs, ups,
):
    p = device_map()
    y, x, core, par = p["y"], p["x"], p["core"], p["par"]
    greet(p, ("sibling", "over_x", "over_y", "near_z"))

    def rows(py, px):
        return pl.ds(pl.multiple_of(((py * 2 + px) * 2 + core) * 128, 128), 128)

    chunks = [(wq, wq_s, 0, 3072), (wo, wo_s, 0, 1024), (wu, wu_s, 0, 2048), (wu, wu_s, 2048, 2048),
              (wd, None, 0, 2048), (wd, None, 2048, 2048)]
    me, bx, by, diag = rows(y, x), rows(y, 1 - x), rows(1 - y, x), rows(1 - y, 1 - x)

    shared = (2, 3)

    def copy(n, i):
        w, shard, at, size = chunks[n]
        full = part = pl.ds(at, size)
        lo, hi = pl.ds(at, size // 2), pl.ds(at + size // 2, size // 2)
        rest = None
        if n in shared:
            start_at = lambda by: pl.multiple_of(at + by, 512)
            part, rest = pl.ds(start_at(par * 1024), 1024), pl.ds(start_at((1 - par) * 1024), 1024)
            lo, hi = pl.ds(start_at(par * 1024), 512), pl.ds(start_at(par * 1024 + 512), 512)
        own = (lambda cols: w.at[me, cols]) if shard is None else (lambda cols: shard.at[:, cols])
        src, dst, to = (
            (own(lo), w.at[me, lo], "over_x"), (own(hi), w.at[me, hi], "over_y"),
            (own(hi), w.at[me, hi], "over_x"), (own(lo), w.at[me, lo], "over_y"),
            (own(full), w.at[me, full], "sibling"),
            (w.at[bx, lo], w.at[bx, lo], "over_y"), (w.at[by, hi], w.at[by, hi], "over_x"),
            (w.at[bx, part], w.at[bx, part], "sibling"), (w.at[by, part], w.at[by, part], "sibling"),
            (w.at[diag, lo], w.at[diag, lo], "sibling"), (w.at[diag, hi], w.at[diag, hi], "sibling"),
        )[i] if i < 11 else (
            (w.at[bx, part], w.at[bx, part], "near_z"), (w.at[by, part], w.at[by, part], "near_z"),
            (w.at[diag, part], w.at[diag, part], "near_z"),
            (w.at[bx, rest], w.at[bx, rest], "sibling"), (w.at[by, rest], w.at[by, rest], "sibling"),
            (w.at[diag, rest], w.at[diag, rest], "sibling"),
        )[i - 11]
        return remote(src, dst, ws.at[n, i], wr.at[n, i], p[to])

    def start(n, *which):
        for i in which: copy(n, i).start()

    def wait(n, *which):
        for i in which: copy(n, i).wait()

    def local(n):
        w, shard, at, size = chunks[n]
        return pltpu.make_async_copy(shard.at[:, pl.ds(at, size)], w.at[me, pl.ds(at, size)], wl.at[n])

    def own(n):
        start(n, 0, 1, 2, 3, 4)
        if chunks[n][1] is not None: local(n).start()

    def mid(n):
        wait(n, 0, 1)
        start(n, 5, 6)
        if n < 5: own(n + 1)

    def late(n):
        wait(n, 2, 3)
        start(n, 7, 8)
        if n in shared: start(n, 11, 12)

    def end(n):
        wait(n, 5, 6)
        start(n, 9, 10)
        if n in shared: start(n, 13)
        else: settle_chunk(n)

    def settle_chunk(n):
        if n in shared:
            wait(n, 11, 12, 13)
            start(n, 14, 15, 16)
            wait(n, 14, 15, 16)
        wait(n, 4, 7, 8, 9, 10)
        if chunks[n][1] is not None: local(n).wait()

    given, settled = [], []
    def give(src, dst):
        c = pltpu.make_async_copy(src, dst, outs.at[len(given)])
        c.start()
        given.append(c)
        return c

    def settle(c):
        c.wait()
        settled.append(c)

    own(0)
    pk[y, x, core] = pack[...]
    hop1 = remote(pk.at[y, x, core], pk.at[y, x, core], ps.at[0], pr.at[0], p["over_x"])
    hop1.start()
    half = lambda h: pl.ds(pl.multiple_of(h * 256, 256), 256)
    tok = Move(p, [tok_hbm.at[b] for b in range(2)], lambda h: xb.at[half(h)], ms.at[0])
    tok.start()
    cot_move = Move(p, [cotg_hbm.at[b] for b in range(2)], lambda h: cot.at[half(h)], ms.at[1])
    cot_move.start()
    down = pltpu.make_async_copy(wd_s, wdn, wl.at[5])
    down.start()
    hop1.wait()
    hop2 = remote(pk.at[y, :, core], pk.at[y, :, core], ps.at[1], pr.at[1], p["over_y"])
    hop2.start()
    down.wait()
    for j in range(8):
        wd[me, 512 * j : 512 * j + 512] = wdn[512 * j : 512 * j + 512, :].T
    hop2.wait()
    hop3 = remote(pk.at[:, :, core], pk.at[:, :, core], ps.at[2], pr.at[2], p["sibling"])
    hop3.start()
    mid(0)
    hop3.wait()
    for j in range(8):
        block = pk[j // 4, (j // 2) % 2, j % 2]
        for r in range(12):
            if 3 <= r < 7:
                at = 512 * j + 128 * (r - 3)
                up_bias[:, at : at + 128] = block[r : r + 1]
            else:
                to = {0: 4, 1: 5, 2: 6, 7: 7, 8: 8, 9: 9, 10: 10, 11: 11}[r]
                vec[to : to + 1, 128 * j : 128 * j + 128] = block[r : r + 1]
    vec[0:4, :] = jnp.zeros((4, 1024), F32)
    vec[12:16, :] = jnp.zeros((4, 1024), F32)
    tok.wait()

    def stats(value):
        off = value - jnp.mean(value, axis=-1, keepdims=True)
        return off * lax.rsqrt(jnp.mean(off * off, axis=-1, keepdims=True) + norm_eps)

    def norm_one(r):
        n1[r, :] = (stats(xb[r, :].astype(F32)) * vec[8:9, :] + vec[9:10, :]).astype(BF16)
    tiles(8, norm_one, 64)
    x_given = give(xb, x_o)
    late(0)
    turn(p, n1, n1_t)
    give(n1_t, n1_t_o)
    end(0)
    give(wq, wq_o)
    mid(1)

    def project(cols, bias):
        part = dg(n1[...], wq[:, cols], NN)
        qkv[:, cols] = (part if bias is None else part + bias).astype(BF16)
    def key_cols(c): project(pl.ds(pl.multiple_of(1024 + c.start, 256), 256), None)
    tiles(4, key_cols)
    def value_cols(c): project(pl.ds(pl.multiple_of(2048 + c.start, 256), 256), vec[5:6, c])
    tiles(4, value_cols)
    swap = remote(qkv.at[:, pl.ds(1024, 2048)], kv, kvs, kvr, p["sibling"])
    swap.start()
    def query_cols(c): project(c, vec[4:5, c])
    tiles(4, query_cols)
    swap.wait()
    give(qkv, qkv_o)
    give(kv, kv_o)

    lane = lax.broadcasted_iota(jnp.int32, (512, 128), 1)
    def pair(i, carry):
        at = lambda base: pl.ds(pl.multiple_of(base + i * 128, 128), 128)
        q = qkv[:, at(0)] * jnp.asarray(0.125, BF16)
        outs_, ls = [], []
        for h in range(2):
            qh = jnp.where((lane < 64) if h == 0 else (lane >= 64), q, jnp.zeros_like(q))
            sa, sb = dg(qkv[:, at(1024)], qh, NT), dg(kv[:, at(0)], qh, NT)
            m = jnp.maximum(jnp.max(sa, axis=0, keepdims=True), jnp.max(sb, axis=0, keepdims=True))
            pa, pb = jnp.exp(sa - m), jnp.exp(sb - m)
            total = jnp.sum(pa, axis=0, keepdims=True) + jnp.sum(pb, axis=0, keepdims=True)
            o = dg(qkv[:, at(2048)], pa.astype(BF16), TN) + dg(kv[:, at(1024)], pb.astype(BF16), TN)
            outs_.append(o[64 * h : 64 * h + 64] * (1.0 / total))
            ls.append(m + jnp.log(total))
        att[:, at(0)] = jnp.concatenate(outs_, axis=0).T.astype(BF16)
        lse[i] = jnp.concatenate(ls + [jnp.zeros((6, 512), F32)], axis=0)
        @pl.when(i == 1)
        def _():
            late(1)
            end(1)
            late(2)
        @pl.when(i == 3)
        def _():
            end(2)
            mid(3)
        @pl.when(i == 6)
        def _():
            late(3)
            end(3)
        return carry
    mid(2)
    lax.fori_loop(0, 8, pair, 0)
    mid(4)
    give(wo, wo_o)
    give(att, att_o)
    def out_cols(c):
        res[:, c] = xb[:, c].astype(F32) + dg(att[...], wo[:, c], NN) + vec[6:7, c]
    tiles(4, out_cols)
    res_given = give(res, res_o)
    def norm_two(r):
        n2[r, :] = (stats(res[r, :]) * vec[10:11, :] + vec[11:12, :]).astype(BF16)
    tiles(8, norm_two, 64)

    def up_copy(i):
        return pltpu.make_async_copy(upb.at[lax.rem(i, 2)], up_o.at[:, pl.ds(pl.multiple_of(i * 512, 512), 512)], ups.at[lax.rem(i, 2)])
    def up_block(i, carry):
        @pl.when(i >= 2)
        def _(): up_copy(i - 2).wait()
        for t in range(2):
            c = pl.ds(pl.multiple_of(i * 512 + 256 * t, 256), 256)
            u = dg(n2[...], wu[:, c], NN) + up_bias[:, c]
            upb[lax.rem(i, 2), :, 256 * t : 256 * t + 256] = u
            act[:, c] = (0.5 * u * (1.0 + jnp.tanh(0.7978845608028654 * (u + 0.044715 * u * u * u)))).astype(BF16)
        up_copy(i).start()
        return carry
    def to_sib(k):
        return remote(so.at[k % 2], sr.at[k % 2], sib_s.at[k], sib_r.at[k], p["sibling"])

    def down_odd(k):
        def one(cols):
            so[k % 2, :, cols] = dg(cot_t[512:1024, :], act[:, pl.ds(pl.multiple_of(1024 * k + cols.start, 512), 512)], NN).astype(BF16)
        tiles(2, one, 512)
        to_sib(k).start()

    def down_even(k):
        to_sib(k).wait()
        def one(cols):
            part = dg(cot_t[0:512, :], act[:, pl.ds(pl.multiple_of(1024 * k + cols.start, 512), 512)], NN)
            gs[k, :, :, :, cols] = (part + sr[k % 2, :, cols].astype(F32)).astype(BF16).reshape(2, 2, 128, 512)
        tiles(2, one, 512)
        give(gs.at[k], gd_o.at[k])

    turn(p, n2, n2_t)
    give(n2_t, n2_t_o)
    settle_chunk(2)
    lax.fori_loop(0, 4, up_block, 0)
    cot_move.wait()
    turn(p, cot, cot_t)
    give(cot, cot_o)
    late(4)
    down_odd(0)
    end(4)
    down_even(0)
    down_odd(1)
    settle(res_given)
    first, second = pl.ds(0, 2048), pl.ds(2048, 2048)
    def half_down(c):
        res[:, c] += dg(act[:, first], wd[c, first], NT)
    tiles(4, half_down)
    mid(5)
    down_even(1)
    turn(p, att, att_t)
    give(att_t, att_t_o)
    settle_chunk(3)
    give(wu, wu_o)
    lax.fori_loop(4, 8, up_block, 0)
    late(5)
    down_odd(2)
    end(5)
    give(wd, wd_o)
    settle(x_given)
    down_even(2)
    down_odd(3)
    def finish_cols(c):
        xb[:, c] = (res[:, c] + dg(act[:, second], wd[c, second], NT) + vec[7:8, c]).astype(BF16)
    tiles(4, finish_cols)
    give(xb, out_o)
    down_even(3)
    for c in given:
        if not any(c is s for s in settled): c.wait()
    up_copy(jnp.int32(6)).wait()
    up_copy(jnp.int32(7)).wait()


def forward(tokens, cotangent, shards, pack):
    any_, vmem, hbm = (pl.BlockSpec(memory_space=s) for s in (pl.ANY, pltpu.VMEM, HBM))
    dma = pltpu.SemaphoreType.DMA
    wide = [((1024, 3072), BF16), ((1024, 1024), BF16), ((1024, 4096), BF16), ((1024, 4096), BF16)]
    rows, turned = ((512, 1024), BF16), ((1024, 512), BF16)
    shapes = wide + [rows, rows] + [turned] * 3 + [
        ((512, 3072), BF16), ((512, 2048), BF16), rows, ((512, 4096), F32), ((512, 1024), F32), rows, ((4, 2, 2, 128, 1024), BF16)]
    return pl.pallas_call(
        fwd_kernel,
        in_specs=[any_] * 6 + [vmem],
        out_specs=[hbm] * len(shapes) + [vmem, vmem],
        out_shape=[jax.ShapeDtypeStruct(*s) for s in shapes + [((8, 8, 512), F32), ((16, 1024), F32)]],
        scratch_shapes=[pltpu.VMEM(*s) for s in wide + [
            ((4096, 128), BF16), ((2, 2, 2, 12, 128), F32), rows, rows, rows, rows, ((512, 3072), BF16), ((512, 2048), BF16),
            rows, ((512, 4096), BF16), ((2, 512, 512), F32), ((1, 4096), F32), ((512, 1024), F32)] + [turned] * 4 + [
            ((2, 512, 1024), BF16), ((2, 512, 1024), BF16), ((4, 2, 2, 128, 1024), BF16)]]
        + [dma((4,)), dma((4,)), dma((6, 17)), dma((6, 17)), dma((6,)), dma((3,)), dma((3,)), dma((2, 3, 2)), dma, dma, dma((20,)), dma((2,))],
        compiler_params=pltpu.CompilerParams(collective_id=7, has_side_effects=True, vmem_limit_bytes=67043328),
        cost_estimate=pl.CostEstimate(flops=20 * 10**9, bytes_accessed=60 << 20, transcendentals=10**7),
        name="forward",
    )(tokens, cotangent, *shards, pack)


CHUNKS = 12
SLOTS = 10


def gelu_slope(u):
    inner = 0.7978845608028654 * (u + 0.044715 * u * u * u)
    t = jnp.tanh(inner)
    return 0.5 * (1.0 + t) + 0.5 * u * (1.0 - t * t) * (0.7978845608028654 * (1.0 + 3 * 0.044715 * u * u))


def bwd_kernel(
    cot_hbm, gd_hbm, n2_t_hbm, up_hbm, wd_hbm, wu_hbm, wo_hbm, wq_hbm, att_t_hbm, n1_t_hbm,
    qkv_hbm, kv_hbm, att_hbm, out_hbm, res_hbm, x_hbm, lse_ref, vec,
    gd_out, gu_out, go_out, gq_out, result_out, gin_out, small_out,
    sums_ref, sum_in, so, sr, g, h1a, h1b, h2a, h2b, z1, z2, fin, dkv_in, cot, gres, gub, n2_t,
    sib_s, sib_r, hop_s, hop_r, zs, zr, fin_sem, dkv_s, dkv_r, load, ms, ss, sm,
):
    p = device_map()
    x, y, core, par, z = p["x"], p["y"], p["core"], p["par"], p["z"]
    sibling, over_x, over_y, near_z, far_z = (p[n] for n in ("sibling", "over_x", "over_y", "near_z", "far_z"))
    greet(p, ("sibling", "over_x", "over_y", "near_z", "far_z"), True)
    mid, across = p["mid"], p["across"]

    lo, hi = pl.ds(0, 512), pl.ds(512, 512)
    def to_sib(k):
        return remote(so.at[lax.rem(k, 2)], sr.at[lax.rem(k, 2)], sib_s.at[k], sib_r.at[k], sibling)

    def hop(k, j):
        src, dst, to = (
            (g.at[lax.rem(k, SLOTS), 1, :, :, lo], h1a.at[k], over_y),
            (g.at[lax.rem(k, SLOTS), :, 1, :, hi], h1b.at[k], over_x),
            (g.at[lax.rem(k, SLOTS), 0, 1, :, lo], h2a.at[k], over_x),
            (g.at[lax.rem(k, SLOTS), 1, 0, :, hi], h2b.at[k], over_y),
        )[j]
        return remote(src, dst, hop_s.at[k, j], hop_r.at[k, j], to)

    def zhop(k, j, side):
        cols = (lo, hi)[side]
        dst, to = ((z1.at[k, :, cols], near_z), (z2.at[k, :, cols], across), (z2.at[k, :, cols], near_z))[j]
        return remote(g.at[lax.rem(k, SLOTS), 0, 0, :, cols], dst, zs.at[k, 2 * j + side], zr.at[k, 2 * j + side], to)

    def ends(run):
        pl.when(jnp.logical_not(mid))(run)

    def plus(a, b):
        return (a.astype(F32) + b.astype(F32)).astype(BF16)

    def out_copy(k):
        slot = lax.rem(k, 2)
        def with_target(run):
            col = lambda j: pl.ds(pl.multiple_of(j * 1024, 1024), 1024)
            sem = fin_sem.at[slot]
            @pl.when(k < 4)
            def _(): run(pltpu.make_async_copy(fin.at[slot], gd_out.at[:, col(k)], sem))
            @pl.when(jnp.logical_and(k >= 4, k < 8))
            def _(): run(pltpu.make_async_copy(fin.at[slot], gu_out.at[:, col(k - 4)], sem))
            @pl.when(k == 8)
            def _(): run(pltpu.make_async_copy(fin.at[slot], go_out, sem))
            @pl.when(k > 8)
            def _(): run(pltpu.make_async_copy(fin.at[slot], gq_out.at[:, col(k - 9)], sem))
        return with_target

    def tick(n):
        def stage(k, body):
            @pl.when(jnp.logical_and(k >= 0, k < CHUNKS))
            def _(): body(k)

        def c2(k):
            hop(k, 0).wait(); hop(k, 1).wait()
            g[lax.rem(k, SLOTS), 0, :, :, lo] = plus(g[lax.rem(k, SLOTS), 0, :, :, lo], h1a[k])
            g[lax.rem(k, SLOTS), :, 0, :, hi] = plus(g[lax.rem(k, SLOTS), :, 0, :, hi], h1b[k])
            hop(k, 2).start(); hop(k, 3).start()
            @pl.when(k < 7)
            def _():
                hop(k + 2, 0).start(); hop(k + 2, 1).start()

        sides = ((0, lo), (1, hi))

        def c3(k):
            for side, cols in sides:
                hop(k, 2 + side).wait()
                mine = (lax.rem(k, SLOTS), 0, 0, slice(None), cols)
                g[mine] = plus(g[mine], (h2a, h2b)[side][k])
                ends(lambda: zhop(k, 0, side).start())

        def c4(k):
            @pl.when(mid)
            def _():
                for side, cols in sides:
                    zhop(k, 0, side).wait_recv()
                    mine = (lax.rem(k, SLOTS), 0, 0, slice(None), cols)
                    g[mine] = plus(g[mine], z1[k, :, cols])
                    zhop(k, 1, side).start()

        def c5(k):
            @pl.when(mid)
            def _():
                for side, cols in sides:
                    zhop(k, 1, side).wait()
                    mine = (lax.rem(k, SLOTS), 0, 0, slice(None), cols)
                    g[mine] = plus(g[mine], z2[k, :, cols])
                    zhop(k, 2, side).start()

        def c6(k):
            slot = lax.rem(k, 2)
            @pl.when(k >= 2)
            def _(): out_copy(k - 2)(lambda c: c.wait())
            @pl.when(mid)
            def _():
                fin[slot] = g[lax.rem(k, SLOTS), 0, 0].astype(F32)
                for side in range(2): zhop(k, 2, side).wait_send()
            def other():
                for side, cols in sides:
                    zhop(k, 0, side).wait_send()
                    zhop(k, 2, side).wait_recv()
                    fin[slot, :, cols] = z2[k, :, cols].astype(F32)
            ends(other)
            out_copy(k)(lambda c: c.start())

        stage(n - 3, c5); stage(n - 2, c4); stage(n - 1, c3); stage(n, c2); stage(n - 4, c6)

    def send_odd(k, left, right):
        def one(cols):
            so[lax.rem(k, 2), :, cols] = dg(left[512:1024, :], right[:, cols], NN).astype(BF16)
        tiles(2, one, 512)
        to_sib(k).start()

    def add_even(k, left, right):
        to_sib(k).wait()
        def one(cols):
            part = dg(left[0:512, :], right[:, cols], NN) + sr[lax.rem(k, 2), :, cols].astype(F32)
            g[lax.rem(k, SLOTS), :, :, :, cols] = part.astype(BF16).reshape(2, 2, 128, 512)
        tiles(2, one, 512)
        @pl.when(k > 8)
        def _():
            hop(k, 0).start(); hop(k, 1).start()

    def fetch(src, dst, i):
        return pltpu.make_async_copy(src, dst, load.at[i])

    first = fetch(cot_hbm, cot, 0)
    first.start()
    result = Move(p, [out_hbm.at[pl.ds(256 * h, 256)] for h in range(2)], lambda b: result_out.at[b], ms.at[0])
    result.start()
    sums_ref[...] = jnp.zeros_like(sums_ref)

    def up_grad(m):
        return gub.at[:, pl.ds(pl.multiple_of(m * 1024, 1024), 1024)]

    def mlp(upb, wdb, wub, gn2, resb):
        sums4 = fetch(gd_hbm, g.at[pl.ds(0, 4)], 1)
        pieces = [fetch(n2_t_hbm, n2_t, 2), fetch(res_hbm, resb, 3)]
        def part(i, j):
            src, dst = ((up_hbm, upb), (wd_hbm, wdb), (wu_hbm, wub))[i]
            return pltpu.make_async_copy(src.at[:, pl.ds(pl.multiple_of(j * 1024, 1024), 1024)], dst, load.at[4 + i])
        sums4.start()
        for i in range(3): part(i, jnp.int32(0)).start()
        for c in pieces: c.start()
        sums4.wait()
        for k in range(2):
            hop(jnp.int32(k), 0).start()
            hop(jnp.int32(k), 1).start()
        gn2[...] = jnp.zeros_like(gn2)
        first.wait()
        def block(j, carry):
            def more(*which):
                @pl.when(j < 3)
                def _():
                    for i in which: part(i, j + 1).start()
            part(0, j).wait()
            part(1, j).wait()
            def slope(cols):
                back = dg(cot[...], wdb[:, cols], NN)
                low = (back * gelu_slope(upb[:, cols])).astype(BF16)
                gub[:, pl.ds(pl.multiple_of(j * 1024 + cols.start, 256), 256)] = low
                sums_ref[pl.ds(j, 1), cols] = jnp.sum(low.astype(F32), axis=0, keepdims=True)
            tiles(4, slope)
            more(0, 1)
            part(2, j).wait()
            here = pl.ds(pl.multiple_of(j * 1024, 1024), 1024)
            def down(cols):
                gn2[:, cols] += dg(gub[:, here], wub[cols, :], NT)
            tiles(4, down)
            more(2)
            @pl.when(lax.rem(j, 2) == 1)
            def _(): tick(j // 2)
            return carry
        lax.fori_loop(0, 4, block, 0)
        for c in pieces: c.wait()
        send_odd(jnp.int32(4), n2_t, up_grad(0))
        def rows(r):
            res = resb[r, :]
            centre = jnp.mean(res, axis=-1, keepdims=True)
            off = res - centre
            rstd = lax.rsqrt(jnp.mean(off * off, axis=-1, keepdims=True) + norm_eps)
            xhat = off * rstd
            grad = gn2[r, :]
            e = grad * vec[10:11, :]
            back = rstd * (e - jnp.mean(e, axis=-1, keepdims=True) - xhat * jnp.mean(e * xhat, axis=-1, keepdims=True))
            total = cot[r, :].astype(F32) + back
            gres[r, :] = total
            low = total.astype(BF16).astype(F32)
            add = lambda i, v: sums_ref.__setitem__((slice(i, i + 1), slice(None)), sums_ref[i : i + 1, :] + jnp.sum(v, axis=0, keepdims=True))
            add(4, low); add(5, grad * xhat); add(6, grad); add(7, cot[r, :].astype(F32))
        tiles(8, rows, 64)

    pl.run_scoped(
        mlp, pltpu.VMEM((512, 1024), F32),
        pltpu.VMEM((1024, 1024), BF16), pltpu.VMEM((1024, 1024), BF16), pltpu.VMEM((512, 1024), F32),
        pltpu.VMEM((512, 1024), F32),
    )

    def rest(dqkv, n1_t, xb):
        late = [fetch(n1_t_hbm, n1_t, 0), fetch(x_hbm, xb, 1)]

        def attention(wo, att_t, ga, kv, att, do):
            loads = [
                fetch(src, dst, 2 + i) for i, (src, dst) in enumerate((
                    (wo_hbm, wo), (qkv_hbm, dqkv), (kv_hbm, kv), (att_hbm, att), (att_t_hbm, att_t),
                ))
            ]
            for c in loads + late: c.start()
            ga[...] = gres[...].astype(BF16)
            add_even(jnp.int32(4), n2_t, up_grad(0))
            send_odd(jnp.int32(5), n2_t, up_grad(1))
            tick(jnp.int32(2))
            loads[0].wait()
            def mixed(cols):
                do[:, cols] = dg(ga[...], wo[cols, :], NT).astype(BF16)
            tiles(4, mixed)
            add_even(jnp.int32(5), n2_t, up_grad(1))
            for c in loads[1:]: c.wait()
            lane = lax.broadcasted_iota(jnp.int32, (512, 128), 1)
            def pair(i, carry):
                at = lambda base: pl.ds(pl.multiple_of(base + i * 128, 128), 128)
                cols = at(0)
                qs = dqkv[:, cols] * jnp.asarray(0.125, BF16)
                dos = do[:, cols]
                t = (dos.astype(F32) * att[:, cols].astype(F32)).T
                dq, dk, dv = None, [None, None], [None, None]
                plus_ = lambda a, b: b if a is None else a + b
                sides = ((dqkv, at(1024), at(2048)), (kv, at(0), at(1024)))
                for h in range(2):
                    sel = (lane < 64) if h == 0 else (lane >= 64)
                    qh = jnp.where(sel, qs, jnp.zeros_like(qs))
                    doh = jnp.where(sel, dos, jnp.zeros_like(dos))
                    delta = jnp.sum(t[64 * h : 64 * h + 64], axis=0, keepdims=True)
                    lse = lse_ref[i, h : h + 1, :]
                    for n, (ref, k_at, v_at) in enumerate(sides):
                        kk = ref[:, k_at]
                        s = dg(kk, qh, NT)
                        p_ = jnp.exp(s - lse)
                        dp = dg(ref[:, v_at], doh, NT)
                        ds = (p_ * (dp - delta)).astype(BF16)
                        dv[n] = plus_(dv[n], dg(p_.astype(BF16), doh, NN))
                        dk[n] = plus_(dk[n], dg(ds, qh, NN))
                        dq = plus_(dq, dg(jnp.where(sel, kk, jnp.zeros_like(kk)), ds, TN))
                dqkv[:, cols] = (dq * 0.125).T.astype(BF16)
                for n, (ref, k_at, v_at) in enumerate(sides):
                    ref[:, k_at] = dk[n].astype(BF16)
                    ref[:, v_at] = dv[n].astype(BF16)
                m = i // 2
                @pl.when(lax.rem(i, 2) == 1)
                def _():
                    @pl.when(m < 2)
                    def _(): send_odd(6 + m, n2_t, up_grad(2 + m))
                    @pl.when(m == 2)
                    def _(): send_odd(jnp.int32(8), att_t, ga)
                    tick(3 + m)
                @pl.when(jnp.logical_and(lax.rem(i, 2) == 0, i > 0))
                def _():
                    @pl.when(m < 3)
                    def _(): add_even(5 + m, n2_t, up_grad(1 + m))
                    @pl.when(m == 3)
                    def _(): add_even(jnp.int32(8), att_t, ga)
                return carry
            lax.fori_loop(0, 8, pair, 0)
            swap = remote(kv, dkv_in, dkv_s, dkv_r, sibling)
            swap.start()
            late[0].wait()
            tick(jnp.int32(7))
            send_odd(jnp.int32(9), n1_t, dqkv.at[:, pl.ds(0, 1024)])
            swap.wait()

        pl.run_scoped(
            attention, pltpu.VMEM((1024, 1024), BF16), pltpu.VMEM((1024, 512), BF16), pltpu.VMEM((512, 1024), BF16),
            pltpu.VMEM((512, 2048), BF16), pltpu.VMEM((512, 1024), BF16), pltpu.VMEM((512, 1024), BF16),
        )

        def last(wq, gn1):
            def wq_part(i):
                s = lax.rem(i, 2)
                return pltpu.make_async_copy(wq_hbm.at[pl.ds(pl.multiple_of(i * 256, 256), 256), :], wq.at[s], load.at[2 + s])
            wq_part(jnp.int32(0)).start()
            def join(cols):
                there = pl.ds(pl.multiple_of(1024 + cols.start, 256), 256)
                dqkv[:, there] = plus(dqkv[:, there], dkv_in[:, cols])
            tiles(8, join)
            add_even(jnp.int32(9), n1_t, dqkv.at[:, pl.ds(0, 1024)])
            def back(i, carry):
                wq_part(i).wait()
                @pl.when(i < 3)
                def _(): wq_part(i + 1).start()
                gn1[:, pl.ds(pl.multiple_of(i * 256, 256), 256)] = dg(dqkv[...], wq[lax.rem(i, 2)], NT)
                return carry
            lax.fori_loop(0, 4, back, 0)
            tick(jnp.int32(8))
            late[1].wait()
            def rows(r):
                xx = xb[r, :].astype(F32)
                centre = jnp.mean(xx, axis=-1, keepdims=True)
                off = xx - centre
                rstd = lax.rsqrt(jnp.mean(off * off, axis=-1, keepdims=True) + norm_eps)
                xhat = off * rstd
                grad = gn1[r, :]
                e = grad * vec[8:9, :]
                back = rstd * (e - jnp.mean(e, axis=-1, keepdims=True) - xhat * jnp.mean(e * xhat, axis=-1, keepdims=True))
                xb[r, :] = (gres[r, :] + back).astype(BF16)
                add = lambda i, v: sums_ref.__setitem__((slice(i, i + 1), slice(None)), sums_ref[i : i + 1, :] + jnp.sum(v, axis=0, keepdims=True))
                add(8, grad * xhat); add(9, grad)
                add(10, dqkv[r, 0:1024].astype(F32)); add(11, dqkv[r, 2048:3072].astype(F32))
            tiles(8, rows, 64)
            given = [
                Move(p, [xb.at[pl.ds(256 * h + 32 * i, 32)] for h in range(2)],
                     lambda b, i=i: gin_out.at[b, pl.ds(32 * i, 32)], ms.at[1 + i])
                for i in range(8)
            ]
            steps = [
                remote(sums_ref, sum_in.at[i], ss.at[i], sm.at[i], to)
                for i, to in enumerate((sibling, over_x, over_y, near_z, far_z))
            ]
            steps[0].start()
            given[0].start()
            for k in (10, 11):
                right = dqkv.at[:, pl.ds(1024 * (k - 9), 1024)]
                send_odd(jnp.int32(k), n1_t, right)
                if k == 10: tick(jnp.int32(9))
                add_even(jnp.int32(k), n1_t, right)
                for m_ in ((given[1], given[2]) if k == 10 else (given[3],)): m_.start()
            for i in range(6):
                tick(jnp.int32(10 + i))
                if i < 4: given[4 + i].start()
                if i < 5:
                    steps[i].wait()
                    sums_ref[...] += sum_in[i]
                    if i < 4: steps[i + 1].start()
            d = p["d"]
            mine = pl.ds(pl.multiple_of(d * 128, 128), 128)
            for to, at in ((0, 10), (1, 11), (2, 4), (7, 7), (8, 8), (9, 9), (10, 5), (11, 6)):
                small_out[to : to + 1, :] = sums_ref[at : at + 1, mine]
            for t in range(4):
                lanes = pl.ds(pl.multiple_of(lax.rem(d, 2) * 512 + 128 * t, 128), 128)
                part = sums_ref[0:1, lanes]
                for r in range(1, 4):
                    part = jnp.where(d // 2 == r, sums_ref[r : r + 1, lanes], part)
                small_out[3 + t : 4 + t, :] = part
            for k in (CHUNKS - 2, CHUNKS - 1):
                out_copy(jnp.int32(k))(lambda c: c.wait())
            for move in given: move.wait()
            result.wait()

        pl.run_scoped(last, pltpu.VMEM((2, 256, 3072), BF16), pltpu.VMEM((512, 1024), F32))

    pl.run_scoped(rest, pltpu.VMEM((512, 3072), BF16), pltpu.VMEM((1024, 512), BF16), pltpu.VMEM((512, 1024), BF16))


def backward(arrays, lse, vec):
    any_, vmem, hbm = (pl.BlockSpec(memory_space=s) for s in (pl.ANY, pltpu.VMEM, HBM))
    n = CHUNKS
    dma = pltpu.SemaphoreType.DMA
    return pl.pallas_call(
        bwd_kernel,
        in_specs=[any_] * len(arrays) + [vmem, vmem],
        out_specs=[hbm] * 6 + [vmem],
        out_shape=[jax.ShapeDtypeStruct((128, w), F32) for w in (4096, 4096, 1024, 3072)]
        + [jax.ShapeDtypeStruct((2, 256, 1024), BF16)] * 2 + [jax.ShapeDtypeStruct((12, 128), F32)],
        scratch_shapes=[
            pltpu.VMEM((16, 1024), F32), pltpu.VMEM((5, 16, 1024), F32),
            pltpu.VMEM((2, 512, 1024), BF16), pltpu.VMEM((2, 512, 1024), BF16), pltpu.VMEM((SLOTS, 2, 2, 128, 1024), BF16),
            pltpu.VMEM((n, 2, 128, 512), BF16), pltpu.VMEM((n, 2, 128, 512), BF16),
            pltpu.VMEM((n, 128, 512), BF16), pltpu.VMEM((n, 128, 512), BF16),
            pltpu.VMEM((n, 128, 1024), BF16), pltpu.VMEM((n, 128, 1024), BF16),
            pltpu.VMEM((2, 128, 1024), F32), pltpu.VMEM((512, 2048), BF16), pltpu.VMEM((512, 1024), BF16),
            pltpu.VMEM((512, 1024), F32), pltpu.VMEM((512, 4096), BF16), pltpu.VMEM((1024, 512), BF16),
            dma((n,)), dma((n,)), dma((n, 4)), dma((n, 4)), dma((n, 6)), dma((n, 6)), dma((2,)), dma, dma, dma((12,)),
            dma((9, 3, 2)), dma((5,)), dma((5,)),
        ],
        compiler_params=pltpu.CompilerParams(collective_id=8, has_side_effects=True, vmem_limit_bytes=67043328),
        cost_estimate=pl.CostEstimate(flops=40 * 10**9, bytes_accessed=60 << 20, transcendentals=10**7),
        name="backward",
    )(*arrays, lse, vec)


def local_fast(
    tokens, w_qkv, w_out, w_up, w_down, b_query, b_value, b_out, b_up, b_down,
    ln1_gain, ln1_bias, ln2_gain, ln2_bias, cotangent,
):
    small = (b_query, b_value, b_out, b_up, b_down, ln1_gain, ln1_bias, ln2_gain, ln2_bias)
    pack, at = jnp.zeros((12, 128), F32), 0
    for item in small:
        rows = item.shape[0] // 128
        pack = pack + jnp.pad(item.astype(F32).reshape(rows, 128), ((at, 12 - at - rows), (0, 0)))
        at += rows
    (wq, wo, wu, wd, x, cot, n1_t, n2_t, att_t, qkv, kv, att, up, res, out, gd, lse, vec) = forward(
        tokens, cotangent, (w_qkv, w_out, w_up, w_down), pack)
    g_down, g_up, g_out, g_qkv, result, grad_input, sums = backward(
        (cot, gd, n2_t, up, wd, wu, wo, wq, att_t, n1_t, qkv, kv, att, out, res, x), lse, vec)
    outs, at = [], 0
    for item in small:
        rows = item.shape[0] // 128
        outs.append(sums[at : at + rows].reshape(-1))
        at += rows
    return (result, grad_input, g_qkv, g_out, g_up, g_down.T, *outs)


def solution(mesh):
    in_specs = (
        P("dp", "seq", None),
        P("dp", None),
        P("dp", None),
        P("dp", None),
        P(None, "dp"),
        P("dp"),
        P("dp"),
        P("dp"),
        P("dp"),
        P("dp"),
        P("dp"),
        P("dp"),
        P("dp"),
        P("dp"),
        P("dp", "seq", None),
    )
    out_specs = (
        P("dp", "seq", None),
        P("dp", "seq", None),
        P("dp", None),
        P("dp", None),
        P("dp", None),
        P(None, "dp"),
        P("dp"),
        P("dp"),
        P("dp"),
        P("dp"),
        P("dp"),
        P("dp"),
        P("dp"),
        P("dp"),
        P("dp"),
    )
    fn = local_fast if dict(mesh.shape) == {"dp": 8, "seq": 4} else local
    return jax.shard_map(fn, mesh=mesh, in_specs=in_specs, out_specs=out_specs, check_vma=False)
```

```python
import functools

import jax
import jax.numpy as jnp
from jax import lax
from jax.experimental import pallas as pl
from jax.experimental.pallas import tpu as pltpu
from jax.sharding import PartitionSpec as P

H = 16
DH = 64
MICRO = 2
IMG_MB = 1


norm_eps = 1e-06


def normalize(inputs, ln_gain, ln_offset):
    centre = jnp.mean(inputs, axis=-1, keepdims=True)
    spread = jnp.mean(jnp.square(inputs - centre), axis=-1, keepdims=True)
    return (inputs - centre) * lax.rsqrt(spread + norm_eps) * ln_gain + ln_offset


def activate(upward):
    return jax.nn.gelu(upward, approximate=True)


def add_pairs(first_set, second_set):
    return tuple(
        (first_item + second_item for first_item, second_item in zip(first_set, second_set))
    )


def forward_heads(queries, keyed, valued, factor):
    images, length, head_count, head_size = queries.shape
    block_rows = min(512, length)
    blocks = length // block_rows
    query_blocks = queries.reshape(images, blocks, block_rows, head_count, head_size)

    def forward_per_image(element):
        q_image, k_image, v_image = element

        def forward_per_block(q_block):
            scores = (
                jnp.einsum("qhd,khd->hqk", q_block, k_image, preferred_element_type=jnp.float32)
                * factor
            )
            row_max = jnp.max(scores, axis=-1, keepdims=True)
            exponent = jnp.exp(scores - row_max)
            row_total = jnp.sum(exponent, axis=-1, keepdims=True)
            attn_probs = (exponent / row_total).astype(jnp.bfloat16)
            mixture = jnp.einsum(
                "hqk,khd->qhd", attn_probs, v_image, preferred_element_type=jnp.float32
            )
            return (mixture, row_max[..., 0] + jnp.log(row_total[..., 0]))

        return lax.map(forward_per_block, q_image)

    mixture, log_total = lax.map(forward_per_image, (query_blocks, keyed, valued))
    return (mixture.reshape(images, length, head_count * head_size), log_total)


def backward_heads(queries, keyed, valued, grad_mixed, log_total, factor):
    images, length, head_count, head_size = queries.shape
    block_rows = min(512, length)
    blocks = length // block_rows
    query_blocks = queries.reshape(images, blocks, block_rows, head_count, head_size)
    grad_blocks = grad_mixed.reshape(images, blocks, block_rows, head_count, head_size)

    def backward_per_image(element):
        q_image, k_image, v_image, g_image, l_image = element

        def backward_per_block(running, pieces):
            grad_key, grad_value = running
            q_block, g_block, l_block = pieces
            scores = (
                jnp.einsum("qhd,khd->hqk", q_block, k_image, preferred_element_type=jnp.float32)
                * factor
            )
            full_probs = jnp.exp(scores - l_block[..., None])
            grad_probs = jnp.einsum(
                "qhd,khd->hqk", g_block, v_image, preferred_element_type=jnp.float32
            )
            row_inner = jnp.sum(full_probs * grad_probs, axis=-1, keepdims=True)
            grad_scores = (full_probs * (grad_probs - row_inner)).astype(jnp.bfloat16)
            grad_query = (
                jnp.einsum("hqk,khd->qhd", grad_scores, k_image, preferred_element_type=jnp.float32)
                * factor
            )
            grad_key = (
                grad_key
                + jnp.einsum(
                    "hqk,qhd->khd", grad_scores, q_block, preferred_element_type=jnp.float32
                )
                * factor
            )
            grad_value = grad_value + jnp.einsum(
                "hqk,qhd->khd",
                full_probs.astype(jnp.bfloat16),
                g_block,
                preferred_element_type=jnp.float32,
            )
            return ((grad_key, grad_value), grad_query)

        empty_sum = jnp.zeros((length, head_count, head_size), jnp.float32)
        (grad_key, grad_value), grad_query = lax.scan(
            backward_per_block, (empty_sum, empty_sum), (q_image, g_image, l_image)
        )
        return (grad_query.reshape(length, head_count, head_size), grad_key, grad_value)

    return lax.map(backward_per_image, (query_blocks, keyed, valued, grad_blocks, log_total))


def weight_grads(
    normed_one_low,
    grad_projected,
    mixed_tokens,
    grad_attn_low,
    normed_two_low,
    grad_upward_low,
    activated_low,
    grad_branch,
    model_width,
):
    grad_qkv = jnp.einsum(
        "ptd,pte->de", normed_one_low, grad_projected, preferred_element_type=jnp.float32
    )
    grad_bquery = jnp.sum(grad_projected[:, :, :model_width], axis=(0, 1), dtype=jnp.float32)
    grad_bvalue = jnp.sum(grad_projected[:, :, 2 * model_width :], axis=(0, 1), dtype=jnp.float32)
    grad_wout = jnp.einsum(
        "pte,ptd->ed", mixed_tokens, grad_attn_low, preferred_element_type=jnp.float32
    )
    grad_bout = jnp.sum(grad_attn_low, axis=(0, 1), dtype=jnp.float32)
    grad_up = jnp.einsum(
        "ptd,ptf->df", normed_two_low, grad_upward_low, preferred_element_type=jnp.float32
    )
    grad_bup = jnp.sum(grad_upward_low, axis=(0, 1), dtype=jnp.float32)
    grad_down = jnp.einsum(
        "ptf,ptd->fd", activated_low, grad_branch, preferred_element_type=jnp.float32
    )
    grad_bdown = jnp.sum(grad_branch, axis=(0, 1), dtype=jnp.float32)
    return (
        grad_qkv,
        grad_wout,
        grad_up,
        grad_down,
        grad_bquery,
        grad_bvalue,
        grad_bout,
        grad_bup,
        grad_bdown,
    )


def local(
    tokens,
    w_qkv,
    w_out,
    w_up,
    w_down,
    b_query,
    b_value,
    b_out,
    b_up,
    b_down,
    ln1_gain,
    ln1_bias,
    ln2_gain,
    ln2_bias,
    cotangent,
):
    seq_count = lax.axis_size("seq")
    local_patches = tokens.shape[1]
    model_width = tokens.shape[2]
    patches = local_patches * seq_count
    head_local = H // seq_count
    factor = DH ** (-0.5)
    gathered = (
        lax.all_gather(w_qkv, "dp", axis=0, tiled=True),
        lax.all_gather(w_out, "dp", axis=0, tiled=True),
        lax.all_gather(w_up, "dp", axis=0, tiled=True),
        lax.all_gather(w_down, "dp", axis=1, tiled=True),
        lax.all_gather(b_query, "dp", axis=0, tiled=True),
        lax.all_gather(b_value, "dp", axis=0, tiled=True),
        lax.all_gather(b_out, "dp", axis=0, tiled=True),
        lax.all_gather(b_up, "dp", axis=0, tiled=True),
        lax.all_gather(b_down, "dp", axis=0, tiled=True),
        lax.all_gather(ln1_gain, "dp", axis=0, tiled=True),
        lax.all_gather(ln1_bias, "dp", axis=0, tiled=True),
        lax.all_gather(ln2_gain, "dp", axis=0, tiled=True),
        lax.all_gather(ln2_bias, "dp", axis=0, tiled=True),
    )
    outputs = []
    grad_inputs = []
    kept = []
    for micro_idx in range(MICRO):
        w_qkv_full, w_out_full, w_up_full, w_down_full = (
            gathered[0],
            gathered[1],
            gathered[2],
            gathered[3],
        )
        vectors = [piece.astype(jnp.float32) for piece in gathered[4:]]
        (
            bias_query,
            bias_value,
            bias_out,
            bias_up,
            bias_down,
            gain_one,
            offset_one,
            gain_two,
            offset_two,
        ) = vectors
        start = micro_idx * IMG_MB
        inputs = tokens[start : start + IMG_MB].astype(jnp.float32)
        normed_one, norm_one_back = jax.vjp(normalize, inputs, gain_one, offset_one)
        normed_one_low = normed_one.astype(jnp.bfloat16)
        qkv_bias = jnp.concatenate([bias_query, jnp.zeros_like(bias_query), bias_value])
        projected = (
            jnp.einsum(
                "ptd,de->pte", normed_one_low, w_qkv_full, preferred_element_type=jnp.float32
            )
            + qkv_bias
        )
        projected_low = projected.astype(jnp.bfloat16).reshape(
            IMG_MB, local_patches, 3, model_width
        )
        by_heads = lax.all_to_all(projected_low, "seq", split_axis=3, concat_axis=1, tiled=True)
        queries = by_heads[:, :, 0].reshape(IMG_MB, patches, head_local, DH)
        keyed = by_heads[:, :, 1].reshape(IMG_MB, patches, head_local, DH)
        valued = by_heads[:, :, 2].reshape(IMG_MB, patches, head_local, DH)
        attended, log_total = forward_heads(queries, keyed, valued, factor)
        attended_low = attended.astype(jnp.bfloat16)
        mixed_tokens = lax.all_to_all(attended_low, "seq", split_axis=1, concat_axis=2, tiled=True)
        residual = (
            inputs
            + jnp.einsum(
                "pte,ed->ptd", mixed_tokens, w_out_full, preferred_element_type=jnp.float32
            )
            + bias_out
        )
        normed_two, norm_two_back = jax.vjp(normalize, residual, gain_two, offset_two)
        normed_two_low = normed_two.astype(jnp.bfloat16)
        upward = (
            jnp.einsum("ptd,df->ptf", normed_two_low, w_up_full, preferred_element_type=jnp.float32)
            + bias_up
        )
        activated, activate_back = jax.vjp(activate, upward)
        activated_low = activated.astype(jnp.bfloat16)
        layer_out = (
            residual
            + jnp.einsum(
                "ptf,fd->ptd", activated_low, w_down_full, preferred_element_type=jnp.float32
            )
            + bias_down
        )
        outputs.append(layer_out.astype(jnp.bfloat16))
        grad_result = cotangent[start : start + IMG_MB].astype(jnp.float32)
        grad_branch = grad_result.astype(jnp.bfloat16)
        grad_active = jnp.einsum(
            "ptd,fd->ptf", grad_branch, w_down_full, preferred_element_type=jnp.float32
        )
        (grad_upward,) = activate_back(grad_active)
        grad_upward_low = grad_upward.astype(jnp.bfloat16)
        grad_normed_two = jnp.einsum(
            "ptf,df->ptd", grad_upward_low, w_up_full, preferred_element_type=jnp.float32
        )
        grad_from_two, grad_gain2, grad_bias2 = norm_two_back(grad_normed_two)
        grad_residual = grad_result + grad_from_two
        grad_attn_low = grad_residual.astype(jnp.bfloat16)
        grad_mixed = jnp.einsum(
            "ptd,ed->pte", grad_attn_low, w_out_full, preferred_element_type=jnp.float32
        ).astype(jnp.bfloat16)
        grad_heads = lax.all_to_all(grad_mixed, "seq", split_axis=2, concat_axis=1, tiled=True)
        grad_query, grad_key, grad_value = backward_heads(
            queries,
            keyed,
            valued,
            grad_heads.reshape(IMG_MB, patches, head_local, DH),
            log_total,
            factor,
        )
        stacked = (
            jnp.stack([grad_query, grad_key, grad_value], axis=2)
            .reshape(IMG_MB, patches, 3, head_local * DH)
            .astype(jnp.bfloat16)
        )
        grad_parts = lax.all_to_all(stacked, "seq", split_axis=1, concat_axis=3, tiled=True)
        grad_projected = grad_parts.reshape(IMG_MB, local_patches, 3 * model_width)
        grad_normed_one = jnp.einsum(
            "pte,de->ptd", grad_projected, w_qkv_full, preferred_element_type=jnp.float32
        )
        grad_from_one, grad_gain1, grad_bias1 = norm_one_back(grad_normed_one)
        grad_inputs.append((grad_residual + grad_from_one).astype(jnp.bfloat16))
        norm_grads = (grad_gain1, grad_bias1, grad_gain2, grad_bias2)
        norm_total = norm_grads if micro_idx == 0 else add_pairs(norm_total, norm_grads)
        kept.append(
            (
                normed_one_low,
                grad_projected,
                mixed_tokens,
                grad_attn_low,
                normed_two_low,
                grad_upward_low,
                activated_low,
                grad_branch,
            )
        )
    joined = [jnp.concatenate([item[index] for item in kept], axis=0) for index in range(8)]
    big = weight_grads(
        joined[0],
        joined[1],
        joined[2],
        joined[3],
        joined[4],
        joined[5],
        joined[6],
        joined[7],
        model_width,
    )
    owned = (
        lax.psum_scatter(big[0].astype(jnp.bfloat16), "dp", scatter_dimension=0, tiled=True).astype(
            jnp.float32
        ),
        lax.psum_scatter(big[1].astype(jnp.bfloat16), "dp", scatter_dimension=0, tiled=True).astype(
            jnp.float32
        ),
        lax.psum_scatter(big[2].astype(jnp.bfloat16), "dp", scatter_dimension=0, tiled=True).astype(
            jnp.float32
        ),
        lax.psum_scatter(big[3].astype(jnp.bfloat16), "dp", scatter_dimension=1, tiled=True).astype(
            jnp.float32
        ),
        lax.psum_scatter(big[4].astype(jnp.bfloat16), "dp", scatter_dimension=0, tiled=True).astype(
            jnp.float32
        ),
        lax.psum_scatter(big[5].astype(jnp.bfloat16), "dp", scatter_dimension=0, tiled=True).astype(
            jnp.float32
        ),
        lax.psum_scatter(big[6].astype(jnp.bfloat16), "dp", scatter_dimension=0, tiled=True).astype(
            jnp.float32
        ),
        lax.psum_scatter(big[7].astype(jnp.bfloat16), "dp", scatter_dimension=0, tiled=True).astype(
            jnp.float32
        ),
        lax.psum_scatter(big[8].astype(jnp.bfloat16), "dp", scatter_dimension=0, tiled=True).astype(
            jnp.float32
        ),
        lax.psum_scatter(
            norm_total[0].astype(jnp.bfloat16), "dp", scatter_dimension=0, tiled=True
        ).astype(jnp.float32),
        lax.psum_scatter(
            norm_total[1].astype(jnp.bfloat16), "dp", scatter_dimension=0, tiled=True
        ).astype(jnp.float32),
        lax.psum_scatter(
            norm_total[2].astype(jnp.bfloat16), "dp", scatter_dimension=0, tiled=True
        ).astype(jnp.float32),
        lax.psum_scatter(
            norm_total[3].astype(jnp.bfloat16), "dp", scatter_dimension=0, tiled=True
        ).astype(jnp.float32),
    )
    owned = (
        lax.psum(owned[0].astype(jnp.bfloat16), "seq").astype(jnp.float32),
        lax.psum(owned[1].astype(jnp.bfloat16), "seq").astype(jnp.float32),
        lax.psum(owned[2].astype(jnp.bfloat16), "seq").astype(jnp.float32),
        lax.psum(owned[3].astype(jnp.bfloat16), "seq").astype(jnp.float32),
        lax.psum(owned[4].astype(jnp.bfloat16), "seq").astype(jnp.float32),
        lax.psum(owned[5].astype(jnp.bfloat16), "seq").astype(jnp.float32),
        lax.psum(owned[6].astype(jnp.bfloat16), "seq").astype(jnp.float32),
        lax.psum(owned[7].astype(jnp.bfloat16), "seq").astype(jnp.float32),
        lax.psum(owned[8].astype(jnp.bfloat16), "seq").astype(jnp.float32),
        lax.psum(owned[9].astype(jnp.bfloat16), "seq").astype(jnp.float32),
        lax.psum(owned[10].astype(jnp.bfloat16), "seq").astype(jnp.float32),
        lax.psum(owned[11].astype(jnp.bfloat16), "seq").astype(jnp.float32),
        lax.psum(owned[12].astype(jnp.bfloat16), "seq").astype(jnp.float32),
    )
    return (
        jnp.concatenate(outputs, axis=0),
        jnp.concatenate(grad_inputs, axis=0),
        owned[0],
        owned[1],
        owned[2],
        owned[3],
        owned[4],
        owned[5],
        owned[6],
        owned[7],
        owned[8],
        owned[9],
        owned[10],
        owned[11],
        owned[12],
    )


F32=jnp.float32; BF16=jnp.bfloat16
NT=(((1,),(1,)),((),())); TN=(((0,),(0,)),((),())); NN=(((1,),(0,)),((),()))
def dg(a,b,dims): return lax.dot_general(a,b,dims,preferred_element_type=F32)

MESH = pl.DeviceIdType.MESH
HBM = pltpu.MemorySpace.HBM


def device_map():
    d, z = lax.axis_index("dp"), lax.axis_index("seq")
    core, x, y = lax.rem(d, 2), lax.rem(d // 2, 2), d // 4
    par = lax.rem(z, 2)
    return dict(
        d=d, z=z, core=core, x=x, y=y, par=par,
        sibling=(d + 1 - 2 * core, z), over_x=(d + 2 - 4 * x, z), over_y=(d + 4 - 8 * y, z),
        near_z=(d, z + 1 - 2 * par), far_z=(d, z + 2 - 4 * (z // 2)),
        across=(d, 3 - z), mid=z * (3 - z) > 0,
        image=[(d - core + z // 2, 2 * core + b) for b in range(2)],
        home=(z // 2) == core,
    )


def remote(src, dst, send, recv, to):
    return pltpu.make_async_remote_copy(
        src_ref=src, dst_ref=dst, send_sem=send, recv_sem=recv, device_id=to, device_id_type=MESH
    )


def greet(place, names, middle=False):
    barrier = pltpu.get_barrier_semaphore()
    if middle:
        @pl.when(place["mid"])
        def _(): pl.semaphore_signal(barrier, inc=1, device_id=place["across"], device_id_type=MESH)
    for name in names:
        pl.semaphore_signal(barrier, inc=1, device_id=place[name], device_id_type=MESH)
    for b in range(2):
        @pl.when(jnp.logical_not(jnp.logical_and(place["home"], place["par"] == b)))
        def _(): pl.semaphore_signal(barrier, inc=1, device_id=place["image"][b], device_id_type=MESH)
    extra = place["mid"].astype(jnp.int32) if middle else 0
    pl.semaphore_wait(barrier, len(names) + 2 - place["home"].astype(jnp.int32) + extra)


class Move:
    def __init__(self, place, sources, target, sems):
        self.place, self.sources, self.target, self.sems = place, sources, target, sems
    def each(self, far, near):
        p = self.place
        for b in range(2):
            stays = jnp.logical_and(p["home"], p["par"] == b)
            target = self.target(p["par"])
            @pl.when(jnp.logical_not(stays))
            def _(): far(remote(self.sources[b], target, self.sems.at[0, b], self.sems.at[1, p["par"]], p["image"][b]))
            @pl.when(stays)
            def _(): near(pltpu.make_async_copy(self.sources[b], target, self.sems.at[2, 0]))
    def start(self):
        self.each(lambda c: c.start(), lambda c: c.start())
    def wait(self):
        p = self.place
        self.each(lambda c: c.wait_send(), lambda c: c.wait())
        for h in range(2):
            @pl.when(jnp.logical_not(jnp.logical_and(p["home"], p["par"] == h)))
            def _(): remote(self.sources[0], self.target(h), self.sems.at[0, 0], self.sems.at[1, h], p["image"][0]).wait_recv()


def tiles(count, body, size=256):
    def step(i, carry):
        body(pl.ds(pl.multiple_of(i * size, size), size))
        return carry
    lax.fori_loop(0, count, step, 0)


def turn(place, source, target):
    for j in range(8):
        jy, jx, jc = j // 4, (j // 2) % 2, j % 2
        differ = lambda a, b: (a + b) - 2 * a * b
        at = differ(place["core"], jc) * 4 + differ(place["y"], jy) * 2 + differ(place["x"], jx)
        target[pl.ds(pl.multiple_of(at * 128, 128), 128), :] = source[:, 128 * j : 128 * j + 128].T


def fwd_kernel(
    tok_hbm, cotg_hbm, wq_s, wo_s, wu_s, wd_s, pack,
    wq_o, wo_o, wu_o, wd_o, x_o, cot_o, n1_t_o, n2_t_o, att_t_o, qkv_o, kv_o, att_o, up_o, res_o, out_o, gd_o,
    lse, vec,
    wq, wo, wu, wd, wdn, pk, xb, cot, n1, n2, qkv, kv, att, act, upb, up_bias, res, cot_t, n1_t, n2_t, att_t, so, sr, gs,
    sib_s, sib_r, ws, wr, wl, ps, pr, ms, kvs, kvr, outs, ups,
):
    p = device_map()
    y, x, core, par = p["y"], p["x"], p["core"], p["par"]
    greet(p, ("sibling", "over_x", "over_y", "near_z"))

    def rows(py, px):
        return pl.ds(pl.multiple_of(((py * 2 + px) * 2 + core) * 128, 128), 128)

    chunks = [(wq, wq_s, 0, 3072), (wo, wo_s, 0, 1024), (wu, wu_s, 0, 2048), (wu, wu_s, 2048, 2048),
              (wd, None, 0, 2048), (wd, None, 2048, 2048)]
    me, bx, by, diag = rows(y, x), rows(y, 1 - x), rows(1 - y, x), rows(1 - y, 1 - x)

    shared = (2, 3)

    def copy(n, i):
        w, shard, at, size = chunks[n]
        full = part = pl.ds(at, size)
        lo, hi = pl.ds(at, size // 2), pl.ds(at + size // 2, size // 2)
        rest = None
        if n in shared:
            start_at = lambda by: pl.multiple_of(at + by, 512)
            part, rest = pl.ds(start_at(par * 1024), 1024), pl.ds(start_at((1 - par) * 1024), 1024)
            lo, hi = pl.ds(start_at(par * 1024), 512), pl.ds(start_at(par * 1024 + 512), 512)
        own = (lambda cols: w.at[me, cols]) if shard is None else (lambda cols: shard.at[:, cols])
        src, dst, to = (
            (own(lo), w.at[me, lo], "over_x"), (own(hi), w.at[me, hi], "over_y"),
            (own(hi), w.at[me, hi], "over_x"), (own(lo), w.at[me, lo], "over_y"),
            (own(full), w.at[me, full], "sibling"),
            (w.at[bx, lo], w.at[bx, lo], "over_y"), (w.at[by, hi], w.at[by, hi], "over_x"),
            (w.at[bx, part], w.at[bx, part], "sibling"), (w.at[by, part], w.at[by, part], "sibling"),
            (w.at[diag, lo], w.at[diag, lo], "sibling"), (w.at[diag, hi], w.at[diag, hi], "sibling"),
        )[i] if i < 11 else (
            (w.at[bx, part], w.at[bx, part], "near_z"), (w.at[by, part], w.at[by, part], "near_z"),
            (w.at[diag, part], w.at[diag, part], "near_z"),
            (w.at[bx, rest], w.at[bx, rest], "sibling"), (w.at[by, rest], w.at[by, rest], "sibling"),
            (w.at[diag, rest], w.at[diag, rest], "sibling"),
        )[i - 11]
        return remote(src, dst, ws.at[n, i], wr.at[n, i], p[to])

    def start(n, *which):
        for i in which: copy(n, i).start()

    def wait(n, *which):
        for i in which: copy(n, i).wait()

    def local(n):
        w, shard, at, size = chunks[n]
        return pltpu.make_async_copy(shard.at[:, pl.ds(at, size)], w.at[me, pl.ds(at, size)], wl.at[n])

    def own(n):
        start(n, 0, 1, 2, 3, 4)
        if chunks[n][1] is not None: local(n).start()

    def mid(n):
        wait(n, 0, 1)
        start(n, 5, 6)
        if n < 5: own(n + 1)

    def late(n):
        wait(n, 2, 3)
        start(n, 7, 8)
        if n in shared: start(n, 11, 12)

    def end(n):
        wait(n, 5, 6)
        start(n, 9, 10)
        if n in shared: start(n, 13)
        else: settle_chunk(n)

    def settle_chunk(n):
        if n in shared:
            wait(n, 11, 12, 13)
            start(n, 14, 15, 16)
            wait(n, 14, 15, 16)
        wait(n, 4, 7, 8, 9, 10)
        if chunks[n][1] is not None: local(n).wait()

    given, settled = [], []
    def give(src, dst):
        c = pltpu.make_async_copy(src, dst, outs.at[len(given)])
        c.start()
        given.append(c)
        return c

    def settle(c):
        c.wait()
        settled.append(c)

    own(0)
    pk[y, x, core] = pack[...]
    hop1 = remote(pk.at[y, x, core], pk.at[y, x, core], ps.at[0], pr.at[0], p["over_x"])
    hop1.start()
    half = lambda h: pl.ds(pl.multiple_of(h * 256, 256), 256)
    tok = Move(p, [tok_hbm.at[b] for b in range(2)], lambda h: xb.at[half(h)], ms.at[0])
    tok.start()
    cot_move = Move(p, [cotg_hbm.at[b] for b in range(2)], lambda h: cot.at[half(h)], ms.at[1])
    cot_move.start()
    down = pltpu.make_async_copy(wd_s, wdn, wl.at[5])
    down.start()
    hop1.wait()
    hop2 = remote(pk.at[y, :, core], pk.at[y, :, core], ps.at[1], pr.at[1], p["over_y"])
    hop2.start()
    down.wait()
    for j in range(8):
        wd[me, 512 * j : 512 * j + 512] = wdn[512 * j : 512 * j + 512, :].T
    hop2.wait()
    hop3 = remote(pk.at[:, :, core], pk.at[:, :, core], ps.at[2], pr.at[2], p["sibling"])
    hop3.start()
    mid(0)
    hop3.wait()
    for j in range(8):
        block = pk[j // 4, (j // 2) % 2, j % 2]
        for r in range(12):
            if 3 <= r < 7:
                at = 512 * j + 128 * (r - 3)
                up_bias[:, at : at + 128] = block[r : r + 1]
            else:
                to = {0: 4, 1: 5, 2: 6, 7: 7, 8: 8, 9: 9, 10: 10, 11: 11}[r]
                vec[to : to + 1, 128 * j : 128 * j + 128] = block[r : r + 1]
    vec[0:4, :] = jnp.zeros((4, 1024), F32)
    vec[12:16, :] = jnp.zeros((4, 1024), F32)
    tok.wait()

    def stats(value):
        off = value - jnp.mean(value, axis=-1, keepdims=True)
        return off * lax.rsqrt(jnp.mean(off * off, axis=-1, keepdims=True) + norm_eps)

    def norm_one(r):
        n1[r, :] = (stats(xb[r, :].astype(F32)) * vec[8:9, :] + vec[9:10, :]).astype(BF16)
    tiles(8, norm_one, 64)
    x_given = give(xb, x_o)
    late(0)
    turn(p, n1, n1_t)
    give(n1_t, n1_t_o)
    end(0)
    give(wq, wq_o)
    mid(1)

    def project(cols, bias):
        part = dg(n1[...], wq[:, cols], NN)
        qkv[:, cols] = (part if bias is None else part + bias).astype(BF16)
    def key_cols(c): project(pl.ds(pl.multiple_of(1024 + c.start, 256), 256), None)
    tiles(4, key_cols)
    def value_cols(c): project(pl.ds(pl.multiple_of(2048 + c.start, 256), 256), vec[5:6, c])
    tiles(4, value_cols)
    swap = remote(qkv.at[:, pl.ds(1024, 2048)], kv, kvs, kvr, p["sibling"])
    swap.start()
    def query_cols(c): project(c, vec[4:5, c])
    tiles(4, query_cols)
    swap.wait()
    give(qkv, qkv_o)
    give(kv, kv_o)

    lane = lax.broadcasted_iota(jnp.int32, (512, 128), 1)
    def pair(i, carry):
        at = lambda base: pl.ds(pl.multiple_of(base + i * 128, 128), 128)
        q = qkv[:, at(0)] * jnp.asarray(0.125, BF16)
        outs_, ls = [], []
        for h in range(2):
            qh = jnp.where((lane < 64) if h == 0 else (lane >= 64), q, jnp.zeros_like(q))
            sa, sb = dg(qkv[:, at(1024)], qh, NT), dg(kv[:, at(0)], qh, NT)
            m = jnp.maximum(jnp.max(sa, axis=0, keepdims=True), jnp.max(sb, axis=0, keepdims=True))
            pa, pb = jnp.exp(sa - m), jnp.exp(sb - m)
            total = jnp.sum(pa, axis=0, keepdims=True) + jnp.sum(pb, axis=0, keepdims=True)
            o = dg(qkv[:, at(2048)], pa.astype(BF16), TN) + dg(kv[:, at(1024)], pb.astype(BF16), TN)
            outs_.append(o[64 * h : 64 * h + 64] * (1.0 / total))
            ls.append(m + jnp.log(total))
        att[:, at(0)] = jnp.concatenate(outs_, axis=0).T.astype(BF16)
        lse[i] = jnp.concatenate(ls + [jnp.zeros((6, 512), F32)], axis=0)
        @pl.when(i == 1)
        def _():
            late(1)
            end(1)
            late(2)
        @pl.when(i == 3)
        def _():
            end(2)
            mid(3)
        @pl.when(i == 6)
        def _():
            late(3)
            end(3)
        return carry
    mid(2)
    lax.fori_loop(0, 8, pair, 0)
    mid(4)
    give(wo, wo_o)
    give(att, att_o)
    def out_cols(c):
        res[:, c] = xb[:, c].astype(F32) + dg(att[...], wo[:, c], NN) + vec[6:7, c]
    tiles(4, out_cols)
    res_given = give(res, res_o)
    def norm_two(r):
        n2[r, :] = (stats(res[r, :]) * vec[10:11, :] + vec[11:12, :]).astype(BF16)
    tiles(8, norm_two, 64)

    def up_copy(i):
        return pltpu.make_async_copy(upb.at[lax.rem(i, 2)], up_o.at[:, pl.ds(pl.multiple_of(i * 512, 512), 512)], ups.at[lax.rem(i, 2)])
    def up_block(i, carry):
        @pl.when(i >= 2)
        def _(): up_copy(i - 2).wait()
        for t in range(2):
            c = pl.ds(pl.multiple_of(i * 512 + 256 * t, 256), 256)
            u = dg(n2[...], wu[:, c], NN) + up_bias[:, c]
            upb[lax.rem(i, 2), :, 256 * t : 256 * t + 256] = u
            act[:, c] = (0.5 * u * (1.0 + jnp.tanh(0.7978845608028654 * (u + 0.044715 * u * u * u)))).astype(BF16)
        up_copy(i).start()
        return carry
    def to_sib(k):
        return remote(so.at[k % 2], sr.at[k % 2], sib_s.at[k], sib_r.at[k], p["sibling"])

    def down_odd(k):
        def one(cols):
            so[k % 2, :, cols] = dg(cot_t[512:1024, :], act[:, pl.ds(pl.multiple_of(1024 * k + cols.start, 512), 512)], NN).astype(BF16)
        tiles(2, one, 512)
        to_sib(k).start()

    def down_even(k):
        to_sib(k).wait()
        def one(cols):
            part = dg(cot_t[0:512, :], act[:, pl.ds(pl.multiple_of(1024 * k + cols.start, 512), 512)], NN)
            gs[k, :, :, :, cols] = (part + sr[k % 2, :, cols].astype(F32)).astype(BF16).reshape(2, 2, 128, 512)
        tiles(2, one, 512)
        give(gs.at[k], gd_o.at[k])

    turn(p, n2, n2_t)
    give(n2_t, n2_t_o)
    settle_chunk(2)
    lax.fori_loop(0, 4, up_block, 0)
    cot_move.wait()
    turn(p, cot, cot_t)
    give(cot, cot_o)
    late(4)
    down_odd(0)
    end(4)
    down_even(0)
    down_odd(1)
    settle(res_given)
    first, second = pl.ds(0, 2048), pl.ds(2048, 2048)
    def half_down(c):
        res[:, c] += dg(act[:, first], wd[c, first], NT)
    tiles(4, half_down)
    mid(5)
    down_even(1)
    turn(p, att, att_t)
    give(att_t, att_t_o)
    settle_chunk(3)
    give(wu, wu_o)
    lax.fori_loop(4, 8, up_block, 0)
    late(5)
    down_odd(2)
    end(5)
    give(wd, wd_o)
    settle(x_given)
    down_even(2)
    down_odd(3)
    def finish_cols(c):
        xb[:, c] = (res[:, c] + dg(act[:, second], wd[c, second], NT) + vec[7:8, c]).astype(BF16)
    tiles(4, finish_cols)
    give(xb, out_o)
    down_even(3)
    for c in given:
        if not any(c is s for s in settled): c.wait()
    up_copy(jnp.int32(6)).wait()
    up_copy(jnp.int32(7)).wait()


def forward(tokens, cotangent, shards, pack):
    any_, vmem, hbm = (pl.BlockSpec(memory_space=s) for s in (pl.ANY, pltpu.VMEM, HBM))
    dma = pltpu.SemaphoreType.DMA
    wide = [((1024, 3072), BF16), ((1024, 1024), BF16), ((1024, 4096), BF16), ((1024, 4096), BF16)]
    rows, turned = ((512, 1024), BF16), ((1024, 512), BF16)
    shapes = wide + [rows, rows] + [turned] * 3 + [
        ((512, 3072), BF16), ((512, 2048), BF16), rows, ((512, 4096), F32), ((512, 1024), F32), rows, ((4, 2, 2, 128, 1024), BF16)]
    return pl.pallas_call(
        fwd_kernel,
        in_specs=[any_] * 6 + [vmem],
        out_specs=[hbm] * len(shapes) + [vmem, vmem],
        out_shape=[jax.ShapeDtypeStruct(*s) for s in shapes + [((8, 8, 512), F32), ((16, 1024), F32)]],
        scratch_shapes=[pltpu.VMEM(*s) for s in wide + [
            ((4096, 128), BF16), ((2, 2, 2, 12, 128), F32), rows, rows, rows, rows, ((512, 3072), BF16), ((512, 2048), BF16),
            rows, ((512, 4096), BF16), ((2, 512, 512), F32), ((1, 4096), F32), ((512, 1024), F32)] + [turned] * 4 + [
            ((2, 512, 1024), BF16), ((2, 512, 1024), BF16), ((4, 2, 2, 128, 1024), BF16)]]
        + [dma((4,)), dma((4,)), dma((6, 17)), dma((6, 17)), dma((6,)), dma((3,)), dma((3,)), dma((2, 3, 2)), dma, dma, dma((20,)), dma((2,))],
        compiler_params=pltpu.CompilerParams(collective_id=7, has_side_effects=True, vmem_limit_bytes=67043328),
        cost_estimate=pl.CostEstimate(flops=20 * 10**9, bytes_accessed=60 << 20, transcendentals=10**7),
        name="forward",
    )(tokens, cotangent, *shards, pack)


CHUNKS = 12
SLOTS = 10


def gelu_slope(u):
    inner = 0.7978845608028654 * (u + 0.044715 * u * u * u)
    t = jnp.tanh(inner)
    return 0.5 * (1.0 + t) + 0.5 * u * (1.0 - t * t) * (0.7978845608028654 * (1.0 + 3 * 0.044715 * u * u))


def bwd_kernel(
    cot_hbm, gd_hbm, n2_t_hbm, up_hbm, wd_hbm, wu_hbm, wo_hbm, wq_hbm, att_t_hbm, n1_t_hbm,
    qkv_hbm, kv_hbm, att_hbm, out_hbm, res_hbm, x_hbm, lse_ref, vec,
    gd_out, gu_out, go_out, gq_out, result_out, gin_out, small_out,
    sums_ref, sum_in, so, sr, g, h1a, h1b, h2a, h2b, z1, z2, fin, dkv_in, cot, gres, gub, n2_t,
    sib_s, sib_r, hop_s, hop_r, zs, zr, fin_sem, dkv_s, dkv_r, load, ms, ss, sm,
):
    p = device_map()
    x, y, core, par, z = p["x"], p["y"], p["core"], p["par"], p["z"]
    sibling, over_x, over_y, near_z, far_z = (p[n] for n in ("sibling", "over_x", "over_y", "near_z", "far_z"))
    greet(p, ("sibling", "over_x", "over_y", "near_z", "far_z"), True)
    mid, across = p["mid"], p["across"]

    lo, hi = pl.ds(0, 512), pl.ds(512, 512)
    def to_sib(k):
        return remote(so.at[lax.rem(k, 2)], sr.at[lax.rem(k, 2)], sib_s.at[k], sib_r.at[k], sibling)

    def hop(k, j):
        src, dst, to = (
            (g.at[lax.rem(k, SLOTS), 1, :, :, lo], h1a.at[k], over_y),
            (g.at[lax.rem(k, SLOTS), :, 1, :, hi], h1b.at[k], over_x),
            (g.at[lax.rem(k, SLOTS), 0, 1, :, lo], h2a.at[k], over_x),
            (g.at[lax.rem(k, SLOTS), 1, 0, :, hi], h2b.at[k], over_y),
        )[j]
        return remote(src, dst, hop_s.at[k, j], hop_r.at[k, j], to)

    def zhop(k, j, side):
        cols = (lo, hi)[side]
        dst, to = ((z1.at[k, :, cols], near_z), (z2.at[k, :, cols], across), (z2.at[k, :, cols], near_z))[j]
        return remote(g.at[lax.rem(k, SLOTS), 0, 0, :, cols], dst, zs.at[k, 2 * j + side], zr.at[k, 2 * j + side], to)

    def ends(run):
        pl.when(jnp.logical_not(mid))(run)

    def plus(a, b):
        return (a.astype(F32) + b.astype(F32)).astype(BF16)

    def out_copy(k):
        slot = lax.rem(k, 2)
        def with_target(run):
            col = lambda j: pl.ds(pl.multiple_of(j * 1024, 1024), 1024)
            sem = fin_sem.at[slot]
            @pl.when(k < 4)
            def _(): run(pltpu.make_async_copy(fin.at[slot], gd_out.at[:, col(k)], sem))
            @pl.when(jnp.logical_and(k >= 4, k < 8))
            def _(): run(pltpu.make_async_copy(fin.at[slot], gu_out.at[:, col(k - 4)], sem))
            @pl.when(k == 8)
            def _(): run(pltpu.make_async_copy(fin.at[slot], go_out, sem))
            @pl.when(k > 8)
            def _(): run(pltpu.make_async_copy(fin.at[slot], gq_out.at[:, col(k - 9)], sem))
        return with_target

    def tick(n):
        def stage(k, body):
            @pl.when(jnp.logical_and(k >= 0, k < CHUNKS))
            def _(): body(k)

        def c2(k):
            hop(k, 0).wait(); hop(k, 1).wait()
            g[lax.rem(k, SLOTS), 0, :, :, lo] = plus(g[lax.rem(k, SLOTS), 0, :, :, lo], h1a[k])
            g[lax.rem(k, SLOTS), :, 0, :, hi] = plus(g[lax.rem(k, SLOTS), :, 0, :, hi], h1b[k])
            hop(k, 2).start(); hop(k, 3).start()
            @pl.when(k < 7)
            def _():
                hop(k + 2, 0).start(); hop(k + 2, 1).start()

        sides = ((0, lo), (1, hi))

        def c3(k):
            for side, cols in sides:
                hop(k, 2 + side).wait()
                mine = (lax.rem(k, SLOTS), 0, 0, slice(None), cols)
                g[mine] = plus(g[mine], (h2a, h2b)[side][k])
                ends(lambda: zhop(k, 0, side).start())

        def c4(k):
            @pl.when(mid)
            def _():
                for side, cols in sides:
                    zhop(k, 0, side).wait_recv()
                    mine = (lax.rem(k, SLOTS), 0, 0, slice(None), cols)
                    g[mine] = plus(g[mine], z1[k, :, cols])
                    zhop(k, 1, side).start()

        def c5(k):
            @pl.when(mid)
            def _():
                for side, cols in sides:
                    zhop(k, 1, side).wait()
                    mine = (lax.rem(k, SLOTS), 0, 0, slice(None), cols)
                    g[mine] = plus(g[mine], z2[k, :, cols])
                    zhop(k, 2, side).start()

        def c6(k):
            slot = lax.rem(k, 2)
            @pl.when(k >= 2)
            def _(): out_copy(k - 2)(lambda c: c.wait())
            @pl.when(mid)
            def _():
                fin[slot] = g[lax.rem(k, SLOTS), 0, 0].astype(F32)
                for side in range(2): zhop(k, 2, side).wait_send()
            def other():
                for side, cols in sides:
                    zhop(k, 0, side).wait_send()
                    zhop(k, 2, side).wait_recv()
                    fin[slot, :, cols] = z2[k, :, cols].astype(F32)
            ends(other)
            out_copy(k)(lambda c: c.start())

        stage(n - 3, c5); stage(n - 2, c4); stage(n - 1, c3); stage(n, c2); stage(n - 4, c6)

    def send_odd(k, left, right):
        def one(cols):
            so[lax.rem(k, 2), :, cols] = dg(left[512:1024, :], right[:, cols], NN).astype(BF16)
        tiles(2, one, 512)
        to_sib(k).start()

    def add_even(k, left, right):
        to_sib(k).wait()
        def one(cols):
            part = dg(left[0:512, :], right[:, cols], NN) + sr[lax.rem(k, 2), :, cols].astype(F32)
            g[lax.rem(k, SLOTS), :, :, :, cols] = part.astype(BF16).reshape(2, 2, 128, 512)
        tiles(2, one, 512)
        @pl.when(k > 8)
        def _():
            hop(k, 0).start(); hop(k, 1).start()

    def fetch(src, dst, i):
        return pltpu.make_async_copy(src, dst, load.at[i])

    first = fetch(cot_hbm, cot, 0)
    first.start()
    result = Move(p, [out_hbm.at[pl.ds(256 * h, 256)] for h in range(2)], lambda b: result_out.at[b], ms.at[0])
    result.start()
    sums_ref[...] = jnp.zeros_like(sums_ref)

    def up_grad(m):
        return gub.at[:, pl.ds(pl.multiple_of(m * 1024, 1024), 1024)]

    def mlp(upb, wdb, wub, gn2, resb):
        sums4 = fetch(gd_hbm, g.at[pl.ds(0, 4)], 1)
        pieces = [fetch(n2_t_hbm, n2_t, 2), fetch(res_hbm, resb, 3)]
        def part(i, j):
            src, dst = ((up_hbm, upb), (wd_hbm, wdb), (wu_hbm, wub))[i]
            return pltpu.make_async_copy(src.at[:, pl.ds(pl.multiple_of(j * 1024, 1024), 1024)], dst, load.at[4 + i])
        sums4.start()
        for i in range(3): part(i, jnp.int32(0)).start()
        for c in pieces: c.start()
        sums4.wait()
        for k in range(2):
            hop(jnp.int32(k), 0).start()
            hop(jnp.int32(k), 1).start()
        gn2[...] = jnp.zeros_like(gn2)
        first.wait()
        def block(j, carry):
            def more(*which):
                @pl.when(j < 3)
                def _():
                    for i in which: part(i, j + 1).start()
            part(0, j).wait()
            part(1, j).wait()
            def slope(cols):
                back = dg(cot[...], wdb[:, cols], NN)
                low = (back * gelu_slope(upb[:, cols])).astype(BF16)
                gub[:, pl.ds(pl.multiple_of(j * 1024 + cols.start, 256), 256)] = low
                sums_ref[pl.ds(j, 1), cols] = jnp.sum(low.astype(F32), axis=0, keepdims=True)
            tiles(4, slope)
            more(0, 1)
            part(2, j).wait()
            here = pl.ds(pl.multiple_of(j * 1024, 1024), 1024)
            def down(cols):
                gn2[:, cols] += dg(gub[:, here], wub[cols, :], NT)
            tiles(4, down)
            more(2)
            @pl.when(lax.rem(j, 2) == 1)
            def _(): tick(j // 2)
            return carry
        lax.fori_loop(0, 4, block, 0)
        for c in pieces: c.wait()
        send_odd(jnp.int32(4), n2_t, up_grad(0))
        def rows(r):
            res = resb[r, :]
            centre = jnp.mean(res, axis=-1, keepdims=True)
            off = res - centre
            rstd = lax.rsqrt(jnp.mean(off * off, axis=-1, keepdims=True) + norm_eps)
            xhat = off * rstd
            grad = gn2[r, :]
            e = grad * vec[10:11, :]
            back = rstd * (e - jnp.mean(e, axis=-1, keepdims=True) - xhat * jnp.mean(e * xhat, axis=-1, keepdims=True))
            total = cot[r, :].astype(F32) + back
            gres[r, :] = total
            low = total.astype(BF16).astype(F32)
            add = lambda i, v: sums_ref.__setitem__((slice(i, i + 1), slice(None)), sums_ref[i : i + 1, :] + jnp.sum(v, axis=0, keepdims=True))
            add(4, low); add(5, grad * xhat); add(6, grad); add(7, cot[r, :].astype(F32))
        tiles(8, rows, 64)

    pl.run_scoped(
        mlp, pltpu.VMEM((512, 1024), F32),
        pltpu.VMEM((1024, 1024), BF16), pltpu.VMEM((1024, 1024), BF16), pltpu.VMEM((512, 1024), F32),
        pltpu.VMEM((512, 1024), F32),
    )

    def rest(dqkv, n1_t, xb):
        late = [fetch(n1_t_hbm, n1_t, 0), fetch(x_hbm, xb, 1)]

        def attention(wo, att_t, ga, kv, att, do):
            loads = [
                fetch(src, dst, 2 + i) for i, (src, dst) in enumerate((
                    (wo_hbm, wo), (qkv_hbm, dqkv), (kv_hbm, kv), (att_hbm, att), (att_t_hbm, att_t),
                ))
            ]
            for c in loads + late: c.start()
            ga[...] = gres[...].astype(BF16)
            add_even(jnp.int32(4), n2_t, up_grad(0))
            send_odd(jnp.int32(5), n2_t, up_grad(1))
            tick(jnp.int32(2))
            loads[0].wait()
            def mixed(cols):
                do[:, cols] = dg(ga[...], wo[cols, :], NT).astype(BF16)
            tiles(4, mixed)
            add_even(jnp.int32(5), n2_t, up_grad(1))
            for c in loads[1:]: c.wait()
            lane = lax.broadcasted_iota(jnp.int32, (512, 128), 1)
            def pair(i, carry):
                at = lambda base: pl.ds(pl.multiple_of(base + i * 128, 128), 128)
                cols = at(0)
                qs = dqkv[:, cols] * jnp.asarray(0.125, BF16)
                dos = do[:, cols]
                t = (dos.astype(F32) * att[:, cols].astype(F32)).T
                dq, dk, dv = None, [None, None], [None, None]
                plus_ = lambda a, b: b if a is None else a + b
                sides = ((dqkv, at(1024), at(2048)), (kv, at(0), at(1024)))
                for h in range(2):
                    sel = (lane < 64) if h == 0 else (lane >= 64)
                    qh = jnp.where(sel, qs, jnp.zeros_like(qs))
                    doh = jnp.where(sel, dos, jnp.zeros_like(dos))
                    delta = jnp.sum(t[64 * h : 64 * h + 64], axis=0, keepdims=True)
                    lse = lse_ref[i, h : h + 1, :]
                    for n, (ref, k_at, v_at) in enumerate(sides):
                        kk = ref[:, k_at]
                        s = dg(kk, qh, NT)
                        p_ = jnp.exp(s - lse)
                        dp = dg(ref[:, v_at], doh, NT)
                        ds = (p_ * (dp - delta)).astype(BF16)
                        dv[n] = plus_(dv[n], dg(p_.astype(BF16), doh, NN))
                        dk[n] = plus_(dk[n], dg(ds, qh, NN))
                        dq = plus_(dq, dg(jnp.where(sel, kk, jnp.zeros_like(kk)), ds, TN))
                dqkv[:, cols] = (dq * 0.125).T.astype(BF16)
                for n, (ref, k_at, v_at) in enumerate(sides):
                    ref[:, k_at] = dk[n].astype(BF16)
                    ref[:, v_at] = dv[n].astype(BF16)
                m = i // 2
                @pl.when(lax.rem(i, 2) == 1)
                def _():
                    @pl.when(m < 2)
                    def _(): send_odd(6 + m, n2_t, up_grad(2 + m))
                    @pl.when(m == 2)
                    def _(): send_odd(jnp.int32(8), att_t, ga)
                    pass
                @pl.when(i == 0)
                def _(): tick(jnp.int32(3))
                @pl.when(jnp.logical_and(lax.rem(i, 2) == 0, i > 0))
                def _():
                    @pl.when(m < 3)
                    def _(): add_even(5 + m, n2_t, up_grad(1 + m))
                    @pl.when(m == 3)
                    def _(): add_even(jnp.int32(8), att_t, ga)
                    tick(3 + m)
                return carry
            lax.fori_loop(0, 8, pair, 0)
            swap = remote(kv, dkv_in, dkv_s, dkv_r, sibling)
            swap.start()
            late[0].wait()
            tick(jnp.int32(7))
            send_odd(jnp.int32(9), n1_t, dqkv.at[:, pl.ds(0, 1024)])
            swap.wait()

        pl.run_scoped(
            attention, pltpu.VMEM((1024, 1024), BF16), pltpu.VMEM((1024, 512), BF16), pltpu.VMEM((512, 1024), BF16),
            pltpu.VMEM((512, 2048), BF16), pltpu.VMEM((512, 1024), BF16), pltpu.VMEM((512, 1024), BF16),
        )

        def last(wq, gn1):
            def wq_part(i):
                s = lax.rem(i, 2)
                return pltpu.make_async_copy(wq_hbm.at[pl.ds(pl.multiple_of(i * 256, 256), 256), :], wq.at[s], load.at[2 + s])
            wq_part(jnp.int32(0)).start()
            def join(cols):
                there = pl.ds(pl.multiple_of(1024 + cols.start, 256), 256)
                dqkv[:, there] = plus(dqkv[:, there], dkv_in[:, cols])
            tiles(8, join)
            add_even(jnp.int32(9), n1_t, dqkv.at[:, pl.ds(0, 1024)])
            def back(i, carry):
                wq_part(i).wait()
                @pl.when(i < 3)
                def _(): wq_part(i + 1).start()
                gn1[:, pl.ds(pl.multiple_of(i * 256, 256), 256)] = dg(dqkv[...], wq[lax.rem(i, 2)], NT)
                return carry
            lax.fori_loop(0, 4, back, 0)
            tick(jnp.int32(8))
            late[1].wait()
            def rows(r):
                xx = xb[r, :].astype(F32)
                centre = jnp.mean(xx, axis=-1, keepdims=True)
                off = xx - centre
                rstd = lax.rsqrt(jnp.mean(off * off, axis=-1, keepdims=True) + norm_eps)
                xhat = off * rstd
                grad = gn1[r, :]
                e = grad * vec[8:9, :]
                back = rstd * (e - jnp.mean(e, axis=-1, keepdims=True) - xhat * jnp.mean(e * xhat, axis=-1, keepdims=True))
                xb[r, :] = (gres[r, :] + back).astype(BF16)
                add = lambda i, v: sums_ref.__setitem__((slice(i, i + 1), slice(None)), sums_ref[i : i + 1, :] + jnp.sum(v, axis=0, keepdims=True))
                add(8, grad * xhat); add(9, grad)
                add(10, dqkv[r, 0:1024].astype(F32)); add(11, dqkv[r, 2048:3072].astype(F32))
            tiles(8, rows, 64)
            given = [
                Move(p, [xb.at[pl.ds(256 * h + 32 * i, 32)] for h in range(2)],
                     lambda b, i=i: gin_out.at[b, pl.ds(32 * i, 32)], ms.at[1 + i])
                for i in range(8)
            ]
            steps = [
                remote(sums_ref, sum_in.at[i], ss.at[i], sm.at[i], to)
                for i, to in enumerate((sibling, over_x, over_y, near_z, far_z))
            ]
            steps[0].start()
            given[0].start()
            for k in (10, 11):
                right = dqkv.at[:, pl.ds(1024 * (k - 9), 1024)]
                send_odd(jnp.int32(k), n1_t, right)
                if k == 10: tick(jnp.int32(9))
                add_even(jnp.int32(k), n1_t, right)
                for m_ in ((given[1], given[2]) if k == 10 else (given[3],)): m_.start()
            for i in range(6):
                tick(jnp.int32(10 + i))
                if i < 4: given[4 + i].start()
                if i < 5:
                    steps[i].wait()
                    sums_ref[...] += sum_in[i]
                    if i < 4: steps[i + 1].start()
            d = p["d"]
            mine = pl.ds(pl.multiple_of(d * 128, 128), 128)
            for to, at in ((0, 10), (1, 11), (2, 4), (7, 7), (8, 8), (9, 9), (10, 5), (11, 6)):
                small_out[to : to + 1, :] = sums_ref[at : at + 1, mine]
            for t in range(4):
                lanes = pl.ds(pl.multiple_of(lax.rem(d, 2) * 512 + 128 * t, 128), 128)
                part = sums_ref[0:1, lanes]
                for r in range(1, 4):
                    part = jnp.where(d // 2 == r, sums_ref[r : r + 1, lanes], part)
                small_out[3 + t : 4 + t, :] = part
            for k in (CHUNKS - 2, CHUNKS - 1):
                out_copy(jnp.int32(k))(lambda c: c.wait())
            for move in given: move.wait()
            result.wait()

        pl.run_scoped(last, pltpu.VMEM((2, 256, 3072), BF16), pltpu.VMEM((512, 1024), F32))

    pl.run_scoped(rest, pltpu.VMEM((512, 3072), BF16), pltpu.VMEM((1024, 512), BF16), pltpu.VMEM((512, 1024), BF16))


def backward(arrays, lse, vec):
    any_, vmem, hbm = (pl.BlockSpec(memory_space=s) for s in (pl.ANY, pltpu.VMEM, HBM))
    n = CHUNKS
    dma = pltpu.SemaphoreType.DMA
    return pl.pallas_call(
        bwd_kernel,
        in_specs=[any_] * len(arrays) + [vmem, vmem],
        out_specs=[hbm] * 6 + [vmem],
        out_shape=[jax.ShapeDtypeStruct((128, w), F32) for w in (4096, 4096, 1024, 3072)]
        + [jax.ShapeDtypeStruct((2, 256, 1024), BF16)] * 2 + [jax.ShapeDtypeStruct((12, 128), F32)],
        scratch_shapes=[
            pltpu.VMEM((16, 1024), F32), pltpu.VMEM((5, 16, 1024), F32),
            pltpu.VMEM((2, 512, 1024), BF16), pltpu.VMEM((2, 512, 1024), BF16), pltpu.VMEM((SLOTS, 2, 2, 128, 1024), BF16),
            pltpu.VMEM((n, 2, 128, 512), BF16), pltpu.VMEM((n, 2, 128, 512), BF16),
            pltpu.VMEM((n, 128, 512), BF16), pltpu.VMEM((n, 128, 512), BF16),
            pltpu.VMEM((n, 128, 1024), BF16), pltpu.VMEM((n, 128, 1024), BF16),
            pltpu.VMEM((2, 128, 1024), F32), pltpu.VMEM((512, 2048), BF16), pltpu.VMEM((512, 1024), BF16),
            pltpu.VMEM((512, 1024), F32), pltpu.VMEM((512, 4096), BF16), pltpu.VMEM((1024, 512), BF16),
            dma((n,)), dma((n,)), dma((n, 4)), dma((n, 4)), dma((n, 6)), dma((n, 6)), dma((2,)), dma, dma, dma((12,)),
            dma((9, 3, 2)), dma((5,)), dma((5,)),
        ],
        compiler_params=pltpu.CompilerParams(collective_id=8, has_side_effects=True, vmem_limit_bytes=67043328),
        cost_estimate=pl.CostEstimate(flops=40 * 10**9, bytes_accessed=60 << 20, transcendentals=10**7),
        name="backward",
    )(*arrays, lse, vec)


def local_fast(
    tokens, w_qkv, w_out, w_up, w_down, b_query, b_value, b_out, b_up, b_down,
    ln1_gain, ln1_bias, ln2_gain, ln2_bias, cotangent,
):
    small = (b_query, b_value, b_out, b_up, b_down, ln1_gain, ln1_bias, ln2_gain, ln2_bias)
    pack, at = jnp.zeros((12, 128), F32), 0
    for item in small:
        rows = item.shape[0] // 128
        pack = pack + jnp.pad(item.astype(F32).reshape(rows, 128), ((at, 12 - at - rows), (0, 0)))
        at += rows
    (wq, wo, wu, wd, x, cot, n1_t, n2_t, att_t, qkv, kv, att, up, res, out, gd, lse, vec) = forward(
        tokens, cotangent, (w_qkv, w_out, w_up, w_down), pack)
    g_down, g_up, g_out, g_qkv, result, grad_input, sums = backward(
        (cot, gd, n2_t, up, wd, wu, wo, wq, att_t, n1_t, qkv, kv, att, out, res, x), lse, vec)
    outs, at = [], 0
    for item in small:
        rows = item.shape[0] // 128
        outs.append(sums[at : at + rows].reshape(-1))
        at += rows
    return (result, grad_input, g_qkv, g_out, g_up, g_down.T, *outs)


def solution(mesh):
    in_specs = (
        P("dp", "seq", None),
        P("dp", None),
        P("dp", None),
        P("dp", None),
        P(None, "dp"),
        P("dp"),
        P("dp"),
        P("dp"),
        P("dp"),
        P("dp"),
        P("dp"),
        P("dp"),
        P("dp"),
        P("dp"),
        P("dp", "seq", None),
    )
    out_specs = (
        P("dp", "seq", None),
        P("dp", "seq", None),
        P("dp", None),
        P("dp", None),
        P("dp", None),
        P(None, "dp"),
        P("dp"),
        P("dp"),
        P("dp"),
        P("dp"),
        P("dp"),
        P("dp"),
        P("dp"),
        P("dp"),
        P("dp"),
    )
    fn = local_fast if dict(mesh.shape) == {"dp": 8, "seq": 4} else local
    return jax.shard_map(fn, mesh=mesh, in_specs=in_specs, out_specs=out_specs, check_vma=False)
```
